128 devices in a mesh: pipe: 2 (over core), tensor: 2 (over x_lo), dp: 32 (over y, z, x_hi).
Axes of the slice: x: 4 (x_hi: 2, x_lo: 2; x = x_hi * 2 + x_lo), y: 4, z: 4, core: 2. Of those that a mesh axis runs over, the one named last changes fastest.
Arguments:
- section_in: bfloat16 [2, 32, 2, 128, 1024], P('pipe', 'dp', 'tensor'), may hold values from -12 to 12
- lengths: int32 [32, 2], P('dp'), may hold values from 32 to 128, as said below
- qkv_weight: bfloat16 [2, 3, 1024, 1024], P('pipe', None, None, 'tensor'), may hold values from -0.75 to 0.75
- qv_bias: bfloat16 [2, 2, 1024], P('pipe', None, 'tensor'), may hold values from -3 to 3
- out_weight: bfloat16 [2, 1024, 1024], P('pipe', 'tensor'), may hold values from -0.5 to 0.5
- up_weight: bfloat16 [2, 1024, 2048], P('pipe', None, 'tensor'), may hold values from -0.1875 to 0.1875
- up_bias: bfloat16 [2, 2048], P('pipe', 'tensor'), may hold values from -3 to 3
- down_weight: bfloat16 [2, 2048, 1024], P('pipe', 'tensor'), may hold values from -0.125 to 0.125
- norm_gains: float32 [2, 2, 1024], P('pipe'), may hold values from 0.5 to 1.5
- row_biases: float32 [2, 4, 1024], P('pipe'), may hold values from -2 to 2
Outputs:
- section_out: float32 [2, 32, 2, 128, 1024], P('pipe', 'dp', 'tensor')
- qkv_grad: float32 [2, 3, 1024, 1024], P('pipe', None, None, 'tensor')
- qv_bias_grad: float32 [2, 2, 1024], P('pipe', None, 'tensor')
- out_grad: float32 [2, 1024, 1024], P('pipe', 'tensor')
- up_grad: float32 [2, 1024, 2048], P('pipe', None, 'tensor')
- up_bias_grad: float32 [2, 2048], P('pipe', 'tensor')
- down_grad: float32 [2, 2048, 1024], P('pipe', 'tensor')
- gain_grad: float32 [2, 2, 1024], P('pipe')
- bias_grad: float32 [2, 4, 1024], P('pipe')
The draws below stay inside these ranges and needn't reach their ends.
Inputs may be any that keep to these rules, and one draw needn't show every extreme that they name: `lengths`: some sequence has length exactly 128 and some exactly 32.
All inputs are finite; a program needn't handle non-finite values.
Results may differ from the reference program's by a relative error of at most 0.023.
Values may be sent and summed in bfloat16 or wider, within the bound.
No kernel may reach another device: no remote copies, remote signals or barrier semaphores. Data moves between devices by JAX's collectives and lax.ppermute only.
A program may use at most 128 MiB of HBM per device.

```python
import jax
import jax.numpy as jnp
from jax import lax

D = 1024
HEADS = 16
HD = 64
FF = 2048
LEN = 128
MICRO_DEV = 1
HW = 1024
GROUPS = 32
N_TENSOR = 2
N_DP = 32


def draw_section_in(key, part):
    shape_all = (2, GROUPS, N_TENSOR, LEN, D)
    base = jax.random.truncated_normal(jax.random.fold_in(key, 31), -6.0, 6.0, shape_all, jnp.float32)
    group_ids = jnp.arange(GROUPS)[:, None]
    tensor_ids = jnp.arange(N_TENSOR)[None, :]
    place = (tensor_ids * N_DP + group_ids // MICRO_DEV).astype(jnp.float32)
    rising = 1.0 + 2.0 * place / max(N_TENSOR * N_DP - 1, 1)
    scale_all = jnp.stack([jnp.ones((GROUPS, N_TENSOR), jnp.float32), rising])[:, :, :, None, None]
    values = jnp.clip(base * scale_all, -12.0, 12.0)
    return values.astype(jnp.bfloat16)


def draw_lengths(key, part):
    number = GROUPS * N_TENSOR
    drawn = jax.random.randint(jax.random.fold_in(key, 11), (number,), LEN // 4, LEN + 1)
    full_at = jax.random.randint(jax.random.fold_in(key, 12), (), 0, number)
    short_at = (full_at + jax.random.randint(jax.random.fold_in(key, 13), (), 1, number)) % number
    drawn = drawn.at[full_at].set(LEN).at[short_at].set(LEN // 4)
    return drawn.reshape(GROUPS, N_TENSOR).astype(jnp.int32)


def draw_qkv_weight(key, part):
    shape_all = (2, 3, D, HEADS * HD)
    base = jax.random.truncated_normal(jax.random.fold_in(key, 21), -4.0, 4.0, shape_all, jnp.float32) * D ** (-0.5)
    base = jnp.clip(base, -0.75, 0.75)
    return base.astype(jnp.bfloat16)


def level_of(rng, extent, shards, smallest, high):
    def one(position, parts):
        draws = jax.random.uniform(jax.random.fold_in(jax.random.fold_in(rng, 6), position), (parts,), jnp.float32, smallest / len(shards), high / len(shards))
        return jnp.repeat(jnp.exp(draws), extent[position] // parts).reshape((-1,) + (1,) * (len(extent) - position - 1))

    factor_of = one(*shards[0])
    for cut in shards[1:]:
        factor_of = factor_of * one(*cut)
    return factor_of


def gaussian(stream_key, extent, spread, bound, cuts=(), held_as=jnp.bfloat16):
    factor_of = level_of(stream_key, extent, cuts, -0.22, 0.18) if cuts else 1.0
    entries = jax.random.normal(stream_key, extent, jnp.float32) * spread * factor_of
    return jnp.minimum(jnp.maximum(entries, -bound), bound).astype(held_as)


def setup_inputs(seed: int = 0) -> dict:
    keys = jax.random.split(jax.random.key(seed), 11)
    return {
        "section_in": draw_section_in(jax.random.fold_in(keys[10], 71), 0),
        "lengths": draw_lengths(jax.random.fold_in(keys[10], 71), 0),
        "qkv_weight": draw_qkv_weight(jax.random.fold_in(keys[10], 71), 0),
        "qv_bias": gaussian(keys[3], (2, 2, HW), 0.5, 3.0, ((0, 2), (2, 2))),
        "out_weight": gaussian(keys[4], (2, HW, D), (HW // 8) ** -0.5, 0.5, ((0, 2), (1, 2))),
        "up_weight": gaussian(keys[5], (2, D, FF), D ** -0.5, 0.1875, ((0, 2), (2, 2))),
        "up_bias": gaussian(keys[6], (2, FF), 0.5, 3.0, ((0, 2), (1, 2))),
        "down_weight": gaussian(keys[7], (2, FF, D), FF ** -0.5, 0.125, ((0, 2), (1, 2))),
        "norm_gains": jnp.clip(1.0 + 0.1 * jax.random.normal(keys[8], (2, 2, D), jnp.float32), 0.5, 1.5),
        "row_biases": gaussian(keys[9], (2, 4, D), 0.3, 2.0, ((0, 2),), jnp.float32),
    }


norm_eps = 1e-05

def gelu_tanh(pre_act):
    return 0.5 * pre_act * (1.0 + jnp.tanh(0.7978845608028654 * (pre_act + 0.044715 * pre_act * pre_act * pre_act)))

def norm_fwd(values, gain, shift):
    centred = values - lax.optimization_barrier(jnp.mean(values, axis=-1, keepdims=True))
    inv_std = lax.rsqrt(lax.optimization_barrier(jnp.mean(centred * centred, axis=-1, keepdims=True)) + norm_eps)
    normed = centred * inv_std
    return (normed * gain + shift, normed, inv_std)

def norm_back(grad_norm, normed, inv_std, gain):
    scaled = grad_norm * gain
    return inv_std * (scaled - lax.optimization_barrier(jnp.mean(scaled, axis=-1, keepdims=True)) - normed * lax.optimization_barrier(jnp.mean(scaled * normed, axis=-1, keepdims=True)))

def widen_half(values):
    return lax.optimization_barrier(values).astype(jnp.float32)

def masked_scores(queries, keys_all, seq_length):
    offsets = (jnp.arange(LEN)[:, None] - jnp.arange(LEN)[None, :]).astype(jnp.float32)
    slopes = 2.0 ** (-8.0 * (jnp.arange(HEADS) + 1).astype(jnp.float32) / HEADS)
    scores = jnp.einsum('qhd,khd->hqk', widen_half(queries), widen_half(keys_all)) * 0.125 - slopes[:, None, None] * offsets
    allowed = (offsets >= 0)[None] & (jnp.arange(LEN)[None, None, :] < seq_length)
    return jnp.where(allowed, scores, -jnp.inf)

def layer_forward(layer_in, seq_length, params):
    qkv_w, qv_b, out_w, up_w, up_b, down_w, gains, shifts = params
    layer_wide = layer_in.astype(jnp.float32)
    attn_f, _, _ = norm_fwd(layer_wide, gains[0], shifts[0])
    attn_rows = attn_f.astype(jnp.bfloat16)
    bias_three = jnp.stack([qv_b[0], jnp.zeros_like(qv_b[0]), qv_b[1]]).astype(jnp.float32)[:, None, :]
    projected = (jnp.einsum('rd,cdw->crw', widen_half(attn_rows), widen_half(qkv_w)) + bias_three).astype(jnp.bfloat16)
    queries = projected[0].reshape(LEN, HEADS, HD)
    keys_all = projected[1].reshape(LEN, HEADS, HD)
    values_all = projected[2].reshape(LEN, HEADS, HD)
    scores = masked_scores(queries, keys_all, seq_length)
    top_score = lax.optimization_barrier(jnp.max(scores, axis=-1, keepdims=True))
    exp_scores = jnp.exp(scores - top_score)
    totals = lax.optimization_barrier(jnp.sum(exp_scores, axis=-1, keepdims=True))
    att_prob = exp_scores / totals
    log_total = top_score + jnp.log(totals)
    context = jnp.einsum('hqk,khd->qhd', widen_half(att_prob.astype(jnp.bfloat16)), widen_half(values_all)).reshape(LEN, HEADS * HD).astype(jnp.bfloat16)
    residual = layer_wide + (jnp.dot(context, out_w, preferred_element_type=jnp.float32) + shifts[1])
    mlp_f, _, _ = norm_fwd(residual, gains[1], shifts[2])
    mlp_rows = mlp_f.astype(jnp.bfloat16)
    pre_gelu = jnp.dot(mlp_rows, up_w, preferred_element_type=jnp.float32) + up_b.astype(jnp.float32)
    activated = gelu_tanh(pre_gelu).astype(jnp.bfloat16)
    layer_out = residual + (jnp.dot(activated, down_w, preferred_element_type=jnp.float32) + shifts[3])
    return (layer_out, (layer_in, attn_rows, projected, log_total, context, residual, mlp_rows, pre_gelu, activated))

def layer_backward(grad_out, saved, seq_length, params):
    qkv_w, qv_b, out_w, up_w, up_b, down_w, gains, shifts = params
    layer_in, attn_rows, projected, log_total, context, residual, mlp_rows, pre_gelu, activated = saved
    _, attn_norm, attn_inv = norm_fwd(layer_in.astype(jnp.float32), gains[0], shifts[0])
    _, mlp_norm, mlp_inv = norm_fwd(residual, gains[1], shifts[2])
    grad_half = grad_out.astype(jnp.bfloat16)
    grad_down = jnp.dot(activated.T, grad_half, preferred_element_type=jnp.float32)
    grad_act = jnp.dot(grad_half, down_w.T, preferred_element_type=jnp.float32)
    _, pull_back = jax.vjp(gelu_tanh, pre_gelu)
    grad_pre = pull_back(grad_act)[0]
    grad_pre_half = grad_pre.astype(jnp.bfloat16)
    grad_up = jnp.dot(mlp_rows.T, grad_pre_half, preferred_element_type=jnp.float32)
    grad_mlp = jnp.dot(grad_pre_half, up_w.T, preferred_element_type=jnp.float32)
    grad_resid = grad_out + norm_back(grad_mlp, mlp_norm, mlp_inv, gains[1])
    resid_half = grad_resid.astype(jnp.bfloat16)
    grad_outw = jnp.dot(context.T, resid_half, preferred_element_type=jnp.float32)
    grad_context = jnp.dot(resid_half, out_w.T, preferred_element_type=jnp.float32).astype(jnp.bfloat16).reshape(LEN, HEADS, HD)
    queries = projected[0].reshape(LEN, HEADS, HD)
    keys_all = projected[1].reshape(LEN, HEADS, HD)
    values_all = projected[2].reshape(LEN, HEADS, HD)
    att_prob = jnp.exp(masked_scores(queries, keys_all, seq_length) - log_total)
    grad_prob = jnp.einsum('qhd,khd->hqk', widen_half(grad_context), widen_half(values_all))
    grad_values = jnp.einsum('hqk,qhd->khd', widen_half(att_prob.astype(jnp.bfloat16)), widen_half(grad_context))
    row_delta = lax.optimization_barrier(jnp.sum(att_prob * grad_prob, axis=-1, keepdims=True))
    grad_scores = (att_prob * (grad_prob - row_delta) * 0.125).astype(jnp.bfloat16)
    grad_queries = jnp.einsum('hqk,khd->qhd', widen_half(grad_scores), widen_half(keys_all))
    grad_keys = jnp.einsum('hqk,qhd->khd', widen_half(grad_scores), widen_half(queries))
    grad_proj = jnp.stack([grad_queries, grad_keys, grad_values]).reshape(3, LEN, HEADS * HD)
    grad_bias = jnp.stack([lax.optimization_barrier(jnp.sum(grad_proj[0], axis=0)), lax.optimization_barrier(jnp.sum(grad_proj[2], axis=0))])
    proj_half = grad_proj.astype(jnp.bfloat16)
    grad_qkv = jnp.einsum('rd,crw->cdw', widen_half(attn_rows), widen_half(proj_half))
    grad_attn = jnp.einsum('crw,cdw->rd', widen_half(proj_half), widen_half(qkv_w))
    grad_in = grad_resid + norm_back(grad_attn, attn_norm, attn_inv, gains[0])
    grad_gains = jnp.stack([lax.optimization_barrier(jnp.sum(grad_attn * attn_norm, axis=0)), lax.optimization_barrier(jnp.sum(grad_mlp * mlp_norm, axis=0))])
    grad_shifts = jnp.stack([lax.optimization_barrier(jnp.sum(grad_attn, axis=0)), lax.optimization_barrier(jnp.sum(grad_resid, axis=0)), lax.optimization_barrier(jnp.sum(grad_mlp, axis=0)), lax.optimization_barrier(jnp.sum(grad_out, axis=0))])
    return (grad_in, (grad_qkv, grad_bias, grad_outw, grad_up, lax.optimization_barrier(jnp.sum(grad_pre, axis=0)), grad_down, grad_gains, grad_shifts))

def reference(section_in, lengths, qkv_weight, qv_bias, out_weight, up_weight, up_bias, down_weight, norm_gains, row_biases):
    blocks = (qkv_weight, qv_bias, out_weight, up_weight, up_bias, down_weight, norm_gains, row_biases)
    layer_zero = tuple((array[0] for array in blocks))
    layer_one = tuple((array[1] for array in blocks))
    seq_inputs = section_in[0].reshape(-1, LEN, D)
    seq_cots = section_in[1].reshape(-1, LEN, D)
    seq_lengths = lengths.reshape(-1)
    zero_sums = tuple((jnp.zeros(array.shape[1:], jnp.float32) for array in blocks))

    def one_sequence(carry, item):
        sums_zero, sums_one = carry
        seq_in, seq_cot, seq_length = item
        out_zero, saved_zero = layer_forward(seq_in, seq_length, layer_zero)
        hidden_one = out_zero.astype(jnp.bfloat16)
        out_one, saved_one = layer_forward(hidden_one, seq_length, layer_one)
        grad_one, terms_one = layer_backward(seq_cot.astype(jnp.float32), saved_one, seq_length, layer_one)
        grad_zero, terms_zero = layer_backward(widen_half(grad_one.astype(jnp.bfloat16)), saved_zero, seq_length, layer_zero)
        sums_zero = tuple((total + term for total, term in zip(sums_zero, terms_zero)))
        sums_one = tuple((total + term for total, term in zip(sums_one, terms_one)))
        return ((sums_zero, sums_one), (grad_zero, out_one))
    (sums_zero, sums_one), (grad_inputs, outputs) = lax.scan(one_sequence, (zero_sums, zero_sums), (seq_inputs, seq_cots, seq_lengths))
    section_out = jnp.stack([grad_inputs, outputs]).reshape(section_in.shape)
    grads = tuple((jnp.stack([first_term, second_term]) for first_term, second_term in zip(sums_zero, sums_one)))
    return (section_out, grads[0], grads[1], grads[2], grads[3], grads[4], grads[5], grads[6], grads[7])
```

```python
import jax
import jax.numpy as jnp
from jax import lax
from jax.sharding import Mesh
from jax.sharding import PartitionSpec as P

HEADS = 16
HD = 64
LEN = 128
norm_eps = 1e-05

f32 = jnp.float32
bf16 = jnp.bfloat16

SWAP = ((0, 1), (1, 0))
PAIR_E = ((0, 1), (1, 0), (2, 3), (3, 2))
PAIR_F = ((0, 3), (3, 0), (1, 2), (2, 1))
ORDERS = (
    (("y", "E"), ("y", "F"), ("z", "E"), ("z", "F"), ("xh", "X")),
    (("y", "F"), ("y", "E"), ("z", "F"), ("z", "E"), ("xh", "X")),
    (("z", "E"), ("z", "F"), ("y", "E"), ("y", "F"), ("xh", "X")),
    (("z", "F"), ("z", "E"), ("y", "F"), ("y", "E"), ("xh", "X")),
)
PAIRS = {"E": PAIR_E, "F": PAIR_F, "X": SWAP}


def gelu_tanh(pre_act):
    return (
        0.5
        * pre_act
        * (1.0 + jnp.tanh(0.7978845608028654 * (pre_act + 0.044715 * pre_act * pre_act * pre_act)))
    )


def norm_stats(values):
    centred = values - jnp.mean(values, axis=-1, keepdims=True)
    inv_std = lax.rsqrt(jnp.mean(centred * centred, axis=-1, keepdims=True) + norm_eps)
    return centred * inv_std, inv_std


def norm_back(grad_norm, normed, inv_std, gain):
    scaled = grad_norm * gain
    return inv_std * (
        scaled
        - jnp.mean(scaled, axis=-1, keepdims=True)
        - normed * jnp.mean(scaled * normed, axis=-1, keepdims=True)
    )


def dot(form, left, right):
    return jnp.einsum(form, left, right, preferred_element_type=f32)


def step_bit(axis, kind):
    index = lax.axis_index(axis)
    if kind == "E":
        return (index ^ (index >> 1)) & 1
    if kind == "F":
        return (index >> 1) & 1
    return index


def reduce_parts(parts):
    shaped = [part.reshape((2, 2, 2, 2, 2, part.shape[0] // 32, part.shape[1])) for part in parts]
    for level in range(5):
        received = []
        kept = []
        for value, order in zip(shaped, ORDERS):
            axis, kind = order[level]
            bit = step_bit(axis, kind)
            kept.append(lax.dynamic_index_in_dim(value, bit, 0, keepdims=False))
            sent = lax.dynamic_index_in_dim(value, 1 - bit, 0, keepdims=False).astype(bf16)
            received.append(lax.ppermute(sent, axis, PAIRS[kind]))
        shaped = [own + other.astype(f32) for own, other in zip(kept, received)]
    return shaped


def gather_parts(chunks, layer):
    values = [chunk[:, None] for chunk in chunks]
    for level in range(4, -1, -1):
        grown = []
        for value, order in zip(values, ORDERS):
            axis, kind = order[level]
            bit = step_bit(axis, kind)
            size = lax.axis_size(axis)
            pairs = [(layer * size + s, layer * size + d) for s, d in PAIRS[kind]]
            other = lax.ppermute(value, ("pipe", axis), pairs)
            grown.append(
                jnp.where(
                    bit == 0,
                    jnp.concatenate([value, other], axis=1),
                    jnp.concatenate([other, value], axis=1),
                )
            )
        values = grown
    return values


def local(
    section_in,
    lengths,
    qkv_weight,
    qv_bias,
    out_weight,
    up_weight,
    up_bias,
    down_weight,
    norm_gains,
    row_biases,
):
    core = lax.axis_index("pipe")
    tensor_index = lax.axis_index("tensor")
    place = core * 2 + tensor_index
    both = ("pipe", "tensor")

    own_rows = section_in[0, 0, 0]
    near = lax.ppermute(own_rows, both, ((0, 1), (1, 2)))
    far = lax.ppermute(own_rows, both, ((1, 3),))
    layer_in = jnp.where(place == 0, own_rows, jnp.where(place == 3, far, near))

    owned = (
        qkv_weight[0],
        out_weight[0],
        up_weight[0],
        down_weight[0],
        qv_bias[0],
        up_bias[0],
        norm_gains[0],
        row_biases[0],
    )
    other = tuple(lax.ppermute(array, "pipe", SWAP) for array in owned)
    layers = tuple(
        tuple(jnp.where(core == layer, mine, theirs) for mine, theirs in zip(owned, other))
        for layer in range(2)
    )
    cot_near = lax.ppermute(own_rows, both, ((2, 0), (3, 2)))
    cot_far = lax.ppermute(own_rows, both, ((2, 1),))
    cotangent = jnp.where(place == 3, own_rows, jnp.where(place == 1, cot_far, cot_near))

    seq_length = jnp.where(core == 0, lengths[0, 0], lengths[0, 1])
    heads_dev = HEADS // 2
    head_ids = tensor_index * heads_dev + jnp.arange(heads_dev) + 1
    slopes = 2.0 ** (-8.0 * head_ids.astype(f32) / HEADS)
    offsets = (jnp.arange(LEN)[:, None] - jnp.arange(LEN)[None, :]).astype(f32)
    allowed = (offsets >= 0) & (jnp.arange(LEN)[None, :] < seq_length)
    penalty = slopes[:, None, None] * offsets

    def split_heads(block):
        return block.reshape(LEN, heads_dev, HD)

    def masked_scores(projected):
        scores = (
            dot("qhd,khd->hqk", split_heads(projected[0]), split_heads(projected[1])) * 0.125
            - penalty
        )
        return jnp.where(allowed[None], scores, -jnp.inf)

    def tensor_sum(partial):
        swapped = lax.ppermute(partial.astype(bf16), "tensor", SWAP)
        return partial + swapped.astype(f32)

    def layer_forward(rows, params):
        qkv_w, out_w, up_w, down_w, qv_b, up_b, gains, shifts = params
        wide = rows.astype(f32)
        attn_norm, attn_inv = norm_stats(wide)
        attn_rows = (attn_norm * gains[0] + shifts[0]).astype(bf16)
        bias_three = jnp.stack([qv_b[0], jnp.zeros_like(qv_b[0]), qv_b[1]]).astype(f32)[:, None, :]
        projected = (dot("rd,cdw->crw", attn_rows, qkv_w) + bias_three).astype(bf16)
        scores = masked_scores(projected)
        top_score = jnp.max(scores, axis=-1, keepdims=True)
        exp_scores = jnp.exp(scores - top_score)
        totals = jnp.sum(exp_scores, axis=-1, keepdims=True)
        prob = exp_scores / totals
        context = (
            dot("hqk,khd->qhd", prob.astype(bf16), split_heads(projected[2]))
            .reshape(LEN, heads_dev * HD)
            .astype(bf16)
        )
        residual = wide + tensor_sum(dot("rw,wd->rd", context, out_w)) + shifts[1]
        mlp_norm, mlp_inv = norm_stats(residual)
        mlp_rows = (mlp_norm * gains[1] + shifts[2]).astype(bf16)
        pre_gelu = dot("rd,df->rf", mlp_rows, up_w) + up_b.astype(f32)
        activated = gelu_tanh(pre_gelu).astype(bf16)
        layer_out = residual + tensor_sum(dot("rf,fd->rd", activated, down_w)) + shifts[3]
        saved = (
            attn_norm,
            attn_inv,
            attn_rows,
            projected,
            prob,
            context,
            mlp_norm,
            mlp_inv,
            mlp_rows,
            pre_gelu,
            activated,
        )
        return layer_out, saved

    def half_of(block, which):
        width = block.shape[1] // 2
        return lax.dynamic_slice_in_dim(block, which * width, width, 1)

    def weight_grad(left, right):
        kept = half_of(left, core)
        sent = half_of(left, 1 - core)
        left_far = lax.ppermute(sent, "pipe", SWAP)
        right_far = lax.ppermute(right, "pipe", SWAP)
        form = "rx,ry->xy" if right.ndim == 2 else "rx,cry->cxy"
        return dot(form, kept, right) + dot(form, left_far, right_far)

    def layer_backward(grad_out, saved, params, layer):
        qkv_w, out_w, up_w, down_w, qv_b, up_b, gains, shifts = params
        (
            attn_norm,
            attn_inv,
            attn_rows,
            projected,
            prob,
            context,
            mlp_norm,
            mlp_inv,
            mlp_rows,
            pre_gelu,
            activated,
        ) = saved
        grad_half = grad_out.astype(bf16)
        grad_act = dot("rd,fd->rf", grad_half, down_w)
        _, pull_back = jax.vjp(gelu_tanh, pre_gelu)
        grad_pre = pull_back(grad_act)[0]
        grad_pre_half = grad_pre.astype(bf16)
        grad_mlp = tensor_sum(dot("rf,df->rd", grad_pre_half, up_w))
        grad_down = weight_grad(activated, grad_half)
        grad_up = weight_grad(mlp_rows, grad_pre_half)
        early = reduce_parts([grad_down[:256], grad_down[256:], grad_up[:256], grad_up[256:]])
        grad_resid = grad_out + norm_back(grad_mlp, mlp_norm, mlp_inv, gains[1])
        resid_half = grad_resid.astype(bf16)
        grad_context = split_heads(dot("rd,wd->rw", resid_half, out_w).astype(bf16))
        queries = split_heads(projected[0])
        keys_all = split_heads(projected[1])
        values_all = split_heads(projected[2])
        grad_prob = dot("qhd,khd->hqk", grad_context, values_all)
        grad_values = dot("hqk,qhd->khd", prob.astype(bf16), grad_context)
        row_delta = jnp.sum(prob * grad_prob, axis=-1, keepdims=True)
        grad_scores = (prob * (grad_prob - row_delta) * 0.125).astype(bf16)
        grad_queries = dot("hqk,khd->qhd", grad_scores, keys_all)
        grad_keys = dot("hqk,qhd->khd", grad_scores, queries)
        grad_proj = jnp.stack([grad_queries, grad_keys, grad_values]).reshape(
            3, LEN, heads_dev * HD
        )
        proj_half = grad_proj.astype(bf16)
        grad_attn = tensor_sum(dot("crw,cdw->rd", proj_half, qkv_w))
        grad_out_w = weight_grad(context, resid_half)
        grad_qkv = weight_grad(attn_rows, proj_half)
        late = reduce_parts([grad_qkv[0], grad_qkv[1], grad_qkv[2], grad_out_w])
        grad_in = grad_resid + norm_back(grad_attn, attn_norm, attn_inv, gains[0])
        vectors = jnp.stack(
            [
                jnp.concatenate([jnp.sum(grad_proj[0], axis=0), jnp.sum(grad_proj[2], axis=0)]),
                jnp.sum(grad_pre, axis=0),
                jnp.sum(grad_attn * attn_norm, axis=0),
                jnp.sum(grad_mlp * mlp_norm, axis=0),
                jnp.sum(grad_attn, axis=0),
                jnp.sum(grad_resid, axis=0),
                jnp.sum(grad_mlp, axis=0),
                jnp.sum(grad_out, axis=0),
            ]
        )

        def gathered(chunks):
            pairs = []
            for chunk in chunks:
                mine = chunk.astype(bf16).reshape(chunk.shape[-2:])
                theirs = lax.ppermute(mine, "pipe", ((1 - layer, layer),))
                pairs.append(jnp.stack([mine, theirs] if layer == 0 else [theirs, mine]))
            return gather_parts(pairs, layer)

        down_a, down_b, up_a, up_b_ = gathered(early)
        query_g, key_g, value_g, out_g = gathered(late)
        qkv_all = jnp.stack([query_g, key_g, value_g]).reshape(3, 1024, 512)
        out_all = out_g.reshape(512, 1024)
        up_all = jnp.stack([up_a, up_b_], axis=1).reshape(1024, 1024)
        down_all = jnp.stack([down_a, down_b], axis=1).reshape(1024, 1024)
        return grad_in, vectors, (qkv_all, out_all, up_all, down_all)

    out_zero, saved_zero = layer_forward(layer_in, layers[0])
    out_one, saved_one = layer_forward(out_zero.astype(bf16), layers[1])
    grad_one, vectors_one, weights_one = layer_backward(
        cotangent.astype(f32), saved_one, layers[1], 1
    )
    grad_zero, vectors_zero, weights_zero = layer_backward(
        grad_one.astype(bf16).astype(f32), saved_zero, layers[0], 0
    )

    first = core == 0
    swapped = lax.ppermute(jnp.where(first, vectors_one, vectors_zero), "pipe", SWAP)
    vectors = jnp.where(first, vectors_zero, vectors_one) + swapped
    for axis, kind in ORDERS[0]:
        vectors = vectors + lax.ppermute(vectors, axis, PAIRS[kind])
    shared = vectors[2:]
    shared = 0.5 * (shared + lax.ppermute(shared, "tensor", SWAP))

    crossing = lax.ppermute(jnp.where(first, out_one, grad_zero), both, ((0, 2), (3, 1)))
    kept_rows = jnp.where(first, grad_zero, out_one)
    section_out = jnp.where(core == tensor_index, kept_rows, crossing)
    qkv_g, out_g, up_g, down_g = (
        jnp.where(first, zero, one).astype(f32) for zero, one in zip(weights_zero, weights_one)
    )
    return (
        section_out[None, None, None],
        qkv_g[None],
        vectors[0].reshape(1, 2, 512),
        out_g[None],
        up_g[None],
        vectors[1][None],
        down_g[None],
        shared[:2][None],
        shared[2:][None],
    )


def solution(mesh):
    fine = Mesh(mesh.devices.reshape(2, 2, 4, 4, 2), ("pipe", "tensor", "y", "z", "xh"))
    dp = ("y", "z", "xh")
    in_specs = (
        P("pipe", dp, "tensor", None, None),
        P(dp, None),
        P("pipe", None, None, "tensor"),
        P("pipe", None, "tensor"),
        P("pipe", "tensor", None),
        P("pipe", None, "tensor"),
        P("pipe", "tensor"),
        P("pipe", "tensor", None),
        P("pipe", None, None),
        P("pipe", None, None),
    )
    out_specs = (
        P("pipe", dp, "tensor", None, None),
        P("pipe", None, None, "tensor"),
        P("pipe", None, "tensor"),
        P("pipe", "tensor", None),
        P("pipe", None, "tensor"),
        P("pipe", "tensor"),
        P("pipe", "tensor", None),
        P("pipe", None, None),
        P("pipe", None, None),
    )
    return jax.shard_map(local, mesh=fine, in_specs=in_specs, out_specs=out_specs, check_vma=False)
```

```python
import jax
import jax.numpy as jnp
from jax import lax
from jax.sharding import Mesh
from jax.sharding import PartitionSpec as P

HEADS = 16
HD = 64
LEN = 128
norm_eps = 1e-05

f32 = jnp.float32
bf16 = jnp.bfloat16

SWAP = ((0, 1), (1, 0))
PAIR_E = ((0, 1), (1, 0), (2, 3), (3, 2))
PAIR_F = ((0, 3), (3, 0), (1, 2), (2, 1))
DP = ("y", "z", "xh")
ROUNDS = (("y", PAIR_E), ("y", PAIR_F), ("z", PAIR_E), ("z", PAIR_F), ("xh", SWAP))


def gelu_tanh(pre_act):
    return (
        0.5
        * pre_act
        * (1.0 + jnp.tanh(0.7978845608028654 * (pre_act + 0.044715 * pre_act * pre_act * pre_act)))
    )


def norm_stats(values):
    centred = values - jnp.mean(values, axis=-1, keepdims=True)
    inv_std = lax.rsqrt(jnp.mean(centred * centred, axis=-1, keepdims=True) + norm_eps)
    return centred * inv_std, inv_std


def norm_back(grad_norm, normed, inv_std, gain):
    scaled = grad_norm * gain
    return inv_std * (
        scaled
        - jnp.mean(scaled, axis=-1, keepdims=True)
        - normed * jnp.mean(scaled * normed, axis=-1, keepdims=True)
    )


def dot(form, left, right):
    return jnp.einsum(form, left, right, preferred_element_type=f32)


def reduced(packed):
    ranks = lax.axis_size(DP)
    rows, columns = packed.shape
    pieces = packed.astype(bf16).reshape(ranks, rows // ranks, columns)
    pieces = lax.all_to_all(pieces, DP, split_axis=0, concat_axis=0, tiled=True)
    total = jnp.sum(pieces.astype(f32), axis=0).astype(bf16)
    spread = jnp.broadcast_to(total[None], (ranks,) + total.shape)
    return lax.all_to_all(spread, DP, split_axis=0, concat_axis=0, tiled=True)


def local(
    section_in,
    lengths,
    qkv_weight,
    qv_bias,
    out_weight,
    up_weight,
    up_bias,
    down_weight,
    norm_gains,
    row_biases,
):
    core = lax.axis_index("pipe")
    tensor_index = lax.axis_index("tensor")
    place = core * 2 + tensor_index
    both = ("pipe", "tensor")

    own_rows = section_in[0, 0, 0]
    near = lax.ppermute(own_rows, both, ((0, 1), (1, 2)))
    far = lax.ppermute(own_rows, both, ((1, 3),))
    layer_in = jnp.where(place == 0, own_rows, jnp.where(place == 3, far, near))

    owned = (
        qkv_weight[0],
        out_weight[0],
        up_weight[0],
        down_weight[0],
        qv_bias[0],
        up_bias[0],
        norm_gains[0],
        row_biases[0],
    )
    small = jnp.concatenate(
        [owned[4].astype(f32).reshape(1, -1), owned[5].astype(f32)[None], owned[6], owned[7]]
    )
    small_far = lax.ppermute(small, "pipe", SWAP)
    other = tuple(lax.ppermute(array, "pipe", SWAP) for array in owned[:4]) + (
        small_far[0].reshape(2, -1),
        small_far[1],
        small_far[2:4],
        small_far[4:8],
    )
    layers = tuple(
        tuple(jnp.where(core == layer, mine, theirs) for mine, theirs in zip(owned, other))
        for layer in range(2)
    )
    cot_near = lax.ppermute(own_rows, both, ((2, 0), (3, 2)))
    cot_far = lax.ppermute(own_rows, both, ((2, 1),))
    cotangent = jnp.where(place == 3, own_rows, jnp.where(place == 1, cot_far, cot_near))

    seq_length = jnp.where(core == 0, lengths[0, 0], lengths[0, 1])
    heads_dev = HEADS // 2
    head_ids = tensor_index * heads_dev + jnp.arange(heads_dev) + 1
    slopes = 2.0 ** (-8.0 * head_ids.astype(f32) / HEADS)
    offsets = (jnp.arange(LEN)[:, None] - jnp.arange(LEN)[None, :]).astype(f32)
    allowed = (offsets >= 0) & (jnp.arange(LEN)[None, :] < seq_length)
    penalty = slopes[:, None, None] * offsets

    def split_heads(block):
        return block.reshape(LEN, heads_dev, HD)

    def masked_scores(projected):
        scores = (
            dot("qhd,khd->hqk", split_heads(projected[0]), split_heads(projected[1])) * 0.125
            - penalty
        )
        return jnp.where(allowed[None], scores, -jnp.inf)

    def tensor_sum(partial):
        swapped = lax.ppermute(partial.astype(bf16), "tensor", SWAP)
        return partial + swapped.astype(f32)

    def layer_forward(rows, params):
        qkv_w, out_w, up_w, down_w, qv_b, up_b, gains, shifts = params
        wide = rows.astype(f32)
        attn_norm, attn_inv = norm_stats(wide)
        attn_rows = (attn_norm * gains[0] + shifts[0]).astype(bf16)
        bias_three = jnp.stack([qv_b[0], jnp.zeros_like(qv_b[0]), qv_b[1]])[:, None, :]
        projected = (dot("rd,cdw->crw", attn_rows, qkv_w) + bias_three).astype(bf16)
        scores = masked_scores(projected)
        top_score = jnp.max(scores, axis=-1, keepdims=True)
        exp_scores = jnp.exp(scores - top_score)
        totals = jnp.sum(exp_scores, axis=-1, keepdims=True)
        prob = exp_scores / totals
        context = (
            dot("hqk,khd->qhd", prob.astype(bf16), split_heads(projected[2]))
            .reshape(LEN, heads_dev * HD)
            .astype(bf16)
        )
        residual = wide + tensor_sum(dot("rw,wd->rd", context, out_w)) + shifts[1]
        mlp_norm, mlp_inv = norm_stats(residual)
        mlp_rows = (mlp_norm * gains[1] + shifts[2]).astype(bf16)
        pre_gelu = dot("rd,df->rf", mlp_rows, up_w) + up_b
        activated = gelu_tanh(pre_gelu).astype(bf16)
        layer_out = residual + tensor_sum(dot("rf,fd->rd", activated, down_w)) + shifts[3]
        saved = (
            attn_norm,
            attn_inv,
            attn_rows,
            projected,
            prob,
            context,
            mlp_norm,
            mlp_inv,
            mlp_rows,
            pre_gelu,
            activated,
        )
        return layer_out, saved

    def halves(block):
        width = block.shape[1] // 2
        kept = lax.dynamic_slice_in_dim(block, core * width, width, 1)
        return kept, lax.dynamic_slice_in_dim(block, (1 - core) * width, width, 1)

    def exchanged(*blocks):
        packed = lax.ppermute(jnp.concatenate(blocks, axis=1), "pipe", SWAP)
        edges = [0]
        for block in blocks:
            edges.append(edges[-1] + block.shape[1])
        return [packed[:, start:end] for start, end in zip(edges, edges[1:])]

    def outer(left, right, left_far, right_far):
        return dot("rx,ry->xy", left, right) + dot("rx,ry->xy", left_far, right_far)

    def layer_backward(grad_out, saved, params, layer):
        qkv_w, out_w, up_w, down_w, qv_b, up_b, gains, shifts = params
        (
            attn_norm,
            attn_inv,
            attn_rows,
            projected,
            prob,
            context,
            mlp_norm,
            mlp_inv,
            mlp_rows,
            pre_gelu,
            activated,
        ) = saved
        grad_half = grad_out.astype(bf16)
        grad_act = dot("rd,fd->rf", grad_half, down_w)
        _, pull_back = jax.vjp(gelu_tanh, pre_gelu)
        grad_pre = pull_back(grad_act)[0]
        grad_pre_half = grad_pre.astype(bf16)
        grad_mlp = tensor_sum(dot("rf,df->rd", grad_pre_half, up_w))
        act_kept, act_sent = halves(activated)
        mlp_kept, mlp_sent = halves(mlp_rows)
        act_far, grad_far, mlp_far, pre_far = exchanged(act_sent, grad_half, mlp_sent, grad_pre_half)
        grad_down = outer(act_kept, grad_half, act_far, grad_far)
        grad_up = outer(mlp_kept, grad_pre_half, mlp_far, pre_far)
        early = reduced(jnp.concatenate([grad_down, grad_up], axis=0)).reshape(2, 512, 1024)
        grad_resid = grad_out + norm_back(grad_mlp, mlp_norm, mlp_inv, gains[1])
        resid_half = grad_resid.astype(bf16)
        grad_context = split_heads(dot("rd,wd->rw", resid_half, out_w).astype(bf16))
        queries = split_heads(projected[0])
        keys_all = split_heads(projected[1])
        values_all = split_heads(projected[2])
        grad_prob = dot("qhd,khd->hqk", grad_context, values_all)
        grad_values = dot("hqk,qhd->khd", prob.astype(bf16), grad_context)
        row_delta = jnp.sum(prob * grad_prob, axis=-1, keepdims=True)
        grad_scores = (prob * (grad_prob - row_delta) * 0.125).astype(bf16)
        grad_queries = dot("hqk,khd->qhd", grad_scores, keys_all)
        grad_keys = dot("hqk,qhd->khd", grad_scores, queries)
        grad_proj = jnp.stack([grad_queries, grad_keys, grad_values]).reshape(
            3, LEN, heads_dev * HD
        )
        proj_half = grad_proj.astype(bf16)
        grad_attn = tensor_sum(dot("crw,cdw->rd", proj_half, qkv_w))
        resid_kept, resid_sent = halves(resid_half)
        attn_kept, attn_sent = halves(attn_rows)
        context_far, resid_far, attn_far, *proj_far = exchanged(
            context, resid_sent, attn_sent, proj_half[0], proj_half[1], proj_half[2]
        )
        grads = [outer(attn_kept, proj_half[i], attn_far, proj_far[i]) for i in range(3)]
        grads.append(outer(context, resid_kept, context_far, resid_far))
        late = reduced(jnp.concatenate(grads, axis=0)).reshape(4, 512, 512)
        grad_in = grad_resid + norm_back(grad_attn, attn_norm, attn_inv, gains[0])
        vectors = jnp.stack(
            [
                jnp.concatenate([jnp.sum(grad_proj[0], axis=0), jnp.sum(grad_proj[2], axis=0)]),
                jnp.sum(grad_pre, axis=0),
                jnp.sum(grad_attn * attn_norm, axis=0),
                jnp.sum(grad_mlp * mlp_norm, axis=0),
                jnp.sum(grad_attn, axis=0),
                jnp.sum(grad_resid, axis=0),
                jnp.sum(grad_mlp, axis=0),
                jnp.sum(grad_out, axis=0),
            ]
        )

        def both_halves(mine):
            theirs = lax.ppermute(mine, "pipe", ((1 - layer, layer),))
            return (mine, theirs) if layer == 0 else (theirs, mine)

        early = both_halves(early)
        late = both_halves(late)
        return (
            grad_in,
            vectors,
            (
                jnp.concatenate([half[:3] for half in late], axis=1),
                jnp.concatenate([half[3] for half in late], axis=1),
                jnp.concatenate([half[1] for half in early], axis=0),
                jnp.concatenate([half[0] for half in early], axis=0),
            ),
        )

    out_zero, saved_zero = layer_forward(layer_in, layers[0])
    out_one, saved_one = layer_forward(out_zero.astype(bf16), layers[1])
    grad_one, vectors_one, weights_one = layer_backward(
        cotangent.astype(f32), saved_one, layers[1], 1
    )
    grad_zero, vectors_zero, weights_zero = layer_backward(
        grad_one.astype(bf16).astype(f32), saved_zero, layers[0], 0
    )

    first = core == 0
    swapped = lax.ppermute(jnp.where(first, vectors_one, vectors_zero), "pipe", SWAP)
    vectors = jnp.where(first, vectors_zero, vectors_one) + swapped
    for axis, pairs in ROUNDS:
        vectors = vectors + lax.ppermute(vectors, axis, pairs)
    shared = vectors[2:]
    shared = 0.5 * (shared + lax.ppermute(shared, "tensor", SWAP))

    crossing = lax.ppermute(jnp.where(first, out_one, grad_zero), both, ((0, 2), (3, 1)))
    kept_rows = jnp.where(first, grad_zero, out_one)
    section_out = jnp.where(core == tensor_index, kept_rows, crossing)
    qkv_g, out_g, up_g, down_g = (
        jnp.where(first, zero, one).astype(f32) for zero, one in zip(weights_zero, weights_one)
    )
    return (
        section_out[None, None, None],
        qkv_g[None],
        vectors[0].reshape(1, 2, 512),
        out_g[None],
        up_g[None],
        vectors[1][None],
        down_g[None],
        shared[:2][None],
        shared[2:][None],
    )


def solution(mesh):
    fine = Mesh(mesh.devices.reshape(2, 2, 4, 4, 2), ("pipe", "tensor", "y", "z", "xh"))
    dp = ("y", "z", "xh")
    in_specs = (
        P("pipe", dp, "tensor", None, None),
        P(dp, None),
        P("pipe", None, None, "tensor"),
        P("pipe", None, "tensor"),
        P("pipe", "tensor", None),
        P("pipe", None, "tensor"),
        P("pipe", "tensor"),
        P("pipe", "tensor", None),
        P("pipe", None, None),
        P("pipe", None, None),
    )
    out_specs = (
        P("pipe", dp, "tensor", None, None),
        P("pipe", None, None, "tensor"),
        P("pipe", None, "tensor"),
        P("pipe", "tensor", None),
        P("pipe", None, "tensor"),
        P("pipe", "tensor"),
        P("pipe", "tensor", None),
        P("pipe", None, None),
        P("pipe", None, None),
    )
    return jax.shard_map(local, mesh=fine, in_specs=in_specs, out_specs=out_specs, check_vma=False)
```

```python
import jax
import jax.numpy as jnp
from jax import lax
from jax.experimental import pallas as pl
from jax.experimental.pallas import tpu as pltpu
from jax.sharding import Mesh
from jax.sharding import PartitionSpec as P

HEADS = 16
HD = 64
LEN = 128
norm_eps = 1e-05

f32 = jnp.float32
bf16 = jnp.bfloat16

SWAP = ((0, 1), (1, 0))
PAIR_E = ((0, 1), (1, 0), (2, 3), (3, 2))
PAIR_F = ((0, 3), (3, 0), (1, 2), (2, 1))
DP = ("y", "z", "xh")
ROUNDS = (("y", PAIR_E), ("y", PAIR_F), ("z", PAIR_E), ("z", PAIR_F), ("xh", SWAP))


GELU_A = 0.7978845608028654
GELU_B = 0.044715
WIDTH = 1024
HEADS_DEV = HEADS // 2
LOCAL = HEADS_DEV * HD
PAIR = 2 * HD


def matmul(left, right):
    return jnp.dot(left, right, preferred_element_type=f32)


def matmul_nt(left, right):
    return lax.dot_general(left, right, (((1,), (1,)), ((), ())), preferred_element_type=f32)


def matmul_tn(left, right):
    return lax.dot_general(left, right, (((0,), (0,)), ((), ())), preferred_element_type=f32)


def norm_stats(values):
    centred = values - jnp.mean(values, axis=-1, keepdims=True)
    inv_std = lax.rsqrt(jnp.mean(centred * centred, axis=-1, keepdims=True) + norm_eps)
    return centred * inv_std, inv_std


def norm_back(grad_norm, normed, inv_std, gain):
    scaled = grad_norm * gain
    return inv_std * (
        scaled
        - jnp.mean(scaled, axis=-1, keepdims=True)
        - normed * jnp.mean(scaled * normed, axis=-1, keepdims=True)
    )


QV, UP_B, GAIN_A, GAIN_M, SHIFT_A, SHIFT_O, SHIFT_M, SHIFT_D = range(8)


def row(table, index):
    return table[index : index + 1, :]


def table_of(rows):
    zero = jnp.zeros((1, WIDTH), f32)
    return jnp.concatenate([rows.get(index, zero) for index in range(8)], axis=0)


def column_sum(block):
    return jnp.sum(block, axis=0, keepdims=True)


def head_lanes():
    return lax.broadcasted_iota(jnp.int32, (LEN, PAIR), 1) < HD


def attention_rows(rows, table, core, slopes, qkv_w, out_w, outs):
    attn_rows_ref, proj_ref, prob_ref, context_ref, part_ref, sent_ref = outs
    normed, _ = norm_stats(rows.astype(f32))
    attn_rows = (normed * row(table, GAIN_A) + row(table, SHIFT_A)).astype(bf16)
    attn_rows_ref[...] = attn_rows
    for c in range(3):
        block = matmul(attn_rows, qkv_w[c])
        if c == 0:
            block = block + table[QV : QV + 1, :LOCAL]
        if c == 2:
            block = block + table[QV : QV + 1, LOCAL:]
        proj_ref[c] = block.astype(bf16)
    spot_i = lax.broadcasted_iota(jnp.int32, (LEN, LEN), 0)
    spot_j = lax.broadcasted_iota(jnp.int32, (LEN, LEN), 1)
    allowed = (spot_j <= spot_i) & (spot_j < core[1])
    offsets = (spot_i - spot_j).astype(f32)
    first = head_lanes()
    for pair in range(HEADS_DEV // 2):
        lanes = slice(pair * PAIR, (pair + 1) * PAIR)
        query, key, value = (proj_ref[c, :, lanes] for c in range(3))
        found = []
        for side in range(2):
            head = 2 * pair + side
            mine = jnp.where(first if side == 0 else ~first, query, jnp.zeros_like(query))
            scores = matmul_nt(mine, key) * 0.125 - slopes[head] * offsets
            scores = jnp.where(allowed, scores, -jnp.inf)
            top_score = jnp.max(scores, axis=-1, keepdims=True)
            exp_scores = jnp.exp(scores - top_score)
            prob = exp_scores / jnp.sum(exp_scores, axis=-1, keepdims=True)
            prob_ref[head] = prob
            found.append(matmul(prob.astype(bf16), value))
        context_ref[:, lanes] = jnp.where(first, found[0], found[1]).astype(bf16)
    part = matmul(context_ref[...], out_w[...])
    part_ref[...] = part
    sent_ref[...] = part.astype(bf16)


def first_attention(core, slopes, rows, table, qkv_w, out_w, *outs):
    attention_rows(rows[...], table, core, slopes, qkv_w, out_w, outs)


def next_attention(
    core, slopes, resid, part, received, below, table, qkv_w, out_w, out_ref, rows_ref, *outs
):
    layer_out = resid[...] + (part[...] + received[...].astype(f32)) + row(below, SHIFT_D)
    out_ref[...] = layer_out
    rows = layer_out.astype(bf16)
    rows_ref[...] = rows
    attention_rows(rows, table, core, slopes, qkv_w, out_w, outs)


def mlp_forward(
    rows, part, received, table, up_w, down_w, resid_ref, mlp_ref, pre_ref, act_ref, out_ref, sent_ref
):
    resid = (
        rows[...].astype(f32) + (part[...] + received[...].astype(f32)) + row(table, SHIFT_O)
    )
    resid_ref[...] = resid
    normed, _ = norm_stats(resid)
    mlp_rows = (normed * row(table, GAIN_M) + row(table, SHIFT_M)).astype(bf16)
    mlp_ref[...] = mlp_rows
    pre = matmul(mlp_rows, up_w[...]) + row(table, UP_B)
    pre_ref[...] = pre
    act = (0.5 * pre * (1.0 + jnp.tanh(GELU_A * (pre + GELU_B * pre * pre * pre)))).astype(bf16)
    act_ref[...] = act
    out = matmul(act, down_w[...])
    out_ref[...] = out
    sent_ref[...] = out.astype(bf16)


def last_output(resid, part, received, table, out_ref):
    out_ref[...] = resid[...] + (part[...] + received[...].astype(f32)) + row(table, SHIFT_D)


def halves(core, block):
    half = block.shape[1] // 2
    low, high = block[:, :half], block[:, half:]
    own = core[0] == 0
    return jnp.where(own, low, high), jnp.where(own, high, low)


def mlp_back_body(core, grad, pre_in, act, mlp_rows, up_w, down_w, outs):
    pre_half_ref, part_ref, sent_ref, cross_ref, sums_ref = outs
    grad_act = matmul_nt(grad, down_w[...])
    pre = pre_in[...]
    tanh = jnp.tanh(GELU_A * (pre + GELU_B * pre * pre * pre))
    slope = 0.5 * (1.0 + tanh) + 0.5 * pre * (1.0 - tanh * tanh) * (
        GELU_A * (1.0 + 3.0 * GELU_B * pre * pre)
    )
    grad_pre = grad_act * slope
    pre_half = grad_pre.astype(bf16)
    pre_half_ref[...] = pre_half
    part = matmul_nt(pre_half, up_w[...])
    part_ref[...] = part
    sent_ref[...] = part.astype(bf16)
    cross_ref[:, :512] = halves(core, act[...])[1]
    cross_ref[:, 512:1536] = grad
    cross_ref[:, 1536:2048] = halves(core, mlp_rows[...])[1]
    cross_ref[:, 2048:] = pre_half
    return column_sum(grad_pre)


def mlp_backward(core, grad, pre, act, mlp_rows, up_w, down_w, *outs):
    total = mlp_back_body(core, grad[...], pre, act, mlp_rows, up_w, down_w, outs)
    outs[4][...] = table_of({UP_B: total})


def input_grad(grad_resid, part, received, rows, table):
    grad_attn = part[...] + received[...].astype(f32)
    normed, inv_std = norm_stats(rows[...].astype(f32))
    grad_in = grad_resid[...] + norm_back(grad_attn, normed, inv_std, row(table, GAIN_A))
    sums = {GAIN_A: column_sum(grad_attn * normed), SHIFT_A: column_sum(grad_attn)}
    return grad_in, sums


def mlp_backward_below(
    core, grad_resid, da_part, da_received, above_rows, above_table,
    pre, act, mlp_rows, up_w, down_w, grad_ref, above_ref, *outs,
):
    grad_in, sums = input_grad(grad_resid, da_part, da_received, above_rows, above_table)
    above_ref[...] = table_of(sums)
    grad = grad_in.astype(bf16)
    grad_ref[...] = grad
    total = mlp_back_body(core, grad, pre, act, mlp_rows, up_w, down_w, outs)
    outs[4][...] = table_of({UP_B: total})


def last_input_grad(grad_resid, part, received, rows, table, grad_ref, sums_ref):
    grad_in, sums = input_grad(grad_resid, part, received, rows, table)
    grad_ref[...] = grad_in
    sums_ref[...] = table_of(sums)


def attention_backward(
    core, grad_out, dc_part, dc_received, resid, table, out_w, qkv_w, proj, prob_in, context, attn_rows,
    grad_ref, resid_half_ref, proj_grad_ref, part_ref, sent_ref, cross_ref, sums_ref,
):
    grad_mlp = dc_part[...] + dc_received[...].astype(f32)
    normed, inv_std = norm_stats(resid[...])
    wide_out = grad_out[...].astype(f32)
    grad_resid = wide_out + norm_back(grad_mlp, normed, inv_std, row(table, GAIN_M))
    grad_ref[...] = grad_resid
    resid_half = grad_resid.astype(bf16)
    resid_half_ref[...] = resid_half
    grad_context = matmul_nt(resid_half, out_w[...]).astype(bf16)
    first = head_lanes()
    query_sums = []
    value_sums = []
    for pair in range(HEADS_DEV // 2):
        lanes = slice(pair * PAIR, (pair + 1) * PAIR)
        query, key, value = (proj[c, :, lanes] for c in range(3))
        context_grad = grad_context[:, lanes]
        query_g, key_g, value_g = [], [], []
        for side in range(2):
            mask = first if side == 0 else ~first
            prob = prob_in[2 * pair + side]
            mine = jnp.where(mask, context_grad, jnp.zeros_like(context_grad))
            grad_prob = matmul_nt(mine, value)
            value_g.append(matmul_tn(prob.astype(bf16), context_grad))
            delta = jnp.sum(prob * grad_prob, axis=-1, keepdims=True)
            grad_scores = (prob * (grad_prob - delta) * 0.125).astype(bf16)
            query_g.append(matmul(grad_scores, key))
            key_g.append(matmul_tn(grad_scores, query))
        query_g, key_g, value_g = (
            jnp.where(first, low, high) for low, high in (query_g, key_g, value_g)
        )
        query_sums.append(column_sum(query_g))
        value_sums.append(column_sum(value_g))
        proj_grad_ref[0, :, lanes] = query_g.astype(bf16)
        proj_grad_ref[1, :, lanes] = key_g.astype(bf16)
        proj_grad_ref[2, :, lanes] = value_g.astype(bf16)
    part = matmul_nt(proj_grad_ref[0], qkv_w[0])
    part = part + matmul_nt(proj_grad_ref[1], qkv_w[1])
    part = part + matmul_nt(proj_grad_ref[2], qkv_w[2])
    part_ref[...] = part
    sent_ref[...] = part.astype(bf16)
    cross_ref[:, :512] = context[...]
    cross_ref[:, 512:1024] = halves(core, resid_half)[1]
    cross_ref[:, 1024:1536] = halves(core, attn_rows[...])[1]
    for c in range(3):
        cross_ref[:, 1536 + c * LOCAL : 1536 + (c + 1) * LOCAL] = proj_grad_ref[c]
    sums_ref[...] = table_of(
        {
            QV: jnp.concatenate(query_sums + value_sums, axis=1),
            GAIN_M: column_sum(grad_mlp * normed),
            SHIFT_O: column_sum(grad_resid),
            SHIFT_M: column_sum(grad_mlp),
            SHIFT_D: column_sum(wide_out),
        }
    )


def stacked(own, far):
    return jnp.concatenate([own, far], axis=0)


def mlp_weight_grads(core, act, grad, mlp_rows, pre_half, crossed, out_ref):
    left = stacked(halves(core, act[...])[0], crossed[:, :512])
    right = stacked(grad[...], crossed[:, 512:1536])
    out_ref[:512, :] = matmul_tn(left, right).astype(bf16)
    left = stacked(halves(core, mlp_rows[...])[0], crossed[:, 1536:2048])
    right = stacked(pre_half[...], crossed[:, 2048:])
    out_ref[512:, :] = matmul_tn(left, right).astype(bf16)


def attention_weight_grads(core, context, resid_half, attn_rows, proj_grad, crossed, out_ref):
    left = stacked(halves(core, attn_rows[...])[0], crossed[:, 1024:1536])
    for c in range(3):
        far = crossed[:, 1536 + c * LOCAL : 1536 + (c + 1) * LOCAL]
        out_ref[c * 512 : (c + 1) * 512, :] = matmul_tn(left, stacked(proj_grad[c], far)).astype(bf16)
    left = stacked(context[...], crossed[:, :512])
    right = stacked(halves(core, resid_half[...])[0], crossed[:, 512:1024])
    out_ref[1536:, :] = matmul_tn(left, right).astype(bf16)


def device_kernel(body, name, scalars, shapes):
    smem = pl.BlockSpec(memory_space=pltpu.SMEM)
    vmem = pl.BlockSpec(memory_space=pltpu.VMEM)

    def call(*operands):
        return pl.pallas_call(
            body,
            name=name,
            in_specs=[smem] * scalars + [vmem] * (len(operands) - scalars),
            out_specs=[vmem] * len(shapes),
            out_shape=[jax.ShapeDtypeStruct(shape, dtype) for shape, dtype in shapes],
            compiler_params=pltpu.CompilerParams(vmem_limit_bytes=48 * 1024 * 1024),
        )(*operands)

    return call


ROWS = (LEN, WIDTH)
TABLE = ((8, WIDTH), f32)
ATTENTION_OUT = (
    (ROWS, bf16),
    ((3, LEN, LOCAL), bf16),
    ((HEADS_DEV, LEN, LEN), f32),
    ((LEN, LOCAL), bf16),
    (ROWS, f32),
    (ROWS, bf16),
)
MLP_BACK_OUT = ((ROWS, bf16), (ROWS, f32), (ROWS, bf16), ((LEN, 3072), bf16), TABLE)
FIRST_ATTENTION = device_kernel(first_attention, "first_attention", 2, ATTENTION_OUT)
NEXT_ATTENTION = device_kernel(
    next_attention, "next_attention", 2, ((ROWS, f32), (ROWS, bf16)) + ATTENTION_OUT
)
MLP_FORWARD = device_kernel(
    mlp_forward,
    "mlp_forward",
    0,
    ((ROWS, f32), (ROWS, bf16), (ROWS, f32), (ROWS, bf16), (ROWS, f32), (ROWS, bf16)),
)
LAST_OUTPUT = device_kernel(last_output, "last_output", 0, ((ROWS, f32),))
MLP_BACKWARD = device_kernel(mlp_backward, "mlp_backward", 1, MLP_BACK_OUT)
MLP_BACKWARD_BELOW = device_kernel(
    mlp_backward_below, "mlp_backward_below", 1, ((ROWS, bf16), TABLE) + MLP_BACK_OUT
)
ATTENTION_BACKWARD = device_kernel(
    attention_backward,
    "attention_backward",
    1,
    (
        (ROWS, f32),
        (ROWS, bf16),
        ((3, LEN, LOCAL), bf16),
        (ROWS, f32),
        (ROWS, bf16),
        ((LEN, 3072), bf16),
        TABLE,
    ),
)
LAST_INPUT_GRAD = device_kernel(last_input_grad, "last_input_grad", 0, ((ROWS, f32), TABLE))
MLP_WEIGHT_GRADS = device_kernel(mlp_weight_grads, "mlp_weight_grads", 1, (((1024, 1024), bf16),))
ATTENTION_WEIGHT_GRADS = device_kernel(
    attention_weight_grads, "attention_weight_grads", 1, (((2048, 512), bf16),)
)


def reduced(packed):
    ranks = lax.axis_size(DP)
    rows, columns = packed.shape
    pieces = packed.reshape(ranks, rows // ranks, columns)
    pieces = lax.all_to_all(pieces, DP, split_axis=0, concat_axis=0, tiled=True)
    total = jnp.sum(pieces.astype(f32), axis=0).astype(bf16)
    spread = jnp.broadcast_to(total[None], (ranks,) + total.shape)
    return lax.all_to_all(spread, DP, split_axis=0, concat_axis=0, tiled=True)


def local(
    section_in,
    lengths,
    qkv_weight,
    qv_bias,
    out_weight,
    up_weight,
    up_bias,
    down_weight,
    norm_gains,
    row_biases,
):
    core = lax.axis_index("pipe")
    tensor_index = lax.axis_index("tensor")
    place = core * 2 + tensor_index
    both = ("pipe", "tensor")

    own_rows = section_in[0, 0, 0]
    near = lax.ppermute(own_rows, both, ((0, 1), (1, 2)))
    far = lax.ppermute(own_rows, both, ((1, 3),))
    layer_in = jnp.where(place == 0, own_rows, jnp.where(place == 3, far, near))

    table = jnp.concatenate(
        [
            qv_bias[0].astype(f32).reshape(1, WIDTH),
            up_bias[0].astype(f32).reshape(1, WIDTH),
            norm_gains[0],
            row_biases[0],
        ]
    )
    owned = (qkv_weight[0], out_weight[0], up_weight[0], down_weight[0], table)
    other = tuple(lax.ppermute(array, "pipe", SWAP) for array in owned)
    layers = tuple(
        tuple(jnp.where(core == layer, mine, theirs) for mine, theirs in zip(owned, other))
        for layer in range(2)
    )
    cot_near = lax.ppermute(own_rows, both, ((2, 0), (3, 2)))
    cot_far = lax.ppermute(own_rows, both, ((2, 1),))
    cotangent = jnp.where(place == 3, own_rows, jnp.where(place == 1, cot_far, cot_near))

    seq_length = jnp.where(core == 0, lengths[0, 0], lengths[0, 1])
    core_length = jnp.stack([core, seq_length]).astype(jnp.int32)
    head_ids = tensor_index * HEADS_DEV + jnp.arange(HEADS_DEV) + 1
    slopes = 2.0 ** (-8.0 * head_ids.astype(f32) / HEADS)

    def swapped(sent):
        return lax.ppermute(sent, "tensor", SWAP)

    def crossed(sent):
        return lax.ppermute(sent, "pipe", SWAP)

    qkv_0, out_0, up_0, down_0, table_0 = layers[0]
    qkv_1, out_1, up_1, down_1, table_1 = layers[1]

    rows_0 = layer_in
    attn_0, proj_0, prob_0, context_0, part, sent = FIRST_ATTENTION(
        core_length, slopes, rows_0, table_0, qkv_0, out_0
    )
    resid_0, mlp_0, pre_0, act_0, part, sent = MLP_FORWARD(
        rows_0, part, swapped(sent), table_0, up_0, down_0
    )
    _, rows_1, attn_1, proj_1, prob_1, context_1, part, sent = NEXT_ATTENTION(
        core_length, slopes, resid_0, part, swapped(sent), table_0, table_1, qkv_1, out_1
    )
    resid_1, mlp_1, pre_1, act_1, top_part, top_sent = MLP_FORWARD(
        rows_1, part, swapped(sent), table_1, up_1, down_1
    )
    (out_one,) = LAST_OUTPUT(resid_1, top_part, swapped(top_sent), table_1)

    pre_half_1, part, sent, cross_mlp, sums_mlp_1 = MLP_BACKWARD(
        core_length, cotangent, pre_1, act_1, mlp_1, up_1, down_1
    )
    (early_1,) = MLP_WEIGHT_GRADS(
        core_length, act_1, cotangent, mlp_1, pre_half_1, crossed(cross_mlp)
    )
    grad_1, resid_half_1, proj_grad_1, part, sent, cross_attn, sums_attn_1 = ATTENTION_BACKWARD(
        core_length, cotangent, part, swapped(sent), resid_1, table_1, out_1, qkv_1,
        proj_1, prob_1, context_1, attn_1,
    )
    (late_1,) = ATTENTION_WEIGHT_GRADS(
        core_length, context_1, resid_half_1, attn_1, proj_grad_1, crossed(cross_attn)
    )
    grad_half, sums_in_1, pre_half_0, part, sent, cross_mlp, sums_mlp_0 = MLP_BACKWARD_BELOW(
        core_length, grad_1, part, swapped(sent), rows_1, table_1,
        pre_0, act_0, mlp_0, up_0, down_0,
    )
    (early_0,) = MLP_WEIGHT_GRADS(
        core_length, act_0, grad_half, mlp_0, pre_half_0, crossed(cross_mlp)
    )
    grad_0, resid_half_0, proj_grad_0, part, sent, cross_attn, sums_attn_0 = ATTENTION_BACKWARD(
        core_length, grad_half, part, swapped(sent), resid_0, table_0, out_0, qkv_0,
        proj_0, prob_0, context_0, attn_0,
    )
    (late_0,) = ATTENTION_WEIGHT_GRADS(
        core_length, context_0, resid_half_0, attn_0, proj_grad_0, crossed(cross_attn)
    )
    grad_zero, sums_in_0 = LAST_INPUT_GRAD(grad_0, part, swapped(sent), rows_0, table_0)

    def weights_of(layer, early, late):
        def both_halves(mine):
            theirs = lax.ppermute(mine, "pipe", ((1 - layer, layer),))
            return (mine, theirs) if layer == 0 else (theirs, mine)

        early = both_halves(reduced(early).reshape(2, 512, 1024))
        late = both_halves(reduced(late).reshape(4, 512, 512))
        return (
            jnp.concatenate([half[:3] for half in late], axis=1),
            jnp.concatenate([half[3] for half in late], axis=1),
            jnp.concatenate([half[1] for half in early], axis=0),
            jnp.concatenate([half[0] for half in early], axis=0),
        )

    weights_one = weights_of(1, early_1, late_1)
    weights_zero = weights_of(0, early_0, late_0)
    vectors_one = sums_in_1 + sums_mlp_1 + sums_attn_1
    vectors_zero = sums_in_0 + sums_mlp_0 + sums_attn_0

    first = core == 0
    vectors = jnp.where(first, vectors_zero, vectors_one) + crossed(
        jnp.where(first, vectors_one, vectors_zero)
    )
    for axis, pairs in ROUNDS:
        vectors = vectors + lax.ppermute(vectors, axis, pairs)
    shared = vectors[2:]
    shared = 0.5 * (shared + swapped(shared))

    crossing = lax.ppermute(jnp.where(first, out_one, grad_zero), both, ((0, 2), (3, 1)))
    kept_rows = jnp.where(first, grad_zero, out_one)
    section_out = jnp.where(core == tensor_index, kept_rows, crossing)
    qkv_g, out_g, up_g, down_g = (
        jnp.where(first, zero, one).astype(f32) for zero, one in zip(weights_zero, weights_one)
    )
    return (
        section_out[None, None, None],
        qkv_g[None],
        vectors[0].reshape(1, 2, 512),
        out_g[None],
        up_g[None],
        vectors[1][None],
        down_g[None],
        shared[:2][None],
        shared[2:][None],
    )


def solution(mesh):
    fine = Mesh(mesh.devices.reshape(2, 2, 4, 4, 2), ("pipe", "tensor", "y", "z", "xh"))
    dp = ("y", "z", "xh")
    in_specs = (
        P("pipe", dp, "tensor", None, None),
        P(dp, None),
        P("pipe", None, None, "tensor"),
        P("pipe", None, "tensor"),
        P("pipe", "tensor", None),
        P("pipe", None, "tensor"),
        P("pipe", "tensor"),
        P("pipe", "tensor", None),
        P("pipe", None, None),
        P("pipe", None, None),
    )
    out_specs = (
        P("pipe", dp, "tensor", None, None),
        P("pipe", None, None, "tensor"),
        P("pipe", None, "tensor"),
        P("pipe", "tensor", None),
        P("pipe", None, "tensor"),
        P("pipe", "tensor"),
        P("pipe", "tensor", None),
        P("pipe", None, None),
        P("pipe", None, None),
    )
    return jax.shard_map(local, mesh=fine, in_specs=in_specs, out_specs=out_specs, check_vma=False)
```

```python
import jax
import jax.numpy as jnp
from jax import lax
from jax.experimental import pallas as pl
from jax.experimental.pallas import tpu as pltpu
from jax.sharding import Mesh
from jax.sharding import PartitionSpec as P

HEADS = 16
HD = 64
LEN = 128
norm_eps = 1e-05

f32 = jnp.float32
bf16 = jnp.bfloat16

SWAP = ((0, 1), (1, 0))
DP = ("y", "z", "xh")


GELU_A = 0.7978845608028654
GELU_B = 0.044715
WIDTH = 1024
HEADS_DEV = HEADS // 2
LOCAL = HEADS_DEV * HD
PAIR = 2 * HD


def matmul(left, right):
    return jnp.dot(left, right, preferred_element_type=f32)


def matmul_nt(left, right):
    return lax.dot_general(left, right, (((1,), (1,)), ((), ())), preferred_element_type=f32)


def matmul_tn(left, right):
    return lax.dot_general(left, right, (((0,), (0,)), ((), ())), preferred_element_type=f32)


def norm_stats(values):
    centred = values - jnp.mean(values, axis=-1, keepdims=True)
    inv_std = lax.rsqrt(jnp.mean(centred * centred, axis=-1, keepdims=True) + norm_eps)
    return centred * inv_std, inv_std


def norm_back(grad_norm, normed, inv_std, gain):
    scaled = grad_norm * gain
    return inv_std * (
        scaled
        - jnp.mean(scaled, axis=-1, keepdims=True)
        - normed * jnp.mean(scaled * normed, axis=-1, keepdims=True)
    )


QV, UP_B, GAIN_A, GAIN_M, SHIFT_A, SHIFT_O, SHIFT_M, SHIFT_D = range(8)


def row(table, index):
    return table[index : index + 1, :]


def table_of(rows):
    zero = jnp.zeros((1, WIDTH), f32)
    return jnp.concatenate([rows.get(index, zero) for index in range(8)], axis=0)


def column_sum(block):
    return jnp.sum(block, axis=0, keepdims=True)


def head_lanes():
    return lax.broadcasted_iota(jnp.int32, (LEN, PAIR), 1) < HD


def attention_rows(rows, table, core, slopes, qkv_w, out_w, outs):
    attn_rows_ref, proj_ref, prob_ref, context_ref, part_ref, sent_ref = outs
    normed, _ = norm_stats(rows.astype(f32))
    attn_rows = (normed * row(table, GAIN_A) + row(table, SHIFT_A)).astype(bf16)
    attn_rows_ref[...] = attn_rows
    for c in range(3):
        block = matmul(attn_rows, qkv_w[c])
        if c == 0:
            block = block + table[QV : QV + 1, :LOCAL]
        if c == 2:
            block = block + table[QV : QV + 1, LOCAL:]
        proj_ref[c] = block.astype(bf16)
    spot_i = lax.broadcasted_iota(jnp.int32, (LEN, LEN), 0)
    spot_j = lax.broadcasted_iota(jnp.int32, (LEN, LEN), 1)
    allowed = (spot_j <= spot_i) & (spot_j < core[1])
    offsets = (spot_i - spot_j).astype(f32)
    first = head_lanes()
    for pair in range(HEADS_DEV // 2):
        lanes = slice(pair * PAIR, (pair + 1) * PAIR)
        query, key, value = (proj_ref[c, :, lanes] for c in range(3))
        found = []
        for side in range(2):
            head = 2 * pair + side
            mine = jnp.where(first if side == 0 else ~first, query, jnp.zeros_like(query))
            scores = matmul_nt(mine, key) * 0.125 - slopes[head] * offsets
            scores = jnp.where(allowed, scores, -jnp.inf)
            top_score = jnp.max(scores, axis=-1, keepdims=True)
            exp_scores = jnp.exp(scores - top_score)
            prob = exp_scores / jnp.sum(exp_scores, axis=-1, keepdims=True)
            prob_ref[head] = prob
            found.append(matmul(prob.astype(bf16), value))
        context_ref[:, lanes] = jnp.where(first, found[0], found[1]).astype(bf16)
    part = matmul(context_ref[...], out_w[...])
    part_ref[...] = part
    sent_ref[...] = part.astype(bf16)


def first_attention(core, slopes, rows, table, qkv_w, out_w, *outs):
    attention_rows(rows[...], table, core, slopes, qkv_w, out_w, outs)


def next_attention(
    core, slopes, resid, part, received, below, table, qkv_w, out_w, out_ref, rows_ref, *outs
):
    layer_out = resid[...] + (part[...] + received[...].astype(f32)) + row(below, SHIFT_D)
    out_ref[...] = layer_out
    rows = layer_out.astype(bf16)
    rows_ref[...] = rows
    attention_rows(rows, table, core, slopes, qkv_w, out_w, outs)


def mlp_forward(
    rows, part, received, table, up_w, down_w, resid_ref, mlp_ref, pre_ref, act_ref, out_ref, sent_ref
):
    resid = (
        rows[...].astype(f32) + (part[...] + received[...].astype(f32)) + row(table, SHIFT_O)
    )
    resid_ref[...] = resid
    normed, _ = norm_stats(resid)
    mlp_rows = (normed * row(table, GAIN_M) + row(table, SHIFT_M)).astype(bf16)
    mlp_ref[...] = mlp_rows
    pre = matmul(mlp_rows, up_w[...]) + row(table, UP_B)
    pre_ref[...] = pre
    act = (0.5 * pre * (1.0 + jnp.tanh(GELU_A * (pre + GELU_B * pre * pre * pre)))).astype(bf16)
    act_ref[...] = act
    out = matmul(act, down_w[...])
    out_ref[...] = out
    sent_ref[...] = out.astype(bf16)


def last_output(resid, part, received, table, out_ref):
    out_ref[...] = resid[...] + (part[...] + received[...].astype(f32)) + row(table, SHIFT_D)


def halves(core, block):
    half = block.shape[1] // 2
    low, high = block[:, :half], block[:, half:]
    own = core[0] == 0
    return jnp.where(own, low, high), jnp.where(own, high, low)


def mlp_back_body(core, grad, pre_in, act, mlp_rows, up_w, down_w, outs):
    pre_half_ref, part_ref, sent_ref, cross_ref, sums_ref = outs
    grad_act = matmul_nt(grad, down_w[...])
    pre = pre_in[...]
    tanh = jnp.tanh(GELU_A * (pre + GELU_B * pre * pre * pre))
    slope = 0.5 * (1.0 + tanh) + 0.5 * pre * (1.0 - tanh * tanh) * (
        GELU_A * (1.0 + 3.0 * GELU_B * pre * pre)
    )
    grad_pre = grad_act * slope
    pre_half = grad_pre.astype(bf16)
    pre_half_ref[...] = pre_half
    part = matmul_nt(pre_half, up_w[...])
    part_ref[...] = part
    sent_ref[...] = part.astype(bf16)
    cross_ref[:, :512] = halves(core, act[...])[1]
    cross_ref[:, 512:1536] = grad
    cross_ref[:, 1536:2048] = halves(core, mlp_rows[...])[1]
    cross_ref[:, 2048:] = pre_half
    return column_sum(grad_pre)


def mlp_backward(core, grad, pre, act, mlp_rows, up_w, down_w, *outs):
    total = mlp_back_body(core, grad[...], pre, act, mlp_rows, up_w, down_w, outs)
    outs[4][...] = table_of({UP_B: total})


def input_grad(grad_resid, part, received, rows, table):
    grad_attn = part[...] + received[...].astype(f32)
    normed, inv_std = norm_stats(rows[...].astype(f32))
    grad_in = grad_resid[...] + norm_back(grad_attn, normed, inv_std, row(table, GAIN_A))
    sums = {GAIN_A: column_sum(grad_attn * normed), SHIFT_A: column_sum(grad_attn)}
    return grad_in, sums


def mlp_backward_below(
    core, grad_resid, da_part, da_received, above_rows, above_table,
    pre, act, mlp_rows, up_w, down_w, grad_ref, above_ref, *outs,
):
    grad_in, sums = input_grad(grad_resid, da_part, da_received, above_rows, above_table)
    above_ref[...] = table_of(sums)
    grad = grad_in.astype(bf16)
    grad_ref[...] = grad
    total = mlp_back_body(core, grad, pre, act, mlp_rows, up_w, down_w, outs)
    outs[4][...] = table_of({UP_B: total})


def last_input_grad(grad_resid, part, received, rows, table, grad_ref, sums_ref):
    grad_in, sums = input_grad(grad_resid, part, received, rows, table)
    grad_ref[...] = grad_in
    sums_ref[...] = table_of(sums)


def attention_backward(
    core, grad_out, dc_part, dc_received, resid, table, out_w, qkv_w, proj, prob_in, context, attn_rows,
    grad_ref, resid_half_ref, proj_grad_ref, part_ref, sent_ref, cross_ref, sums_ref,
):
    grad_mlp = dc_part[...] + dc_received[...].astype(f32)
    normed, inv_std = norm_stats(resid[...])
    wide_out = grad_out[...].astype(f32)
    grad_resid = wide_out + norm_back(grad_mlp, normed, inv_std, row(table, GAIN_M))
    grad_ref[...] = grad_resid
    resid_half = grad_resid.astype(bf16)
    resid_half_ref[...] = resid_half
    grad_context = matmul_nt(resid_half, out_w[...]).astype(bf16)
    first = head_lanes()
    query_sums = []
    value_sums = []
    for pair in range(HEADS_DEV // 2):
        lanes = slice(pair * PAIR, (pair + 1) * PAIR)
        query, key, value = (proj[c, :, lanes] for c in range(3))
        context_grad = grad_context[:, lanes]
        query_g, key_g, value_g = [], [], []
        for side in range(2):
            mask = first if side == 0 else ~first
            prob = prob_in[2 * pair + side]
            mine = jnp.where(mask, context_grad, jnp.zeros_like(context_grad))
            grad_prob = matmul_nt(mine, value)
            value_g.append(matmul_tn(prob.astype(bf16), context_grad))
            delta = jnp.sum(prob * grad_prob, axis=-1, keepdims=True)
            grad_scores = (prob * (grad_prob - delta) * 0.125).astype(bf16)
            query_g.append(matmul(grad_scores, key))
            key_g.append(matmul_tn(grad_scores, query))
        query_g, key_g, value_g = (
            jnp.where(first, low, high) for low, high in (query_g, key_g, value_g)
        )
        query_sums.append(column_sum(query_g))
        value_sums.append(column_sum(value_g))
        proj_grad_ref[0, :, lanes] = query_g.astype(bf16)
        proj_grad_ref[1, :, lanes] = key_g.astype(bf16)
        proj_grad_ref[2, :, lanes] = value_g.astype(bf16)
    part = matmul_nt(proj_grad_ref[0], qkv_w[0])
    part = part + matmul_nt(proj_grad_ref[1], qkv_w[1])
    part = part + matmul_nt(proj_grad_ref[2], qkv_w[2])
    part_ref[...] = part
    sent_ref[...] = part.astype(bf16)
    cross_ref[:, :512] = context[...]
    cross_ref[:, 512:1024] = halves(core, resid_half)[1]
    cross_ref[:, 1024:1536] = halves(core, attn_rows[...])[1]
    for c in range(3):
        cross_ref[:, 1536 + c * LOCAL : 1536 + (c + 1) * LOCAL] = proj_grad_ref[c]
    sums_ref[...] = table_of(
        {
            QV: jnp.concatenate(query_sums + value_sums, axis=1),
            GAIN_M: column_sum(grad_mlp * normed),
            SHIFT_O: column_sum(grad_resid),
            SHIFT_M: column_sum(grad_mlp),
            SHIFT_D: column_sum(wide_out),
        }
    )


def stacked(own, far):
    return jnp.concatenate([own, far], axis=0)


def mlp_weight_grads(core, act, grad, mlp_rows, pre_half, crossed, out_ref):
    left = stacked(halves(core, act[...])[0], crossed[:, :512])
    right = stacked(grad[...], crossed[:, 512:1536])
    out_ref[:512, :] = matmul_tn(left, right).astype(bf16)
    left = stacked(halves(core, mlp_rows[...])[0], crossed[:, 1536:2048])
    right = stacked(pre_half[...], crossed[:, 2048:])
    out_ref[512:, :] = matmul_tn(left, right).astype(bf16)


def attention_weight_grads(core, context, resid_half, attn_rows, proj_grad, crossed, _, out_ref):
    left = stacked(halves(core, attn_rows[...])[0], crossed[:, 1024:1536])
    for c in range(3):
        far = crossed[:, 1536 + c * LOCAL : 1536 + (c + 1) * LOCAL]
        spot = (slice(512 * (c // 2), 512 * (c // 2 + 1)), slice(512 * (c % 2), 512 * (c % 2 + 1)))
        out_ref[spot] = matmul_tn(left, stacked(proj_grad[c], far)).astype(bf16)
    left = stacked(context[...], crossed[:, :512])
    right = stacked(halves(core, resid_half[...])[0], crossed[:, 512:1024])
    out_ref[512:, 512:] = matmul_tn(left, right).astype(bf16)


def pack_kernel(body, name, place):
    def whole(operand):
        zeros = (0,) * operand.ndim
        return pl.BlockSpec(operand.shape, lambda i: zeros)

    def call(core_length, *operands):
        specs = [whole(operand) for operand in operands]
        if place:
            specs[-1] = pl.BlockSpec(memory_space=pl.ANY)
        return pl.pallas_call(
            body,
            name=name,
            grid=(1,),
            in_specs=[pl.BlockSpec(memory_space=pltpu.SMEM)] + specs,
            out_specs=pl.BlockSpec((1024, WIDTH), lambda i: (place, 0)),
            out_shape=jax.ShapeDtypeStruct((2048, WIDTH), bf16),
            input_output_aliases={len(operands): 0} if place else {},
            compiler_params=pltpu.CompilerParams(vmem_limit_bytes=48 * 1024 * 1024),
        )(core_length, *operands)

    return call


RANKS = 32
CHUNK = 2048 // RANKS


def sum_spread(pieces, out_ref):
    total = pieces[0].astype(f32)
    for rank in range(1, RANKS):
        total = total + pieces[rank].astype(f32)
    out_ref[...] = jnp.broadcast_to(total.astype(bf16)[None], out_ref.shape)


def sum_and_spread(pieces):
    block = pl.BlockSpec((RANKS, 16, WIDTH), lambda i: (0, i, 0))
    return pl.pallas_call(
        sum_spread,
        name="sum_and_spread",
        grid=(CHUNK // 16,),
        in_specs=[block],
        out_specs=block,
        out_shape=jax.ShapeDtypeStruct(pieces.shape, bf16),
        compiler_params=pltpu.CompilerParams(vmem_limit_bytes=48 * 1024 * 1024),
    )(pieces)


def assemble_body(core, *refs):
    packs = [refs[4 * i : 4 * i + 4] for i in range(4)]
    qkv_ref, out_ref, up_ref, down_ref = refs[16:]
    low_core = core[0] == 0
    low_half = pl.program_id(0) == 0

    def piece(segment):
        mine_0, theirs_0, mine_1, theirs_1 = (pack[segment][...] for pack in packs)
        at_0 = jnp.where(low_half, mine_0, theirs_0)
        at_1 = jnp.where(low_half, theirs_1, mine_1)
        return jnp.where(low_core, at_0, at_1).reshape(2 * CHUNK, WIDTH).astype(f32)

    down_ref[...] = piece(0)
    up_ref[...] = piece(1)
    block = piece(2)
    qkv_ref[0] = block[:, :512]
    qkv_ref[1] = block[:, 512:]
    block = piece(3)
    qkv_ref[2] = block[:, :512]
    out_ref[...] = block[:, 512:]


def assemble(core_length, mine_0, theirs_0, mine_1, theirs_1):
    def spec(segment, layer, half):
        def index(h, q, core):
            live = (core[0] == layer) & (h == half)
            return (segment * 4 + jnp.where(live, q, 0), 0, 0)

        return pl.BlockSpec((2, CHUNK, WIDTH), index)

    operands = []
    specs = []
    for array, layer, half in ((mine_0, 0, 0), (theirs_0, 0, 1), (mine_1, 1, 1), (theirs_1, 1, 0)):
        for segment in range(4):
            operands.append(array)
            specs.append(spec(segment, layer, half))
    rows = pl.BlockSpec((2 * CHUNK, WIDTH), lambda h, q, core: (4 * h + q, 0))
    return pl.pallas_call(
        assemble_body,
        name="assemble",
        grid_spec=pltpu.PrefetchScalarGridSpec(
            num_scalar_prefetch=1,
            grid=(2, 4),
            in_specs=specs,
            out_specs=[
                pl.BlockSpec((3, 2 * CHUNK, 512), lambda h, q, core: (0, 4 * h + q, 0)),
                pl.BlockSpec((2 * CHUNK, 512), lambda h, q, core: (q, h)),
                rows,
                rows,
            ],
        ),
        out_shape=[
            jax.ShapeDtypeStruct((3, 1024, 512), f32),
            jax.ShapeDtypeStruct((512, 1024), f32),
            jax.ShapeDtypeStruct((1024, 1024), f32),
            jax.ShapeDtypeStruct((1024, 1024), f32),
        ],
        compiler_params=pltpu.CompilerParams(vmem_limit_bytes=48 * 1024 * 1024),
    )(core_length, *operands)


def device_kernel(body, name, scalars, shapes):
    smem = pl.BlockSpec(memory_space=pltpu.SMEM)
    vmem = pl.BlockSpec(memory_space=pltpu.VMEM)

    def call(*operands):
        return pl.pallas_call(
            body,
            name=name,
            in_specs=[smem] * scalars + [vmem] * (len(operands) - scalars),
            out_specs=[vmem] * len(shapes),
            out_shape=[jax.ShapeDtypeStruct(shape, dtype) for shape, dtype in shapes],
            compiler_params=pltpu.CompilerParams(vmem_limit_bytes=48 * 1024 * 1024),
        )(*operands)

    return call


ROWS = (LEN, WIDTH)
TABLE = ((8, WIDTH), f32)
ATTENTION_OUT = (
    (ROWS, bf16),
    ((3, LEN, LOCAL), bf16),
    ((HEADS_DEV, LEN, LEN), f32),
    ((LEN, LOCAL), bf16),
    (ROWS, f32),
    (ROWS, bf16),
)
MLP_BACK_OUT = ((ROWS, bf16), (ROWS, f32), (ROWS, bf16), ((LEN, 3072), bf16), TABLE)
FIRST_ATTENTION = device_kernel(first_attention, "first_attention", 2, ATTENTION_OUT)
NEXT_ATTENTION = device_kernel(
    next_attention, "next_attention", 2, ((ROWS, f32), (ROWS, bf16)) + ATTENTION_OUT
)
MLP_FORWARD = device_kernel(
    mlp_forward,
    "mlp_forward",
    0,
    ((ROWS, f32), (ROWS, bf16), (ROWS, f32), (ROWS, bf16), (ROWS, f32), (ROWS, bf16)),
)
LAST_OUTPUT = device_kernel(last_output, "last_output", 0, ((ROWS, f32),))
MLP_BACKWARD = device_kernel(mlp_backward, "mlp_backward", 1, MLP_BACK_OUT)
MLP_BACKWARD_BELOW = device_kernel(
    mlp_backward_below, "mlp_backward_below", 1, ((ROWS, bf16), TABLE) + MLP_BACK_OUT
)
ATTENTION_BACKWARD = device_kernel(
    attention_backward,
    "attention_backward",
    1,
    (
        (ROWS, f32),
        (ROWS, bf16),
        ((3, LEN, LOCAL), bf16),
        (ROWS, f32),
        (ROWS, bf16),
        ((LEN, 3072), bf16),
        TABLE,
    ),
)
LAST_INPUT_GRAD = device_kernel(last_input_grad, "last_input_grad", 0, ((ROWS, f32), TABLE))
MLP_WEIGHT_GRADS = pack_kernel(mlp_weight_grads, "mlp_weight_grads", 0)
ATTENTION_WEIGHT_GRADS = pack_kernel(attention_weight_grads, "attention_weight_grads", 1)


def exchange(pieces):
    return lax.all_to_all(pieces, DP, split_axis=0, concat_axis=0, tiled=True)


def local(
    section_in,
    lengths,
    qkv_weight,
    qv_bias,
    out_weight,
    up_weight,
    up_bias,
    down_weight,
    norm_gains,
    row_biases,
):
    core = lax.axis_index("pipe")
    tensor_index = lax.axis_index("tensor")
    place = core * 2 + tensor_index
    both = ("pipe", "tensor")

    own_rows = section_in[0, 0, 0]
    near = lax.ppermute(own_rows, both, ((0, 1), (1, 2)))
    far = lax.ppermute(own_rows, both, ((1, 3),))

    table = jnp.concatenate(
        [
            qv_bias[0].astype(f32).reshape(1, WIDTH),
            up_bias[0].astype(f32).reshape(1, WIDTH),
            norm_gains[0],
            row_biases[0],
        ]
    )
    owned = (qkv_weight[0], out_weight[0], up_weight[0], down_weight[0], table)
    first_far = [lax.ppermute(array, "pipe", SWAP) for array in (qkv_weight[0], out_weight[0], table)]
    up_own, down_own, near, far, *first_far = lax.optimization_barrier(
        (up_weight[0], down_weight[0], near, far, *first_far)
    )
    layer_in = jnp.where(place == 0, own_rows, jnp.where(place == 3, far, near))
    second_far = [lax.ppermute(array, "pipe", SWAP) for array in (up_own, down_own)]
    other = (first_far[0], first_far[1], second_far[0], second_far[1], first_far[2])
    layers = tuple(
        tuple(jnp.where(core == layer, mine, theirs) for mine, theirs in zip(owned, other))
        for layer in range(2)
    )
    seq_length = jnp.where(core == 0, lengths[0, 0], lengths[0, 1])
    core_length = jnp.stack([core, seq_length]).astype(jnp.int32)
    head_ids = tensor_index * HEADS_DEV + jnp.arange(HEADS_DEV) + 1
    slopes = 2.0 ** (-8.0 * head_ids.astype(f32) / HEADS)

    def swapped(sent):
        return lax.ppermute(sent, "tensor", SWAP)

    def crossed(sent):
        return lax.ppermute(sent, "pipe", SWAP)

    qkv_0, out_0, up_0, down_0, table_0 = layers[0]
    qkv_1, out_1, up_1, down_1, table_1 = layers[1]

    rows_0 = layer_in
    attn_0, proj_0, prob_0, context_0, part, sent = FIRST_ATTENTION(
        core_length, slopes, rows_0, table_0, qkv_0, out_0
    )
    received, cot_own = lax.optimization_barrier((swapped(sent), own_rows))
    cot_near = lax.ppermute(cot_own, both, ((2, 0), (3, 2)))
    cot_far = lax.ppermute(cot_own, both, ((2, 1),))
    cotangent = jnp.where(place == 3, own_rows, jnp.where(place == 1, cot_far, cot_near))
    resid_0, mlp_0, pre_0, act_0, part, sent = MLP_FORWARD(
        rows_0, part, received, table_0, up_0, down_0
    )
    _, rows_1, attn_1, proj_1, prob_1, context_1, part, sent = NEXT_ATTENTION(
        core_length, slopes, resid_0, part, swapped(sent), table_0, table_1, qkv_1, out_1
    )
    resid_1, mlp_1, pre_1, act_1, top_part, top_sent = MLP_FORWARD(
        rows_1, part, swapped(sent), table_1, up_1, down_1
    )
    (out_one,) = LAST_OUTPUT(resid_1, top_part, swapped(top_sent), table_1)

    pre_half_1, part, sent, cross_mlp, sums_mlp_1 = MLP_BACKWARD(
        core_length, cotangent, pre_1, act_1, mlp_1, up_1, down_1
    )
    pack_1 = MLP_WEIGHT_GRADS(
        core_length, act_1, cotangent, mlp_1, pre_half_1, crossed(cross_mlp)
    )
    received, pack_1, out_one = lax.optimization_barrier((swapped(sent), pack_1, out_one))
    grad_1, resid_half_1, proj_grad_1, part, sent, cross_attn, sums_attn_1 = ATTENTION_BACKWARD(
        core_length, cotangent, part, received, resid_1, table_1, out_1, qkv_1,
        proj_1, prob_1, context_1, attn_1,
    )
    pack_1 = ATTENTION_WEIGHT_GRADS(
        core_length, context_1, resid_half_1, attn_1, proj_grad_1, crossed(cross_attn), pack_1
    )
    received, pack_1 = lax.optimization_barrier((swapped(sent), pack_1))
    grad_half, sums_in_1, pre_half_0, part, sent, cross_mlp, sums_mlp_0 = MLP_BACKWARD_BELOW(
        core_length, grad_1, part, received, rows_1, table_1,
        pre_0, act_0, mlp_0, up_0, down_0,
    )
    pack_0 = MLP_WEIGHT_GRADS(
        core_length, act_0, grad_half, mlp_0, pre_half_0, crossed(cross_mlp)
    )
    received, pack_0 = lax.optimization_barrier((swapped(sent), pack_0))
    grad_0, resid_half_0, proj_grad_0, part, sent, cross_attn, sums_attn_0 = ATTENTION_BACKWARD(
        core_length, grad_half, part, received, resid_0, table_0, out_0, qkv_0,
        proj_0, prob_0, context_0, attn_0,
    )
    pack_0 = ATTENTION_WEIGHT_GRADS(
        core_length, context_0, resid_half_0, attn_0, proj_grad_0, crossed(cross_attn), pack_0
    )
    received = swapped(sent)
    received, pack_1, pack_0 = lax.optimization_barrier((received, pack_1, pack_0))
    grad_zero, sums_in_0 = LAST_INPUT_GRAD(grad_0, part, received, rows_0, table_0)

    vectors_one = sums_in_1 + sums_mlp_1 + sums_attn_1
    vectors_zero = sums_in_0 + sums_mlp_0 + sums_attn_0
    first = core == 0
    vectors = jnp.where(first, vectors_zero, vectors_one) + crossed(
        jnp.where(first, vectors_one, vectors_zero)
    )
    shared = vectors[GAIN_A:]
    shared = 0.5 * (shared + swapped(shared))
    vectors = jnp.concatenate([vectors[:GAIN_A], shared])

    pieces_1 = exchange(pack_1.reshape(RANKS, CHUNK, WIDTH))
    pieces_0 = exchange(pack_0.reshape(RANKS, CHUNK, WIDTH))
    crossing = lax.ppermute(jnp.where(first, out_one, grad_zero), both, ((0, 2), (3, 1)))
    total_1 = jnp.sum(pieces_1.astype(f32), axis=0).astype(bf16)
    total_1, crossing = lax.optimization_barrier((total_1, crossing))
    mine_1 = lax.all_gather(jnp.concatenate([total_1, vectors.astype(bf16)]), DP, axis=0)
    mine_0 = exchange(sum_and_spread(pieces_0))
    theirs_1 = lax.ppermute(mine_1, "pipe", ((0, 1),))
    theirs_0 = lax.ppermute(mine_0, "pipe", ((1, 0),))
    qkv_g, out_g, up_g, down_g = assemble(core_length, mine_0, theirs_0, mine_1, theirs_1)
    vectors = jnp.sum(mine_1[:, CHUNK:].astype(f32), axis=0)

    kept_rows = jnp.where(first, grad_zero, out_one)
    section_out = jnp.where(core == tensor_index, kept_rows, crossing)
    return (
        section_out[None, None, None],
        qkv_g[None],
        vectors[0].reshape(1, 2, 512),
        out_g[None],
        up_g[None],
        vectors[1][None],
        down_g[None],
        vectors[2:4][None],
        vectors[4:][None],
    )


def solution(mesh):
    fine = Mesh(mesh.devices.reshape(2, 2, 4, 4, 2), ("pipe", "tensor", "y", "z", "xh"))
    dp = ("y", "z", "xh")
    in_specs = (
        P("pipe", dp, "tensor", None, None),
        P(dp, None),
        P("pipe", None, None, "tensor"),
        P("pipe", None, "tensor"),
        P("pipe", "tensor", None),
        P("pipe", None, "tensor"),
        P("pipe", "tensor"),
        P("pipe", "tensor", None),
        P("pipe", None, None),
        P("pipe", None, None),
    )
    out_specs = (
        P("pipe", dp, "tensor", None, None),
        P("pipe", None, None, "tensor"),
        P("pipe", None, "tensor"),
        P("pipe", "tensor", None),
        P("pipe", None, "tensor"),
        P("pipe", "tensor"),
        P("pipe", "tensor", None),
        P("pipe", None, None),
        P("pipe", None, None),
    )
    return jax.shard_map(local, mesh=fine, in_specs=in_specs, out_specs=out_specs, check_vma=False)
```

```python
import functools

import jax
import jax.numpy as jnp
from jax import lax
from jax.experimental import pallas as pl
from jax.experimental.pallas import tpu as pltpu
from jax.sharding import Mesh
from jax.sharding import PartitionSpec as P

HEADS = 16
HD = 64
LEN = 128
norm_eps = 1e-05

f32 = jnp.float32
bf16 = jnp.bfloat16

SWAP = ((0, 1), (1, 0))
PAIR_E = ((0, 1), (1, 0), (2, 3), (3, 2))
PAIR_F = ((0, 3), (3, 0), (1, 2), (2, 1))
DP = ("y", "z", "xh")
ROUTES = (
    (("y", PAIR_E), ("y", PAIR_F), ("z", PAIR_E), ("z", PAIR_F), ("xh", SWAP)),
    (("y", PAIR_F), ("y", PAIR_E), ("z", PAIR_F), ("z", PAIR_E), ("xh", SWAP)),
    (("z", PAIR_E), ("z", PAIR_F), ("y", PAIR_E), ("y", PAIR_F), ("xh", SWAP)),
    (("z", PAIR_F), ("z", PAIR_E), ("y", PAIR_F), ("y", PAIR_E), ("xh", SWAP)),
)
CORE, LENGTH, TENSOR, BITS = 0, 1, 2, 4


GELU_A = 0.7978845608028654
GELU_B = 0.044715
WIDTH = 1024
HEADS_DEV = HEADS // 2
LOCAL = HEADS_DEV * HD
PAIR = 2 * HD


def matmul(left, right):
    return jnp.dot(left, right, preferred_element_type=f32)


def matmul_nt(left, right):
    return lax.dot_general(left, right, (((1,), (1,)), ((), ())), preferred_element_type=f32)


def matmul_tn(left, right):
    return lax.dot_general(left, right, (((0,), (0,)), ((), ())), preferred_element_type=f32)


def norm_stats(values):
    centred = values - jnp.mean(values, axis=-1, keepdims=True)
    inv_std = lax.rsqrt(jnp.mean(centred * centred, axis=-1, keepdims=True) + norm_eps)
    return centred * inv_std, inv_std


def norm_back(grad_norm, normed, inv_std, gain):
    scaled = grad_norm * gain
    return inv_std * (
        scaled
        - jnp.mean(scaled, axis=-1, keepdims=True)
        - normed * jnp.mean(scaled * normed, axis=-1, keepdims=True)
    )


QV, UP_B, GAIN_A, GAIN_M, SHIFT_A, SHIFT_O, SHIFT_M, SHIFT_D = range(8)


def row(table, index):
    return table[index : index + 1, :]


def table_of(rows):
    zero = jnp.zeros((1, WIDTH), f32)
    return jnp.concatenate([rows.get(index, zero) for index in range(8)], axis=0)


def column_sum(block):
    return jnp.sum(block, axis=0, keepdims=True)


def head_lanes():
    return lax.broadcasted_iota(jnp.int32, (LEN, PAIR), 1) < HD


def attention_rows(rows, table, info, slopes, weights, outs):
    attn_rows_ref, proj_ref, prob_ref, context_ref, part_ref, sent_ref = outs
    normed, _ = norm_stats(rows.astype(f32))
    attn_rows = (normed * row(table, GAIN_A) + row(table, SHIFT_A)).astype(bf16)
    attn_rows_ref[...] = attn_rows
    qkv_w = weights[0].ready()
    for c in range(3):
        block = matmul(attn_rows, qkv_w[c])
        if c == 0:
            block = block + table[QV : QV + 1, :LOCAL]
        if c == 2:
            block = block + table[QV : QV + 1, LOCAL:]
        proj_ref[c] = block.astype(bf16)
    spot_i = lax.broadcasted_iota(jnp.int32, (LEN, LEN), 0)
    spot_j = lax.broadcasted_iota(jnp.int32, (LEN, LEN), 1)
    allowed = (spot_j <= spot_i) & (spot_j < info[LENGTH])
    offsets = (spot_i - spot_j).astype(f32)
    first = head_lanes()
    for pair in range(HEADS_DEV // 2):
        lanes = slice(pair * PAIR, (pair + 1) * PAIR)
        query, key, value = (proj_ref[c, :, lanes] for c in range(3))
        found = []
        for side in range(2):
            head = 2 * pair + side
            mine = jnp.where(first if side == 0 else ~first, query, jnp.zeros_like(query))
            scores = matmul_nt(mine, key) * 0.125 - slopes[head] * offsets
            scores = jnp.where(allowed, scores, -jnp.inf)
            top_score = jnp.max(scores, axis=-1, keepdims=True)
            exp_scores = jnp.exp(scores - top_score)
            prob = exp_scores / jnp.sum(exp_scores, axis=-1, keepdims=True)
            prob_ref[head] = prob
            found.append(matmul(prob.astype(bf16), value))
        context_ref[:, lanes] = jnp.where(first, found[0], found[1]).astype(bf16)
    part = matmul(context_ref[...], weights[1].ready()[...])
    part_ref[...] = part
    sent_ref[...] = part.astype(bf16)


def table_for(info, tables, layer):
    own, far = tables
    return jnp.where(info[CORE] == layer, own[...], far[...])


def first_attention(ins, weights, outs):
    info, slopes, own_rows, near, far, *tables = ins
    rows_ref, *outs = outs
    place = 2 * info[CORE] + info[TENSOR]
    rows = jnp.where(place == 0, own_rows[...], jnp.where(place == 3, far[...], near[...]))
    rows_ref[...] = rows
    attention_rows(rows, table_for(info, tables, 0), info, slopes, weights, outs)


def next_attention(ins, weights, outs):
    info, slopes, resid, part, received, *tables = ins
    rows_ref, *outs = outs
    below = table_for(info, tables, 0)
    layer_out = resid[...] + (part[...] + received[...].astype(f32)) + row(below, SHIFT_D)
    rows = layer_out.astype(bf16)
    rows_ref[...] = rows
    attention_rows(rows, table_for(info, tables, 1), info, slopes, weights, outs)


def mlp_forward(layer, ins, weights, outs):
    info, rows, part, received, *tables = ins
    resid_ref, mlp_ref, pre_ref, act_ref, out_ref, sent_ref = outs
    table = table_for(info, tables, layer)
    resid = (
        rows[...].astype(f32) + (part[...] + received[...].astype(f32)) + row(table, SHIFT_O)
    )
    resid_ref[...] = resid
    normed, _ = norm_stats(resid)
    mlp_rows = (normed * row(table, GAIN_M) + row(table, SHIFT_M)).astype(bf16)
    mlp_ref[...] = mlp_rows
    pre = matmul(mlp_rows, weights[0].ready()[...]) + row(table, UP_B)
    pre_ref[...] = pre
    act = (0.5 * pre * (1.0 + jnp.tanh(GELU_A * (pre + GELU_B * pre * pre * pre)))).astype(bf16)
    act_ref[...] = act
    out = matmul(act, weights[1].ready()[...])
    out_ref[...] = out
    sent_ref[...] = out.astype(bf16)


def last_output(ins, weights, outs):
    info, resid, part, received, *tables = ins
    table = table_for(info, tables, 1)
    outs[0][...] = resid[...] + (part[...] + received[...].astype(f32)) + row(table, SHIFT_D)


def halves(core, block):
    half = block.shape[1] // 2
    low, high = block[:, :half], block[:, half:]
    own = core[CORE] == 0
    return jnp.where(own, low, high), jnp.where(own, high, low)


def mlp_back_body(info, grad, pre_in, act, mlp_rows, weights, outs):
    pre_half_ref, part_ref, sent_ref, cross_ref, sums_ref = outs
    grad_act = matmul_nt(grad, weights[0].ready()[...])
    pre = pre_in[...]
    tanh = jnp.tanh(GELU_A * (pre + GELU_B * pre * pre * pre))
    slope = 0.5 * (1.0 + tanh) + 0.5 * pre * (1.0 - tanh * tanh) * (
        GELU_A * (1.0 + 3.0 * GELU_B * pre * pre)
    )
    grad_pre = grad_act * slope
    pre_half = grad_pre.astype(bf16)
    pre_half_ref[...] = pre_half
    part = matmul_nt(pre_half, weights[1].ready()[...])
    part_ref[...] = part
    sent_ref[...] = part.astype(bf16)
    cross_ref[:, :512] = halves(info, act[...])[1]
    cross_ref[:, 512:1536] = grad
    cross_ref[:, 1536:2048] = halves(info, mlp_rows[...])[1]
    cross_ref[:, 2048:] = pre_half
    return column_sum(grad_pre)


def mlp_backward(ins, weights, outs):
    info, cot_own, cot_near, cot_far, pre, act, mlp_rows = ins
    grad_ref, *outs = outs
    place = 2 * info[CORE] + info[TENSOR]
    grad = jnp.where(place == 3, cot_own[...], jnp.where(place == 1, cot_far[...], cot_near[...]))
    grad_ref[...] = grad
    total = mlp_back_body(info, grad, pre, act, mlp_rows, weights, outs)
    outs[4][...] = table_of({UP_B: total})


def input_grad(grad_resid, part, received, rows, table):
    grad_attn = part[...] + received[...].astype(f32)
    normed, inv_std = norm_stats(rows[...].astype(f32))
    grad_in = grad_resid[...] + norm_back(grad_attn, normed, inv_std, row(table, GAIN_A))
    sums = {GAIN_A: column_sum(grad_attn * normed), SHIFT_A: column_sum(grad_attn)}
    return grad_in, sums


def mlp_backward_below(ins, weights, outs):
    info, grad_resid, da_part, da_received, above_rows, pre, act, mlp_rows, *tables = ins
    grad_ref, above_ref, *outs = outs
    above = table_for(info, tables, 1)
    grad_in, sums = input_grad(grad_resid, da_part, da_received, above_rows, above)
    above_ref[...] = table_of(sums)
    grad = grad_in.astype(bf16)
    grad_ref[...] = grad
    total = mlp_back_body(info, grad, pre, act, mlp_rows, weights, outs)
    outs[4][...] = table_of({UP_B: total})


def last_input_grad(ins, weights, outs):
    info, grad_resid, part, received, rows, *tables = ins
    grad_in, sums = input_grad(grad_resid, part, received, rows, table_for(info, tables, 0))
    outs[0][...] = grad_in
    outs[1][...] = table_of(sums)


def attention_backward(layer, ins, weights, outs):
    info, grad_out, dc_part, dc_received, resid, proj, prob_in, context, attn_rows, *tables = ins
    grad_ref, resid_half_ref, proj_grad_ref, part_ref, sent_ref, cross_ref, sums_ref = outs
    table = table_for(info, tables, layer)
    grad_mlp = dc_part[...] + dc_received[...].astype(f32)
    normed, inv_std = norm_stats(resid[...])
    wide_out = grad_out[...].astype(f32)
    grad_resid = wide_out + norm_back(grad_mlp, normed, inv_std, row(table, GAIN_M))
    grad_ref[...] = grad_resid
    resid_half = grad_resid.astype(bf16)
    resid_half_ref[...] = resid_half
    grad_context = matmul_nt(resid_half, weights[0].ready()[...]).astype(bf16)
    first = head_lanes()
    query_sums = []
    value_sums = []
    for pair in range(HEADS_DEV // 2):
        lanes = slice(pair * PAIR, (pair + 1) * PAIR)
        query, key, value = (proj[c, :, lanes] for c in range(3))
        context_grad = grad_context[:, lanes]
        query_g, key_g, value_g = [], [], []
        for side in range(2):
            mask = first if side == 0 else ~first
            prob = prob_in[2 * pair + side]
            mine = jnp.where(mask, context_grad, jnp.zeros_like(context_grad))
            grad_prob = matmul_nt(mine, value)
            value_g.append(matmul_tn(prob.astype(bf16), context_grad))
            delta = jnp.sum(prob * grad_prob, axis=-1, keepdims=True)
            grad_scores = (prob * (grad_prob - delta) * 0.125).astype(bf16)
            query_g.append(matmul(grad_scores, key))
            key_g.append(matmul_tn(grad_scores, query))
        query_g, key_g, value_g = (
            jnp.where(first, low, high) for low, high in (query_g, key_g, value_g)
        )
        query_sums.append(column_sum(query_g))
        value_sums.append(column_sum(value_g))
        proj_grad_ref[0, :, lanes] = query_g.astype(bf16)
        proj_grad_ref[1, :, lanes] = key_g.astype(bf16)
        proj_grad_ref[2, :, lanes] = value_g.astype(bf16)
    qkv_w = weights[1].ready()
    part = matmul_nt(proj_grad_ref[0], qkv_w[0])
    part = part + matmul_nt(proj_grad_ref[1], qkv_w[1])
    part = part + matmul_nt(proj_grad_ref[2], qkv_w[2])
    part_ref[...] = part
    sent_ref[...] = part.astype(bf16)
    cross_ref[:, :512] = context[...]
    cross_ref[:, 512:1024] = halves(info, resid_half)[1]
    cross_ref[:, 1024:1536] = halves(info, attn_rows[...])[1]
    for c in range(3):
        cross_ref[:, 1536 + c * LOCAL : 1536 + (c + 1) * LOCAL] = proj_grad_ref[c]
    sums_ref[...] = table_of(
        {
            QV: jnp.concatenate(query_sums + value_sums, axis=1),
            GAIN_M: column_sum(grad_mlp * normed),
            SHIFT_O: column_sum(grad_resid),
            SHIFT_M: column_sum(grad_mlp),
            SHIFT_D: column_sum(wide_out),
        }
    )


def stacked(own, far):
    return jnp.concatenate([own, far], axis=0)


def bit_of(info, segment, level):
    return info[BITS + 5 * segment + level]


def split(info, segment, level, block, keep_ref, send_ref):
    half = block.shape[-2] // 2
    low, high = block[..., :half, :], block[..., half:, :]
    own_low = bit_of(info, segment, level) == 0
    keep_ref[...] = jnp.where(own_low, low, high)
    send_ref[...] = jnp.where(own_low, high, low).astype(bf16)


def mlp_weight_grads(ins, weights, outs):
    info, act, grad, mlp_rows, pre_half, crossed = ins
    left = stacked(halves(info, act[...])[0], crossed[:, :512])
    right = stacked(grad[...], crossed[:, 512:1536])
    split(info, 0, 0, matmul_tn(left, right), outs[0], outs[2])
    left = stacked(halves(info, mlp_rows[...])[0], crossed[:, 1536:2048])
    right = stacked(pre_half[...], crossed[:, 2048:])
    split(info, 1, 0, matmul_tn(left, right), outs[1], outs[3])


def attention_weight_grads(ins, weights, outs):
    info, context, resid_half, attn_rows, proj_grad, crossed = ins
    left = stacked(halves(info, attn_rows[...])[0], crossed[:, 1024:1536])
    blocks = []
    for c in range(3):
        far = crossed[:, 1536 + c * LOCAL : 1536 + (c + 1) * LOCAL]
        blocks.append(matmul_tn(left, stacked(proj_grad[c], far)))
    left = stacked(context[...], crossed[:, :512])
    right = stacked(halves(info, resid_half[...])[0], crossed[:, 512:1024])
    blocks.append(matmul_tn(left, right))
    split(info, 2, 0, jnp.concatenate(blocks[:2], axis=1), outs[0], outs[2])
    split(info, 3, 0, jnp.concatenate(blocks[2:], axis=1), outs[1], outs[3])


def join_layers(ins, weights, outs):
    info = ins[0]
    kept = (ins[1:5], ins[5:9])
    received = (ins[9:13], ins[13:17])
    for segment in range(4):
        for layer in range(2):
            total = kept[layer][segment][...] + received[layer][segment][...].astype(f32)
            split(info, segment, 1, total, outs[segment].at[layer], outs[4 + segment].at[layer])


def reduce_level(level, ins, weights, outs):
    info, vector, vector_in = ins[:3]
    for segment in range(4):
        total = ins[3 + segment][...] + ins[7 + segment][...].astype(f32)
        split(info, segment, level, total, outs[1 + segment], outs[5 + segment])
    outs[0][...] = vector[...] + vector_in[...]


def reduce_last(ins, weights, outs):
    info, vector, vector_in = ins[:3]
    low_core = info[CORE] == 0
    for segment in range(4):
        total = (ins[3 + segment][...] + ins[7 + segment][...].astype(f32)).astype(bf16)
        outs[1][segment] = jnp.where(low_core, total[0], total[1])
        outs[2][segment] = jnp.where(low_core, total[1], total[0])
    outs[0][...] = vector[...] + vector_in[...]


def gather_start(ins, weights, outs):
    info, vector, vector_in, own, far = ins
    low_core = info[CORE] == 0
    outs[0][...] = vector[...] + vector_in[...]
    for segment in range(4):
        outs[1 + segment][0] = jnp.where(low_core, own[segment], far[segment])
        outs[1 + segment][1] = jnp.where(low_core, far[segment], own[segment])


def gather_level(level, ins, weights, outs):
    info = ins[0]
    for segment in range(4):
        own, far = ins[1 + segment][...], ins[5 + segment][...]
        half = own.shape[1]
        own_low = bit_of(info, segment, level) == 0
        outs[segment][:, :half] = jnp.where(own_low, own, far)
        outs[segment][:, half:] = jnp.where(own_low, far, own)


class Fetched:
    def __init__(self, info, layer, own, far, buffer, semaphore):
        self.copy = pltpu.make_async_copy(own, buffer, semaphore)
        self.buffer = buffer
        other = pltpu.make_async_copy(far, buffer, semaphore)
        pl.when(info[CORE] == layer)(self.copy.start)
        pl.when(info[CORE] != layer)(other.start)

    def ready(self):
        self.copy.wait()
        return self.buffer


def device_kernel(body, name, scalars, shapes, layer=0):
    def call(*operands, weights=()):
        def whole(shape):
            zeros = (0,) * len(shape)
            return pl.BlockSpec(shape, lambda i: zeros)

        count = len(operands)
        total = len(weights)

        def kernel(*refs):
            ins = refs[:count]
            pairs = refs[count : count + 2 * total]
            outs = refs[count + 2 * total : count + 2 * total + len(shapes)]
            rest = refs[count + 2 * total + len(shapes) :]
            fetched = [
                Fetched(ins[0], layer, pairs[2 * i], pairs[2 * i + 1], rest[i], rest[total + i])
                for i in range(total)
            ]
            body(ins, fetched, outs)

        smem = pl.BlockSpec(memory_space=pltpu.SMEM)
        hbm = pl.BlockSpec(memory_space=pl.ANY)
        flat = [array for pair in weights for array in pair]
        return pl.pallas_call(
            kernel,
            name=name,
            grid=(1,),
            in_specs=[smem] * scalars
            + [whole(operand.shape) for operand in operands[scalars:]]
            + [hbm] * len(flat),
            out_specs=[whole(shape) for shape, _ in shapes],
            out_shape=[jax.ShapeDtypeStruct(shape, dtype) for shape, dtype in shapes],
            scratch_shapes=[pltpu.VMEM(own.shape, own.dtype) for own, _ in weights]
            + [pltpu.SemaphoreType.DMA(())] * total,
            compiler_params=pltpu.CompilerParams(vmem_limit_bytes=56 * 1024 * 1024),
        )(*operands, *flat)

    return call


def assemble_body(info, *refs):
    qkv_ref, out_ref, up_ref, down_ref = refs[8:]
    low_rows = pl.program_id(1) < 2

    def piece(segment):
        own = (bit_of(info, segment, 0) == 0) == low_rows
        block = jnp.where(own, refs[segment][...], refs[4 + segment][...])
        return block.reshape(128, WIDTH).astype(f32)

    down_ref[...] = piece(0)
    up_ref[...] = piece(1)
    block = piece(2)
    qkv_ref[0] = block[:, :512]
    qkv_ref[1] = block[:, 512:]
    block = piece(3)
    qkv_ref[2] = block[:, :512]
    out_ref[...] = block[:, 512:]


def assemble(info, own, far):
    def spec(segment, bit):
        def index(h, q, info):
            live = (q // 2) == (bit_of(info, segment, 0) ^ bit)
            return (h, jnp.where(live, q % 2, bit_of(info, segment, 0) ^ bit ^ 1), 0)

        return pl.BlockSpec((1, 128, WIDTH), index)

    rows = pl.BlockSpec((128, WIDTH), lambda h, q, info: (4 * h + q, 0))
    return pl.pallas_call(
        assemble_body,
        name="assemble",
        grid_spec=pltpu.PrefetchScalarGridSpec(
            num_scalar_prefetch=1,
            grid=(2, 4),
            in_specs=[spec(segment, bit) for bit in range(2) for segment in range(4)],
            out_specs=[
                pl.BlockSpec((3, 128, 512), lambda h, q, info: (0, 4 * h + q, 0)),
                pl.BlockSpec((128, 512), lambda h, q, info: (q, h)),
                rows,
                rows,
            ],
        ),
        out_shape=[
            jax.ShapeDtypeStruct((3, 1024, 512), f32),
            jax.ShapeDtypeStruct((512, 1024), f32),
            jax.ShapeDtypeStruct((1024, 1024), f32),
            jax.ShapeDtypeStruct((1024, 1024), f32),
        ],
        compiler_params=pltpu.CompilerParams(vmem_limit_bytes=48 * 1024 * 1024),
    )(info, *own, *far)


ROWS = (LEN, WIDTH)
TABLE = ((8, WIDTH), f32)
ATTENTION_OUT = (
    (ROWS, bf16),
    (ROWS, bf16),
    ((3, LEN, LOCAL), bf16),
    ((HEADS_DEV, LEN, LEN), f32),
    ((LEN, LOCAL), bf16),
    (ROWS, f32),
    (ROWS, bf16),
)
MLP_OUT = ((ROWS, f32), (ROWS, bf16), (ROWS, f32), (ROWS, bf16), (ROWS, f32), (ROWS, bf16))
MLP_BACK_OUT = ((ROWS, bf16), (ROWS, f32), (ROWS, bf16), ((LEN, 3072), bf16), TABLE)
ATTENTION_BACK_OUT = (
    (ROWS, f32),
    (ROWS, bf16),
    ((3, LEN, LOCAL), bf16),
    (ROWS, f32),
    (ROWS, bf16),
    ((LEN, 3072), bf16),
    TABLE,
)
FIRST_ATTENTION = device_kernel(first_attention, "first_attention", 2, ATTENTION_OUT, 0)
NEXT_ATTENTION = device_kernel(next_attention, "next_attention", 2, ATTENTION_OUT, 1)
MLP_FORWARD = tuple(
    device_kernel(functools.partial(mlp_forward, layer), "mlp_forward", 1, MLP_OUT, layer)
    for layer in range(2)
)
LAST_OUTPUT = device_kernel(last_output, "last_output", 1, ((ROWS, f32),))
MLP_BACKWARD = device_kernel(
    mlp_backward, "mlp_backward", 1, ((ROWS, bf16),) + MLP_BACK_OUT, 1
)
MLP_BACKWARD_BELOW = device_kernel(
    mlp_backward_below, "mlp_backward_below", 1, ((ROWS, bf16), TABLE) + MLP_BACK_OUT, 0
)
ATTENTION_BACKWARD = tuple(
    device_kernel(
        functools.partial(attention_backward, layer),
        "attention_backward",
        1,
        ATTENTION_BACK_OUT,
        layer,
    )
    for layer in range(2)
)
LAST_INPUT_GRAD = device_kernel(last_input_grad, "last_input_grad", 1, ((ROWS, f32), TABLE))
FIRST_HALVES = (((256, WIDTH), f32),) * 2 + (((256, WIDTH), bf16),) * 2
MLP_WEIGHT_GRADS = device_kernel(mlp_weight_grads, "mlp_weight_grads", 1, FIRST_HALVES)
ATTENTION_WEIGHT_GRADS = device_kernel(
    attention_weight_grads, "attention_weight_grads", 1, FIRST_HALVES
)


def blocks(rows, dtype):
    return (((2, rows, WIDTH), dtype),) * 4


JOIN_LAYERS = device_kernel(join_layers, "join_layers", 1, blocks(128, f32) + blocks(128, bf16))
REDUCE_LEVEL = {
    level: device_kernel(
        functools.partial(reduce_level, level),
        "reduce_level",
        1,
        (TABLE,) + blocks(256 >> level, f32) + blocks(256 >> level, bf16),
    )
    for level in (2, 3, 4)
}
REDUCE_LAST = device_kernel(
    reduce_last, "reduce_last", 1, (TABLE,) + (((4, 16, WIDTH), bf16),) * 2
)
GATHER_START = device_kernel(gather_start, "gather_start", 1, (TABLE,) + blocks(16, bf16))
GATHER_LEVEL = {
    level: device_kernel(
        functools.partial(gather_level, level), "gather_level", 1, blocks(512 >> level, bf16)
    )
    for level in (4, 3, 2, 1)
}


def step_bit(axis, pairs):
    index = lax.axis_index(axis)
    if pairs is PAIR_E:
        return (index ^ (index >> 1)) & 1
    if pairs is PAIR_F:
        return (index >> 1) & 1
    return index


def local(
    section_in,
    lengths,
    qkv_weight,
    qv_bias,
    out_weight,
    up_weight,
    up_bias,
    down_weight,
    norm_gains,
    row_biases,
):
    core = lax.axis_index("pipe")
    tensor_index = lax.axis_index("tensor")
    place = core * 2 + tensor_index
    both = ("pipe", "tensor")

    own_rows = section_in[0, 0, 0]
    near = lax.ppermute(own_rows, both, ((0, 1), (1, 2)))
    far = lax.ppermute(own_rows, both, ((1, 3),))

    table = jnp.concatenate(
        [
            qv_bias[0].astype(f32).reshape(1, WIDTH),
            up_bias[0].astype(f32).reshape(1, WIDTH),
            norm_gains[0],
            row_biases[0],
        ]
    )
    first_far = [lax.ppermute(array, "pipe", SWAP) for array in (qkv_weight[0], out_weight[0], table)]
    up_own, down_own, near, far, *first_far = lax.optimization_barrier(
        (up_weight[0], down_weight[0], near, far, *first_far)
    )
    second_far = [lax.ppermute(array, "pipe", SWAP) for array in (up_own, down_own)]
    table_far = first_far[2]
    qkv_w = (qkv_weight[0], first_far[0])
    out_w = (out_weight[0], first_far[1])
    up_w = (up_weight[0], second_far[0])
    down_w = (down_weight[0], second_far[1])
    tables = (table, table_far)

    seq_length = jnp.where(core == 0, lengths[0, 0], lengths[0, 1])
    bits = [step_bit(axis, pairs) for route in ROUTES for axis, pairs in route]
    info = jnp.stack([core, seq_length, tensor_index, core] + bits).astype(jnp.int32)
    head_ids = tensor_index * HEADS_DEV + jnp.arange(HEADS_DEV) + 1
    slopes = 2.0 ** (-8.0 * head_ids.astype(f32) / HEADS)

    def swapped(sent):
        return lax.ppermute(sent, "tensor", SWAP)

    def crossed(sent):
        return lax.ppermute(sent, "pipe", SWAP)

    rows_0, attn_0, proj_0, prob_0, context_0, part, sent = FIRST_ATTENTION(
        info, slopes, own_rows, near, far, *tables, weights=(qkv_w, out_w)
    )
    received, cot_own = lax.optimization_barrier((swapped(sent), own_rows))
    cot_near = lax.ppermute(cot_own, both, ((2, 0), (3, 2)))
    cot_far = lax.ppermute(cot_own, both, ((2, 1),))
    resid_0, mlp_0, pre_0, act_0, part, sent = MLP_FORWARD[0](
        info, rows_0, part, received, *tables, weights=(up_w, down_w)
    )
    rows_1, attn_1, proj_1, prob_1, context_1, part, sent = NEXT_ATTENTION(
        info, slopes, resid_0, part, swapped(sent), *tables, weights=(qkv_w, out_w)
    )
    resid_1, mlp_1, pre_1, act_1, top_part, top_sent = MLP_FORWARD[1](
        info, rows_1, part, swapped(sent), *tables, weights=(up_w, down_w)
    )

    cotangent, pre_half_1, part, sent, cross_mlp, sums_mlp_1 = MLP_BACKWARD(
        info, own_rows, cot_near, cot_far, pre_1, act_1, mlp_1, weights=(down_w, up_w)
    )
    early_1 = MLP_WEIGHT_GRADS(info, act_1, cotangent, mlp_1, pre_half_1, crossed(cross_mlp))
    received, *early_1 = lax.optimization_barrier((swapped(sent), *early_1))
    top_sent, received = lax.optimization_barrier((top_sent, received))
    grad_1, resid_half_1, proj_grad_1, part, sent, cross_attn, sums_attn_1 = ATTENTION_BACKWARD[1](
        info, cotangent, part, received, resid_1, proj_1, prob_1, context_1, attn_1, *tables,
        weights=(out_w, qkv_w),
    )
    late_1 = ATTENTION_WEIGHT_GRADS(
        info, context_1, resid_half_1, attn_1, proj_grad_1, crossed(cross_attn)
    )
    received, *late_1 = lax.optimization_barrier((swapped(sent), *late_1))
    grad_half, sums_in_1, pre_half_0, part, sent, cross_mlp, sums_mlp_0 = MLP_BACKWARD_BELOW(
        info, grad_1, part, received, rows_1, pre_0, act_0, mlp_0, *tables,
        weights=(down_w, up_w),
    )
    early_0 = MLP_WEIGHT_GRADS(info, act_0, grad_half, mlp_0, pre_half_0, crossed(cross_mlp))
    received, *early_0 = lax.optimization_barrier((swapped(sent), *early_0))
    grad_0, resid_half_0, proj_grad_0, part, sent, cross_attn, sums_attn_0 = ATTENTION_BACKWARD[0](
        info, grad_half, part, received, resid_0, proj_0, prob_0, context_0, attn_0, *tables,
        weights=(out_w, qkv_w),
    )
    late_0 = ATTENTION_WEIGHT_GRADS(
        info, context_0, resid_half_0, attn_0, proj_grad_0, crossed(cross_attn)
    )
    received, *late_0 = lax.optimization_barrier((swapped(sent), *late_0))

    def half_steps(arrays, level):
        arrays = lax.optimization_barrier(tuple(arrays))
        return [
            lax.ppermute(array, *route[level]) for array, route in zip(arrays, ROUTES)
        ]

    kept_1 = (*early_1[:2], *late_1[:2])
    kept_0 = (*early_0[:2], *late_0[:2])
    received_1 = half_steps((*early_1[2:], *late_1[2:]), 0)
    received_0 = half_steps((*early_0[2:], *late_0[2:]), 0)

    grad_zero, sums_in_0 = LAST_INPUT_GRAD(info, grad_0, part, received, rows_0, *tables)
    vectors_one = sums_in_1 + sums_mlp_1 + sums_attn_1
    vectors_zero = sums_in_0 + sums_mlp_0 + sums_attn_0
    first = core == 0
    vectors = jnp.where(first, vectors_zero, vectors_one) + crossed(
        jnp.where(first, vectors_one, vectors_zero)
    )
    shared = vectors[GAIN_A:]
    shared = 0.5 * (shared + swapped(shared))
    vectors = jnp.concatenate([vectors[:GAIN_A], shared])

    stepped = JOIN_LAYERS(info, *kept_0, *kept_1, *received_0, *received_1)
    kept, sent = stepped[:4], stepped[4:]
    for level in (1, 2, 3, 4):
        *arrived, vector_in = lax.optimization_barrier(
            (*half_steps(sent, level), lax.ppermute(vectors, *ROUTES[0][level - 1]))
        )
        if level < 4:
            vectors, *stepped = REDUCE_LEVEL[level + 1](info, vectors, vector_in, *kept, *arrived)
            kept, sent = stepped[:4], stepped[4:]
    vectors, own, far = REDUCE_LAST(info, vectors, vector_in, *kept, *arrived)
    vectors, *held = GATHER_START(
        info, vectors, lax.ppermute(vectors, "xh", SWAP), own, crossed(far)
    )
    for level in (4, 3, 2, 1):
        arrived = lax.optimization_barrier(half_steps(held, level))
        held = GATHER_LEVEL[level](info, *held, *arrived)
    arrived = lax.optimization_barrier(half_steps(held, 0))
    qkv_g, out_g, up_g, down_g = assemble(info, held, arrived)

    (out_one,) = LAST_OUTPUT(info, resid_1, top_part, swapped(top_sent), *tables)
    crossing = lax.ppermute(jnp.where(first, out_one, grad_zero), both, ((0, 2), (3, 1)))
    kept_rows = jnp.where(first, grad_zero, out_one)
    section_out = jnp.where(core == tensor_index, kept_rows, crossing)
    return (
        section_out[None, None, None],
        qkv_g[None],
        vectors[0].reshape(1, 2, 512),
        out_g[None],
        up_g[None],
        vectors[1][None],
        down_g[None],
        vectors[2:4][None],
        vectors[4:][None],
    )


def solution(mesh):
    fine = Mesh(mesh.devices.reshape(2, 2, 4, 4, 2), ("pipe", "tensor", "y", "z", "xh"))
    dp = ("y", "z", "xh")
    in_specs = (
        P("pipe", dp, "tensor", None, None),
        P(dp, None),
        P("pipe", None, None, "tensor"),
        P("pipe", None, "tensor"),
        P("pipe", "tensor", None),
        P("pipe", None, "tensor"),
        P("pipe", "tensor"),
        P("pipe", "tensor", None),
        P("pipe", None, None),
        P("pipe", None, None),
    )
    out_specs = (
        P("pipe", dp, "tensor", None, None),
        P("pipe", None, None, "tensor"),
        P("pipe", None, "tensor"),
        P("pipe", "tensor", None),
        P("pipe", None, "tensor"),
        P("pipe", "tensor"),
        P("pipe", "tensor", None),
        P("pipe", None, None),
        P("pipe", None, None),
    )
    return jax.shard_map(local, mesh=fine, in_specs=in_specs, out_specs=out_specs, check_vma=False)
```

```python
import functools

import jax
import jax.numpy as jnp
from jax import lax
from jax.experimental import pallas as pl
from jax.experimental.pallas import tpu as pltpu
from jax.sharding import Mesh
from jax.sharding import PartitionSpec as P

HEADS = 16
HD = 64
LEN = 128
norm_eps = 1e-05

f32 = jnp.float32
bf16 = jnp.bfloat16

SWAP = ((0, 1), (1, 0))
PAIR_E = ((0, 1), (1, 0), (2, 3), (3, 2))
PAIR_F = ((0, 3), (3, 0), (1, 2), (2, 1))
DP = ("y", "z", "xh")
ROUTES = (
    (("y", PAIR_E), ("y", PAIR_F), ("z", PAIR_E), ("z", PAIR_F), ("xh", SWAP)),
    (("y", PAIR_F), ("y", PAIR_E), ("z", PAIR_F), ("z", PAIR_E), ("xh", SWAP)),
    (("z", PAIR_E), ("z", PAIR_F), ("y", PAIR_E), ("y", PAIR_F), ("xh", SWAP)),
    (("z", PAIR_F), ("z", PAIR_E), ("y", PAIR_F), ("y", PAIR_E), ("xh", SWAP)),
)
CORE, TENSOR, BITS = 0, 1, 2


GELU_A = 0.7978845608028654
GELU_B = 0.044715
WIDTH = 1024
HEADS_DEV = HEADS // 2
LOCAL = HEADS_DEV * HD
PAIR = 2 * HD


def matmul(left, right):
    return jnp.dot(left, right, preferred_element_type=f32)


def matmul_nt(left, right):
    return lax.dot_general(left, right, (((1,), (1,)), ((), ())), preferred_element_type=f32)


def matmul_tn(left, right):
    return lax.dot_general(left, right, (((0,), (0,)), ((), ())), preferred_element_type=f32)


def norm_stats(values):
    centred = values - jnp.mean(values, axis=-1, keepdims=True)
    inv_std = lax.rsqrt(jnp.mean(centred * centred, axis=-1, keepdims=True) + norm_eps)
    return centred * inv_std, inv_std


def norm_back(grad_norm, normed, inv_std, gain):
    scaled = grad_norm * gain
    return inv_std * (
        scaled
        - jnp.mean(scaled, axis=-1, keepdims=True)
        - normed * jnp.mean(scaled * normed, axis=-1, keepdims=True)
    )


QV, UP_B, GAIN_A, GAIN_M, SHIFT_A, SHIFT_O, SHIFT_M, SHIFT_D = range(8)


def row(table, index):
    return table[index : index + 1, :]


def table_of(rows):
    zero = jnp.zeros((1, WIDTH), f32)
    return jnp.concatenate([rows.get(index, zero) for index in range(8)], axis=0)


def column_sum(block):
    return jnp.sum(block, axis=0, keepdims=True)


def head_lanes():
    return lax.broadcasted_iota(jnp.int32, (LEN, PAIR), 1) < HD


def attention_rows(rows, table, info, lengths, weights, outs):
    attn_rows_ref, proj_ref, prob_ref, context_ref, part_ref, sent_ref = outs
    normed, _ = norm_stats(rows.astype(f32))
    attn_rows = (normed * row(table, GAIN_A) + row(table, SHIFT_A)).astype(bf16)
    attn_rows_ref[...] = attn_rows
    qkv_w = weights[0].ready()
    for c in range(3):
        block = matmul(attn_rows, qkv_w[c])
        if c == 0:
            block = block + table[QV : QV + 1, :LOCAL]
        if c == 2:
            block = block + table[QV : QV + 1, LOCAL:]
        proj_ref[c] = block.astype(bf16)
    spot_i = lax.broadcasted_iota(jnp.int32, (LEN, LEN), 0)
    spot_j = lax.broadcasted_iota(jnp.int32, (LEN, LEN), 1)
    allowed = (spot_j <= spot_i) & (spot_j < jnp.where(info[CORE] == 0, lengths[0, 0], lengths[0, 1]))
    offsets = (spot_i - spot_j).astype(f32)
    first = head_lanes()
    for pair in range(HEADS_DEV // 2):
        lanes = slice(pair * PAIR, (pair + 1) * PAIR)
        query, key, value = (proj_ref[c, :, lanes] for c in range(3))
        found = []
        for side in range(2):
            head = 2 * pair + side
            mine = jnp.where(first if side == 0 else ~first, query, jnp.zeros_like(query))
            slope = jnp.where(
                info[TENSOR] == 0,
                2.0 ** (-8.0 * (head + 1) / HEADS),
                2.0 ** (-8.0 * (head + HEADS_DEV + 1) / HEADS),
            )
            scores = matmul_nt(mine, key) * 0.125 - slope * offsets
            scores = jnp.where(allowed, scores, -jnp.inf)
            top_score = jnp.max(scores, axis=-1, keepdims=True)
            exp_scores = jnp.exp(scores - top_score)
            prob = exp_scores / jnp.sum(exp_scores, axis=-1, keepdims=True)
            prob_ref[head] = prob
            found.append(matmul(prob.astype(bf16), value))
        context_ref[:, lanes] = jnp.where(first, found[0], found[1]).astype(bf16)
    part = matmul(context_ref[...], weights[1].ready()[...])
    part_ref[...] = part
    sent_ref[...] = part.astype(bf16)


def make_table(ins, weights, outs):
    qv_b, up_b, gains, shifts = ins
    outs[0][QV : QV + 1, :LOCAL] = qv_b[0:1, :].astype(f32)
    outs[0][QV : QV + 1, LOCAL:] = qv_b[1:2, :].astype(f32)
    outs[0][UP_B : UP_B + 1, :] = up_b[...].astype(f32)
    outs[0][GAIN_A : SHIFT_A, :] = gains[...]
    outs[0][SHIFT_A:, :] = shifts[...]


def table_for(info, tables, layer):
    own, far = tables
    return jnp.where(info[CORE] == layer, own[...], far[...])


def first_attention(ins, weights, outs):
    info, lengths, own_rows, near, far, *tables = ins
    rows_ref, *outs = outs
    place = 2 * info[CORE] + info[TENSOR]
    rows = jnp.where(place == 0, own_rows[...], jnp.where(place == 3, far[...], near[...]))
    rows_ref[...] = rows
    attention_rows(rows, table_for(info, tables, 0), info, lengths, weights, outs)


def next_attention(ins, weights, outs):
    info, lengths, resid, part, received, *tables = ins
    rows_ref, *outs = outs
    below = table_for(info, tables, 0)
    layer_out = resid[...] + (part[...] + received[...].astype(f32)) + row(below, SHIFT_D)
    rows = layer_out.astype(bf16)
    rows_ref[...] = rows
    attention_rows(rows, table_for(info, tables, 1), info, lengths, weights, outs)


def mlp_forward(layer, ins, weights, outs):
    info, rows, part, received, *tables = ins
    resid_ref, mlp_ref, pre_ref, act_ref, out_ref, sent_ref = outs
    table = table_for(info, tables, layer)
    resid = (
        rows[...].astype(f32) + (part[...] + received[...].astype(f32)) + row(table, SHIFT_O)
    )
    resid_ref[...] = resid
    normed, _ = norm_stats(resid)
    mlp_rows = (normed * row(table, GAIN_M) + row(table, SHIFT_M)).astype(bf16)
    mlp_ref[...] = mlp_rows
    pre = matmul(mlp_rows, weights[0].ready()[...]) + row(table, UP_B)
    pre_ref[...] = pre
    act = (0.5 * pre * (1.0 + jnp.tanh(GELU_A * (pre + GELU_B * pre * pre * pre)))).astype(bf16)
    act_ref[...] = act
    out = matmul(act, weights[1].ready()[...])
    out_ref[...] = out
    sent_ref[...] = out.astype(bf16)


def halves(core, block):
    half = block.shape[1] // 2
    low, high = block[:, :half], block[:, half:]
    own = core[CORE] == 0
    return jnp.where(own, low, high), jnp.where(own, high, low)


def mlp_back_body(info, grad, pre_in, act, mlp_rows, weights, outs):
    pre_half_ref, part_ref, sent_ref, cross_ref, sums_ref = outs
    grad_act = matmul_nt(grad, weights[0].ready()[...])
    pre = pre_in[...]
    tanh = jnp.tanh(GELU_A * (pre + GELU_B * pre * pre * pre))
    slope = 0.5 * (1.0 + tanh) + 0.5 * pre * (1.0 - tanh * tanh) * (
        GELU_A * (1.0 + 3.0 * GELU_B * pre * pre)
    )
    grad_pre = grad_act * slope
    pre_half = grad_pre.astype(bf16)
    pre_half_ref[...] = pre_half
    part = matmul_nt(pre_half, weights[1].ready()[...])
    part_ref[...] = part
    sent_ref[...] = part.astype(bf16)
    cross_ref[:, :512] = halves(info, act[...])[1]
    cross_ref[:, 512:1536] = grad
    cross_ref[:, 1536:2048] = halves(info, mlp_rows[...])[1]
    cross_ref[:, 2048:] = pre_half
    return column_sum(grad_pre)


def mlp_backward(ins, weights, outs):
    info, cot_own, cot_near, cot_far, pre, act, mlp_rows = ins
    grad_ref, *outs = outs
    place = 2 * info[CORE] + info[TENSOR]
    grad = jnp.where(place == 3, cot_own[...], jnp.where(place == 1, cot_far[...], cot_near[...]))
    grad_ref[...] = grad
    total = mlp_back_body(info, grad, pre, act, mlp_rows, weights, outs)
    outs[4][...] = table_of({UP_B: total})


def input_grad(grad_resid, part, received, rows, table):
    grad_attn = part[...] + received[...].astype(f32)
    normed, inv_std = norm_stats(rows[...].astype(f32))
    grad_in = grad_resid[...] + norm_back(grad_attn, normed, inv_std, row(table, GAIN_A))
    sums = {GAIN_A: column_sum(grad_attn * normed), SHIFT_A: column_sum(grad_attn)}
    return grad_in, sums


def mlp_backward_below(ins, weights, outs):
    info, grad_resid, da_part, da_received, above_rows, pre, act, mlp_rows, *tables = ins
    grad_ref, above_ref, *outs = outs
    above = table_for(info, tables, 1)
    grad_in, sums = input_grad(grad_resid, da_part, da_received, above_rows, above)
    above_ref[...] = table_of(sums)
    grad = grad_in.astype(bf16)
    grad_ref[...] = grad
    total = mlp_back_body(info, grad, pre, act, mlp_rows, weights, outs)
    outs[4][...] = table_of({UP_B: total})


def last_input_grad(ins, weights, outs):
    info, grad_resid, part, received, rows, out_one, *tables = ins
    grad_in, sums = input_grad(grad_resid, part, received, rows, table_for(info, tables[:2], 0))
    low_core = info[CORE] == 0
    top = out_one[...]
    outs[0][...] = jnp.where(low_core, grad_in, top)
    outs[1][...] = jnp.where(low_core, top, grad_in)
    outs[2][0] = table_of(sums) + tables[2][...] + tables[3][...]
    outs[2][1] = tables[4][...] + tables[5][...] + tables[6][...]


def attention_backward(layer, ins, weights, outs):
    info, grad_out, dc_part, dc_received, resid, proj, prob_in, context, attn_rows, *tables = ins
    if layer == 1:
        *outs, out_ref = outs
        top_part, top_received, *tables = tables
        top = table_for(info, tables, 1)
        out_ref[...] = (
            resid[...] + (top_part[...] + top_received[...].astype(f32)) + row(top, SHIFT_D)
        )
    grad_ref, resid_half_ref, proj_grad_ref, part_ref, sent_ref, cross_ref, sums_ref = outs
    table = table_for(info, tables, layer)
    grad_mlp = dc_part[...] + dc_received[...].astype(f32)
    normed, inv_std = norm_stats(resid[...])
    wide_out = grad_out[...].astype(f32)
    grad_resid = wide_out + norm_back(grad_mlp, normed, inv_std, row(table, GAIN_M))
    grad_ref[...] = grad_resid
    resid_half = grad_resid.astype(bf16)
    resid_half_ref[...] = resid_half
    grad_context = matmul_nt(resid_half, weights[0].ready()[...]).astype(bf16)
    first = head_lanes()
    query_sums = []
    value_sums = []
    for pair in range(HEADS_DEV // 2):
        lanes = slice(pair * PAIR, (pair + 1) * PAIR)
        query, key, value = (proj[c, :, lanes] for c in range(3))
        context_grad = grad_context[:, lanes]
        query_g, key_g, value_g = [], [], []
        for side in range(2):
            mask = first if side == 0 else ~first
            prob = prob_in[2 * pair + side]
            mine = jnp.where(mask, context_grad, jnp.zeros_like(context_grad))
            grad_prob = matmul_nt(mine, value)
            value_g.append(matmul_tn(prob.astype(bf16), context_grad))
            delta = jnp.sum(prob * grad_prob, axis=-1, keepdims=True)
            grad_scores = (prob * (grad_prob - delta) * 0.125).astype(bf16)
            query_g.append(matmul(grad_scores, key))
            key_g.append(matmul_tn(grad_scores, query))
        query_g, key_g, value_g = (
            jnp.where(first, low, high) for low, high in (query_g, key_g, value_g)
        )
        query_sums.append(column_sum(query_g))
        value_sums.append(column_sum(value_g))
        proj_grad_ref[0, :, lanes] = query_g.astype(bf16)
        proj_grad_ref[1, :, lanes] = key_g.astype(bf16)
        proj_grad_ref[2, :, lanes] = value_g.astype(bf16)
    qkv_w = weights[1].ready()
    part = matmul_nt(proj_grad_ref[0], qkv_w[0])
    part = part + matmul_nt(proj_grad_ref[1], qkv_w[1])
    part = part + matmul_nt(proj_grad_ref[2], qkv_w[2])
    part_ref[...] = part
    sent_ref[...] = part.astype(bf16)
    cross_ref[:, :512] = context[...]
    cross_ref[:, 512:1024] = halves(info, resid_half)[1]
    cross_ref[:, 1024:1536] = halves(info, attn_rows[...])[1]
    for c in range(3):
        cross_ref[:, 1536 + c * LOCAL : 1536 + (c + 1) * LOCAL] = proj_grad_ref[c]
    sums_ref[...] = table_of(
        {
            QV: jnp.concatenate(query_sums + value_sums, axis=1),
            GAIN_M: column_sum(grad_mlp * normed),
            SHIFT_O: column_sum(grad_resid),
            SHIFT_M: column_sum(grad_mlp),
            SHIFT_D: column_sum(wide_out),
        }
    )


def stacked(own, far):
    return jnp.concatenate([own, far], axis=0)


def bit_of(info, segment, level):
    return info[BITS + 5 * segment + level]


def split(info, segment, level, block, keep_ref, send_ref):
    half = block.shape[-2] // 2
    low, high = block[..., :half, :], block[..., half:, :]
    own_low = bit_of(info, segment, level) == 0
    keep_ref[...] = jnp.where(own_low, low, high)
    send_ref[...] = jnp.where(own_low, high, low).astype(bf16)


def mlp_weight_grads(ins, weights, outs):
    info, act, grad, mlp_rows, pre_half, crossed = ins
    left = stacked(halves(info, act[...])[0], crossed[:, :512])
    right = stacked(grad[...], crossed[:, 512:1536])
    split(info, 0, 0, matmul_tn(left, right), outs[0], outs[2])
    left = stacked(halves(info, mlp_rows[...])[0], crossed[:, 1536:2048])
    right = stacked(pre_half[...], crossed[:, 2048:])
    split(info, 1, 0, matmul_tn(left, right), outs[1], outs[3])


def attention_weight_grads(ins, weights, outs):
    info, context, resid_half, attn_rows, proj_grad, crossed = ins
    left = stacked(halves(info, attn_rows[...])[0], crossed[:, 1024:1536])
    blocks = []
    for c in range(3):
        far = crossed[:, 1536 + c * LOCAL : 1536 + (c + 1) * LOCAL]
        blocks.append(matmul_tn(left, stacked(proj_grad[c], far)))
    left = stacked(context[...], crossed[:, :512])
    right = stacked(halves(info, resid_half[...])[0], crossed[:, 512:1024])
    blocks.append(matmul_tn(left, right))
    split(info, 2, 0, jnp.concatenate(blocks[:2], axis=1), outs[0], outs[2])
    split(info, 3, 0, jnp.concatenate(blocks[2:], axis=1), outs[1], outs[3])


def two_parts(vector):
    high = vector.astype(bf16)
    low = (vector - high.astype(f32)).astype(bf16)
    return high, low, high.astype(f32) + low.astype(f32)


def join_layers(ins, weights, outs):
    info = ins[0]
    kept = (ins[1:5], ins[5:9])
    received = (ins[9:13], ins[13:17])
    vector, vector_in = ins[17:]
    for segment in range(4):
        for layer in range(2):
            total = kept[layer][segment][...] + received[layer][segment][...].astype(f32)
            sent = outs[5 + segment].at[layer, :128]
            split(info, segment, 1, total, outs[1 + segment].at[layer], sent)
    high, low, outs[0][...] = two_parts(vector[...] + vector_in[...])
    outs[5][:, 128:136] = high
    outs[5][:, 136:] = low


def reduce_level(level, ins, weights, outs):
    info, vector = ins[:2]
    rows = ins[2].shape[1]
    half = rows // 2
    total = vector[...] + (ins[6][:, rows : rows + 8].astype(f32) + ins[6][:, rows + 8 :].astype(f32))
    high, low, outs[0][...] = two_parts(total)
    for segment in range(4):
        total = ins[2 + segment][...] + ins[6 + segment][:, :rows].astype(f32)
        if level < 4:
            split(info, segment, level, total, outs[1 + segment], outs[5 + segment].at[:, :half])
        else:
            place = slice(2 * segment, 2 * segment + 2)
            split(info, segment, level, total, outs[1].at[place], outs[2].at[place])
    if level < 4:
        outs[5][:, half : half + 8] = high
        outs[5][:, half + 8 :] = low
    else:
        outs[2][8:, :8] = high
        outs[2][8:, 8:] = low


def reduce_last(ins, weights, outs):
    info, vector, kept, received = ins
    low_core = info[CORE] == 0
    for segment in range(4):
        place = slice(2 * segment, 2 * segment + 2)
        total = (kept[place] + received[place].astype(f32)).astype(bf16)
        outs[1][segment] = jnp.where(low_core, total[0], total[1])
        outs[2][segment] = jnp.where(low_core, total[1], total[0])
    total = vector[...] + (received[8:, :8].astype(f32) + received[8:, 8:].astype(f32))
    outs[0][...] = jnp.where(low_core, total[0], total[1])
    high, low, _ = two_parts(jnp.where(low_core, total[1], total[0]))
    outs[2][4, :8] = high
    outs[2][4, 8:] = low


def gather_start(ins, weights, outs):
    info, vector, own, far = ins
    low_core = info[CORE] == 0
    outs[0][...] = vector[...] + (far[4, :8].astype(f32) + far[4, 8:].astype(f32))
    for segment in range(4):
        outs[1][2 * segment] = jnp.where(low_core, own[segment], far[segment])
        outs[1][2 * segment + 1] = jnp.where(low_core, far[segment], own[segment])


def gather_first(ins, weights, outs):
    info, mine, theirs = ins
    for segment in range(4):
        place = slice(2 * segment, 2 * segment + 2)
        own, far = mine[place], theirs[place]
        own_low = bit_of(info, segment, 4) == 0
        outs[segment][:, :16] = jnp.where(own_low, own, far)
        outs[segment][:, 16:] = jnp.where(own_low, far, own)


def gather_level(level, ins, weights, outs):
    info = ins[0]
    for segment in range(4):
        own, far = ins[1 + segment][...], ins[5 + segment][...]
        half = own.shape[1]
        own_low = bit_of(info, segment, level) == 0
        outs[segment][:, :half] = jnp.where(own_low, own, far)
        outs[segment][:, half:] = jnp.where(own_low, far, own)


class Fetched:
    def __init__(self, info, layer, own, far, buffer, semaphore):
        self.copy = pltpu.make_async_copy(own, buffer, semaphore)
        self.buffer = buffer
        other = pltpu.make_async_copy(far, buffer, semaphore)
        pl.when(info[CORE] == layer)(self.copy.start)
        pl.when(info[CORE] != layer)(other.start)

    def ready(self):
        self.copy.wait()
        return self.buffer


def device_kernel(body, name, scalars, shapes, layer=0):
    def call(*operands, weights=()):
        def whole(shape):
            zeros = (0,) * len(shape)
            return pl.BlockSpec(shape, lambda i: zeros)

        count = len(operands)
        total = len(weights)

        def kernel(*refs):
            ins = refs[:count]
            pairs = refs[count : count + 2 * total]
            outs = refs[count + 2 * total : count + 2 * total + len(shapes)]
            rest = refs[count + 2 * total + len(shapes) :]
            fetched = [
                Fetched(ins[0], layer, pairs[2 * i], pairs[2 * i + 1], rest[i], rest[total + i])
                for i in range(total)
            ]
            body(ins, fetched, outs)

        smem = pl.BlockSpec(memory_space=pltpu.SMEM)
        hbm = pl.BlockSpec(memory_space=pl.ANY)
        flat = [array for pair in weights for array in pair]
        return pl.pallas_call(
            kernel,
            name=name,
            grid=(1,),
            in_specs=[smem] * scalars
            + [whole(operand.shape) for operand in operands[scalars:]]
            + [hbm] * len(flat),
            out_specs=[whole(shape) for shape, _ in shapes],
            out_shape=[jax.ShapeDtypeStruct(shape, dtype) for shape, dtype in shapes],
            scratch_shapes=[pltpu.VMEM(own.shape, own.dtype) for own, _ in weights]
            + [pltpu.SemaphoreType.DMA(())] * total,
            compiler_params=pltpu.CompilerParams(vmem_limit_bytes=56 * 1024 * 1024),
        )(*operands, *flat)

    return call


def assemble_body(info, *refs):
    qkv_ref, out_ref, up_ref, down_ref = refs[8:]
    low_rows = pl.program_id(1) < 2

    def piece(segment):
        own = (bit_of(info, segment, 0) == 0) == low_rows
        block = jnp.where(own, refs[segment][...], refs[4 + segment][...])
        return block.reshape(128, WIDTH).astype(f32)

    down_ref[...] = piece(0)
    up_ref[...] = piece(1)
    block = piece(2)
    qkv_ref[0] = block[:, :512]
    qkv_ref[1] = block[:, 512:]
    block = piece(3)
    qkv_ref[2] = block[:, :512]
    out_ref[...] = block[:, 512:]


def assemble(info, own, far):
    def spec(segment, bit):
        def index(h, q, info):
            live = (q // 2) == (bit_of(info, segment, 0) ^ bit)
            return (h, jnp.where(live, q % 2, bit_of(info, segment, 0) ^ bit ^ 1), 0)

        return pl.BlockSpec((1, 128, WIDTH), index)

    rows = pl.BlockSpec((128, WIDTH), lambda h, q, info: (4 * h + q, 0))
    return pl.pallas_call(
        assemble_body,
        name="assemble",
        grid_spec=pltpu.PrefetchScalarGridSpec(
            num_scalar_prefetch=1,
            grid=(2, 4),
            in_specs=[spec(segment, bit) for bit in range(2) for segment in range(4)],
            out_specs=[
                pl.BlockSpec((3, 128, 512), lambda h, q, info: (0, 4 * h + q, 0)),
                pl.BlockSpec((128, 512), lambda h, q, info: (q, h)),
                rows,
                rows,
            ],
        ),
        out_shape=[
            jax.ShapeDtypeStruct((3, 1024, 512), f32),
            jax.ShapeDtypeStruct((512, 1024), f32),
            jax.ShapeDtypeStruct((1024, 1024), f32),
            jax.ShapeDtypeStruct((1024, 1024), f32),
        ],
        compiler_params=pltpu.CompilerParams(vmem_limit_bytes=48 * 1024 * 1024),
    )(info, *own, *far)


ROWS = (LEN, WIDTH)
TABLE = ((8, WIDTH), f32)
BOTH_TABLES = ((2, 8, WIDTH), f32)
ATTENTION_OUT = (
    (ROWS, bf16),
    (ROWS, bf16),
    ((3, LEN, LOCAL), bf16),
    ((HEADS_DEV, LEN, LEN), f32),
    ((LEN, LOCAL), bf16),
    (ROWS, f32),
    (ROWS, bf16),
)
MLP_OUT = ((ROWS, f32), (ROWS, bf16), (ROWS, f32), (ROWS, bf16), (ROWS, f32), (ROWS, bf16))
MLP_BACK_OUT = ((ROWS, bf16), (ROWS, f32), (ROWS, bf16), ((LEN, 3072), bf16), TABLE)
ATTENTION_BACK_OUT = (
    (ROWS, f32),
    (ROWS, bf16),
    ((3, LEN, LOCAL), bf16),
    (ROWS, f32),
    (ROWS, bf16),
    ((LEN, 3072), bf16),
    TABLE,
)
MAKE_TABLE = device_kernel(make_table, "make_table", 0, (TABLE,))
FIRST_ATTENTION = device_kernel(first_attention, "first_attention", 2, ATTENTION_OUT, 0)
NEXT_ATTENTION = device_kernel(next_attention, "next_attention", 2, ATTENTION_OUT, 1)
MLP_FORWARD = tuple(
    device_kernel(functools.partial(mlp_forward, layer), "mlp_forward", 1, MLP_OUT, layer)
    for layer in range(2)
)
MLP_BACKWARD = device_kernel(
    mlp_backward, "mlp_backward", 1, ((ROWS, bf16),) + MLP_BACK_OUT, 1
)
MLP_BACKWARD_BELOW = device_kernel(
    mlp_backward_below, "mlp_backward_below", 1, ((ROWS, bf16), TABLE) + MLP_BACK_OUT, 0
)
ATTENTION_BACKWARD = tuple(
    device_kernel(
        functools.partial(attention_backward, layer),
        "attention_backward",
        1,
        ATTENTION_BACK_OUT + ((ROWS, f32),) * layer,
        layer,
    )
    for layer in range(2)
)
LAST_INPUT_GRAD = device_kernel(last_input_grad, "last_input_grad", 1, ((ROWS, f32), (ROWS, f32), BOTH_TABLES))
FIRST_HALVES = (((256, WIDTH), f32),) * 2 + (((256, WIDTH), bf16),) * 2
MLP_WEIGHT_GRADS = device_kernel(mlp_weight_grads, "mlp_weight_grads", 1, FIRST_HALVES)
ATTENTION_WEIGHT_GRADS = device_kernel(
    attention_weight_grads, "attention_weight_grads", 1, FIRST_HALVES
)


def blocks(rows, dtype):
    return (((2, rows, WIDTH), dtype),) * 4


def sent_blocks(rows):
    return (((2, rows + 16, WIDTH), bf16),) + (((2, rows, WIDTH), bf16),) * 3


JOIN_LAYERS = device_kernel(
    join_layers, "join_layers", 1, (BOTH_TABLES,) + blocks(128, f32) + sent_blocks(128)
)
REDUCE_LEVEL = {
    level: device_kernel(
        functools.partial(reduce_level, level),
        "reduce_level",
        1,
        (BOTH_TABLES,) + blocks(256 >> level, f32) + sent_blocks(256 >> level)
        if level < 4
        else (BOTH_TABLES, ((8, 16, WIDTH), f32), ((10, 16, WIDTH), bf16)),
    )
    for level in (2, 3, 4)
}
REDUCE_LAST = device_kernel(
    reduce_last, "reduce_last", 1, (TABLE, ((4, 16, WIDTH), bf16), ((5, 16, WIDTH), bf16))
)
GATHER_START = device_kernel(gather_start, "gather_start", 1, (TABLE, ((8, 16, WIDTH), bf16)))
GATHER_FIRST = device_kernel(gather_first, "gather_first", 1, blocks(32, bf16))
GATHER_LEVEL = {
    level: device_kernel(
        functools.partial(gather_level, level), "gather_level", 1, blocks(512 >> level, bf16)
    )
    for level in (3, 2, 1)
}


def step_bit(axis, pairs):
    index = lax.axis_index(axis)
    if pairs is PAIR_E:
        return (index ^ (index >> 1)) & 1
    if pairs is PAIR_F:
        return (index >> 1) & 1
    return index


def local(
    section_in,
    lengths,
    qkv_weight,
    qv_bias,
    out_weight,
    up_weight,
    up_bias,
    down_weight,
    norm_gains,
    row_biases,
):
    core = lax.axis_index("pipe")
    tensor_index = lax.axis_index("tensor")
    place = core * 2 + tensor_index
    both = ("pipe", "tensor")

    own_rows = section_in[0, 0, 0]
    near = lax.ppermute(own_rows, both, ((0, 1), (1, 2)))
    far = lax.ppermute(own_rows, both, ((1, 3),))

    (table,) = MAKE_TABLE(qv_bias[0], up_bias, norm_gains[0], row_biases[0])
    first_far = [lax.ppermute(array, "pipe", SWAP) for array in (qkv_weight[0], out_weight[0], table)]
    up_own, down_own, near, far, *first_far = lax.optimization_barrier(
        (up_weight[0], down_weight[0], near, far, *first_far)
    )
    second_far = [lax.ppermute(array, "pipe", SWAP) for array in (up_own, down_own)]
    table_far = first_far[2]
    qkv_w = (qkv_weight[0], first_far[0])
    out_w = (out_weight[0], first_far[1])
    up_w = (up_weight[0], second_far[0])
    down_w = (down_weight[0], second_far[1])
    tables = (table, table_far)

    bits = [step_bit(axis, pairs) for route in ROUTES for axis, pairs in route]
    info = jnp.stack([core, tensor_index] + bits).astype(jnp.int32)

    def swapped(sent):
        return lax.ppermute(sent, "tensor", SWAP)

    def crossed(sent):
        return lax.ppermute(sent, "pipe", SWAP)

    def first_step(grads, segment):
        return [
            lax.ppermute(array, *ROUTES[segment + i][0]) for i, array in enumerate(grads[2:])
        ]

    rows_0, attn_0, proj_0, prob_0, context_0, part, sent = FIRST_ATTENTION(
        info, lengths, own_rows, near, far, *tables, weights=(qkv_w, out_w)
    )
    received, cot_own = lax.optimization_barrier((swapped(sent), own_rows))
    cot_near = lax.ppermute(cot_own, both, ((2, 0), (3, 2)))
    cot_far = lax.ppermute(cot_own, both, ((2, 1),))
    resid_0, mlp_0, pre_0, act_0, part, sent = MLP_FORWARD[0](
        info, rows_0, part, received, *tables, weights=(up_w, down_w)
    )
    rows_1, attn_1, proj_1, prob_1, context_1, part, sent = NEXT_ATTENTION(
        info, lengths, resid_0, part, swapped(sent), *tables, weights=(qkv_w, out_w)
    )
    resid_1, mlp_1, pre_1, act_1, top_part, top_sent = MLP_FORWARD[1](
        info, rows_1, part, swapped(sent), *tables, weights=(up_w, down_w)
    )

    cotangent, pre_half_1, part, sent, cross_mlp, sums_mlp_1 = MLP_BACKWARD(
        info, own_rows, cot_near, cot_far, pre_1, act_1, mlp_1, weights=(down_w, up_w)
    )
    early_1 = MLP_WEIGHT_GRADS(info, act_1, cotangent, mlp_1, pre_half_1, crossed(cross_mlp))
    received, *early_1 = lax.optimization_barrier((swapped(sent), *early_1))
    *back_1, out_one = ATTENTION_BACKWARD[1](
        info, cotangent, part, received, resid_1, proj_1, prob_1, context_1, attn_1,
        top_part, swapped(top_sent), *tables, weights=(out_w, qkv_w),
    )
    grad_1, resid_half_1, proj_grad_1, part, sent, cross_attn, sums_attn_1 = back_1
    late_1 = ATTENTION_WEIGHT_GRADS(
        info, context_1, resid_half_1, attn_1, proj_grad_1, crossed(cross_attn)
    )
    received, *moved = lax.optimization_barrier(
        (swapped(sent), *late_1, *first_step(early_1, 0))
    )
    late_1, received_1 = moved[:4], moved[4:]
    grad_half, sums_in_1, pre_half_0, part, sent, cross_mlp, sums_mlp_0 = MLP_BACKWARD_BELOW(
        info, grad_1, part, received, rows_1, pre_0, act_0, mlp_0, *tables,
        weights=(down_w, up_w),
    )
    early_0 = MLP_WEIGHT_GRADS(info, act_0, grad_half, mlp_0, pre_half_0, crossed(cross_mlp))
    received, *moved = lax.optimization_barrier(
        (swapped(sent), *early_0, *first_step(late_1, 2))
    )
    early_0, received_1 = moved[:4], received_1 + moved[4:]
    grad_0, resid_half_0, proj_grad_0, part, sent, cross_attn, sums_attn_0 = ATTENTION_BACKWARD[0](
        info, grad_half, part, received, resid_0, proj_0, prob_0, context_0, attn_0, *tables,
        weights=(out_w, qkv_w),
    )
    late_0 = ATTENTION_WEIGHT_GRADS(
        info, context_0, resid_half_0, attn_0, proj_grad_0, crossed(cross_attn)
    )
    received, *moved = lax.optimization_barrier(
        (swapped(sent), *late_0, *first_step(early_0, 0))
    )
    late_0, received_0 = moved[:4], moved[4:]
    received_0 += first_step(late_0, 2)

    def half_steps(arrays, level):
        arrays = lax.optimization_barrier(tuple(arrays))
        return [
            lax.ppermute(array, *route[level]) for array, route in zip(arrays, ROUTES)
        ]

    kept_1 = (*early_1[:2], *late_1[:2])
    kept_0 = (*early_0[:2], *late_0[:2])

    kept_rows, crossing, vectors = LAST_INPUT_GRAD(
        info, grad_0, part, received, rows_0, out_one, *tables,
        sums_mlp_0, sums_attn_0, sums_in_1, sums_mlp_1, sums_attn_1,
    )
    vectors_in = lax.ppermute(vectors, *ROUTES[0][0])
    vectors, *stepped = JOIN_LAYERS(
        info, *kept_0, *kept_1, *received_0, *received_1, vectors, vectors_in
    )
    for level in (1, 2, 3):
        kept, sent = stepped[:4], stepped[4:]
        arrived = lax.optimization_barrier(half_steps(sent, level))
        vectors, *stepped = REDUCE_LEVEL[level + 1](info, vectors, *kept, *arrived)
    kept, sent = stepped
    vectors, own, far = REDUCE_LAST(info, vectors, kept, lax.ppermute(sent, "xh", SWAP))
    vectors, held = GATHER_START(info, vectors, own, crossed(far))
    shared = vectors[GAIN_A:]
    shared = 0.5 * (shared + swapped(shared))
    held = GATHER_FIRST(info, held, lax.ppermute(held, "xh", SWAP))
    for level in (3, 2, 1):
        arrived = lax.optimization_barrier(half_steps(held, level))
        held = GATHER_LEVEL[level](info, *held, *arrived)
    arrived = lax.optimization_barrier(half_steps(held, 0))
    qkv_g, out_g, up_g, down_g = assemble(info, held, arrived)

    crossing = lax.ppermute(crossing, both, ((0, 2), (3, 1)))
    section_out = jnp.where(core == tensor_index, kept_rows, crossing)
    return (
        section_out[None, None, None],
        qkv_g[None],
        vectors[0].reshape(1, 2, 512),
        out_g[None],
        up_g[None],
        vectors[1][None],
        down_g[None],
        shared[:2][None],
        shared[2:][None],
    )


def solution(mesh):
    fine = Mesh(mesh.devices.reshape(2, 2, 4, 4, 2), ("pipe", "tensor", "y", "z", "xh"))
    dp = ("y", "z", "xh")
    in_specs = (
        P("pipe", dp, "tensor", None, None),
        P(dp, None),
        P("pipe", None, None, "tensor"),
        P("pipe", None, "tensor"),
        P("pipe", "tensor", None),
        P("pipe", None, "tensor"),
        P("pipe", "tensor"),
        P("pipe", "tensor", None),
        P("pipe", None, None),
        P("pipe", None, None),
    )
    out_specs = (
        P("pipe", dp, "tensor", None, None),
        P("pipe", None, None, "tensor"),
        P("pipe", None, "tensor"),
        P("pipe", "tensor", None),
        P("pipe", None, "tensor"),
        P("pipe", "tensor"),
        P("pipe", "tensor", None),
        P("pipe", None, None),
        P("pipe", None, None),
    )
    return jax.shard_map(local, mesh=fine, in_specs=in_specs, out_specs=out_specs, check_vma=False)
```

```python
import functools

import jax
import jax.numpy as jnp
from jax import lax
from jax.experimental import pallas as pl
from jax.experimental.pallas import tpu as pltpu
from jax.sharding import Mesh
from jax.sharding import PartitionSpec as P

HEADS = 16
HD = 64
LEN = 128
norm_eps = 1e-05

f32 = jnp.float32
bf16 = jnp.bfloat16

SWAP = ((0, 1), (1, 0))
PAIR_E = ((0, 1), (1, 0), (2, 3), (3, 2))
PAIR_F = ((0, 3), (3, 0), (1, 2), (2, 1))
DP = ("y", "z", "xh")
ROUTES = (
    (("y", PAIR_E), ("y", PAIR_F), ("z", PAIR_E), ("z", PAIR_F), ("xh", SWAP)),
    (("y", PAIR_F), ("y", PAIR_E), ("z", PAIR_F), ("z", PAIR_E), ("xh", SWAP)),
    (("z", PAIR_E), ("z", PAIR_F), ("y", PAIR_E), ("y", PAIR_F), ("xh", SWAP)),
    (("z", PAIR_F), ("z", PAIR_E), ("y", PAIR_F), ("y", PAIR_E), ("xh", SWAP)),
)
CORE, TENSOR, BITS = 0, 1, 2


GELU_A = 0.7978845608028654
GELU_B = 0.044715
WIDTH = 1024
HEADS_DEV = HEADS // 2
LOCAL = HEADS_DEV * HD
PAIR = 2 * HD


def matmul(left, right):
    return jnp.dot(left, right, preferred_element_type=f32)


def matmul_nt(left, right):
    return lax.dot_general(left, right, (((1,), (1,)), ((), ())), preferred_element_type=f32)


def matmul_tn(left, right):
    return lax.dot_general(left, right, (((0,), (0,)), ((), ())), preferred_element_type=f32)


def norm_stats(values):
    centred = values - jnp.mean(values, axis=-1, keepdims=True)
    inv_std = lax.rsqrt(jnp.mean(centred * centred, axis=-1, keepdims=True) + norm_eps)
    return centred * inv_std, inv_std


def norm_back(grad_norm, normed, inv_std, gain):
    scaled = grad_norm * gain
    return inv_std * (
        scaled
        - jnp.mean(scaled, axis=-1, keepdims=True)
        - normed * jnp.mean(scaled * normed, axis=-1, keepdims=True)
    )


QV, UP_B, GAIN_A, GAIN_M, SHIFT_A, SHIFT_O, SHIFT_M, SHIFT_D = range(8)


def row(table, index):
    return table[index : index + 1, :]


def table_of(rows):
    zero = jnp.zeros((1, WIDTH), f32)
    return jnp.concatenate([rows.get(index, zero) for index in range(8)], axis=0)


def column_sum(block):
    return jnp.sum(block, axis=0, keepdims=True)


def head_lanes():
    return lax.broadcasted_iota(jnp.int32, (LEN, PAIR), 1) < HD


def attention_rows(rows, table, info, lengths, weights, outs):
    attn_rows_ref, proj_ref, prob_ref, context_ref, part_ref, sent_ref = outs
    normed, _ = norm_stats(rows.astype(f32))
    attn_rows = (normed * row(table, GAIN_A) + row(table, SHIFT_A)).astype(bf16)
    attn_rows_ref[...] = attn_rows
    attn_rows_ref.flush()
    qkv_w = weights[0].ready()
    for c in range(3):
        block = matmul(attn_rows, qkv_w[c])
        if c == 0:
            block = block + table[QV : QV + 1, :LOCAL]
        if c == 2:
            block = block + table[QV : QV + 1, LOCAL:]
        proj_ref[c] = block.astype(bf16)
    proj_ref.flush()
    spot_i = lax.broadcasted_iota(jnp.int32, (LEN, LEN), 0)
    spot_j = lax.broadcasted_iota(jnp.int32, (LEN, LEN), 1)
    allowed = (spot_j <= spot_i) & (spot_j < jnp.where(info[CORE] == 0, lengths[0, 0], lengths[0, 1]))
    offsets = (spot_i - spot_j).astype(f32)
    first = head_lanes()
    for pair in range(HEADS_DEV // 2):
        lanes = slice(pair * PAIR, (pair + 1) * PAIR)
        query, key, value = (proj_ref[c, :, lanes] for c in range(3))
        found = []
        for side in range(2):
            head = 2 * pair + side
            mine = jnp.where(first if side == 0 else ~first, query, jnp.zeros_like(query))
            slope = jnp.where(
                info[TENSOR] == 0,
                2.0 ** (-8.0 * (head + 1) / HEADS),
                2.0 ** (-8.0 * (head + HEADS_DEV + 1) / HEADS),
            )
            scores = matmul_nt(mine, key) * 0.125 - slope * offsets
            scores = jnp.where(allowed, scores, -jnp.inf)
            top_score = jnp.max(scores, axis=-1, keepdims=True)
            exp_scores = jnp.exp(scores - top_score)
            prob = exp_scores / jnp.sum(exp_scores, axis=-1, keepdims=True)
            prob_ref[head] = prob
            found.append(matmul(prob.astype(bf16), value))
        context_ref[:, lanes] = jnp.where(first, found[0], found[1]).astype(bf16)
    prob_ref.flush()
    context_ref.flush()
    part = matmul(context_ref[...], weights[1].ready()[...])
    part_ref[...] = part
    sent_ref[...] = part.astype(bf16)


def make_table(ins, weights, outs):
    qv_b, up_b, gains, shifts = ins
    outs[0][QV : QV + 1, :LOCAL] = qv_b[0:1, :].astype(f32)
    outs[0][QV : QV + 1, LOCAL:] = qv_b[1:2, :].astype(f32)
    outs[0][UP_B : UP_B + 1, :] = up_b[...].astype(f32)
    outs[0][GAIN_A : SHIFT_A, :] = gains[...]
    outs[0][SHIFT_A:, :] = shifts[...]


def table_for(info, tables, layer):
    own, far = tables
    return jnp.where(info[CORE] == layer, own[...], far[...])


def first_attention(ins, weights, outs):
    info, lengths, own_rows, near, far, *tables = ins
    rows_ref, *outs = outs
    place = 2 * info[CORE] + info[TENSOR]
    rows = jnp.where(place == 0, own_rows[...], jnp.where(place == 3, far[...], near[...]))
    rows_ref[...] = rows
    attention_rows(rows, table_for(info, tables, 0), info, lengths, weights, outs)


def next_attention(ins, weights, outs):
    info, lengths, resid, part, received, *tables = ins
    rows_ref, *outs = outs
    below = table_for(info, tables, 0)
    layer_out = resid[...] + (part[...] + received[...].astype(f32)) + row(below, SHIFT_D)
    rows = layer_out.astype(bf16)
    rows_ref[...] = rows
    attention_rows(rows, table_for(info, tables, 1), info, lengths, weights, outs)


def mlp_forward(layer, ins, weights, outs):
    info, rows, part, received, *tables = ins
    resid_ref, mlp_ref, pre_ref, act_ref, out_ref, sent_ref = outs
    table = table_for(info, tables, layer)
    resid = (
        rows[...].astype(f32) + (part[...] + received[...].astype(f32)) + row(table, SHIFT_O)
    )
    resid_ref[...] = resid
    resid_ref.flush()
    normed, _ = norm_stats(resid)
    mlp_rows = (normed * row(table, GAIN_M) + row(table, SHIFT_M)).astype(bf16)
    mlp_ref[...] = mlp_rows
    mlp_ref.flush()
    pre = matmul(mlp_rows, weights[0].ready()[...]) + row(table, UP_B)
    pre_ref[...] = pre
    pre_ref.flush()
    act = (0.5 * pre * (1.0 + jnp.tanh(GELU_A * (pre + GELU_B * pre * pre * pre)))).astype(bf16)
    act_ref[...] = act
    act_ref.flush()
    out = matmul(act, weights[1].ready()[...])
    out_ref[...] = out
    sent_ref[...] = out.astype(bf16)


def halves(core, block):
    half = block.shape[1] // 2
    low, high = block[:, :half], block[:, half:]
    own = core[CORE] == 0
    return jnp.where(own, low, high), jnp.where(own, high, low)


def mlp_back_body(info, grad, pre_in, act, mlp_rows, weights, outs):
    pre_half_ref, part_ref, sent_ref, cross_ref, sums_ref = outs
    grad_act = matmul_nt(grad, weights[0].ready()[...])
    pre = pre_in[...]
    tanh = jnp.tanh(GELU_A * (pre + GELU_B * pre * pre * pre))
    slope = 0.5 * (1.0 + tanh) + 0.5 * pre * (1.0 - tanh * tanh) * (
        GELU_A * (1.0 + 3.0 * GELU_B * pre * pre)
    )
    grad_pre = grad_act * slope
    pre_half = grad_pre.astype(bf16)
    pre_half_ref[...] = pre_half
    pre_half_ref.flush()
    part = matmul_nt(pre_half, weights[1].ready()[...])
    part_ref[...] = part
    sent_ref[...] = part.astype(bf16)
    cross_ref[:, :512] = halves(info, act[...])[1]
    cross_ref[:, 512:1536] = grad
    cross_ref[:, 1536:2048] = halves(info, mlp_rows[...])[1]
    cross_ref[:, 2048:] = pre_half
    return column_sum(grad_pre)


def mlp_backward(ins, weights, outs):
    info, cot_own, cot_near, cot_far, pre, act, mlp_rows = ins
    grad_ref, *outs = outs
    place = 2 * info[CORE] + info[TENSOR]
    grad = jnp.where(place == 3, cot_own[...], jnp.where(place == 1, cot_far[...], cot_near[...]))
    grad_ref[...] = grad
    total = mlp_back_body(info, grad, pre, act, mlp_rows, weights, outs)
    outs[4][...] = table_of({UP_B: total})


def input_grad(grad_resid, part, received, rows, table):
    grad_attn = part[...] + received[...].astype(f32)
    normed, inv_std = norm_stats(rows[...].astype(f32))
    grad_in = grad_resid[...] + norm_back(grad_attn, normed, inv_std, row(table, GAIN_A))
    sums = {GAIN_A: column_sum(grad_attn * normed), SHIFT_A: column_sum(grad_attn)}
    return grad_in, sums


def mlp_backward_below(ins, weights, outs):
    info, grad_resid, da_part, da_received, above_rows, pre, act, mlp_rows, *tables = ins
    grad_ref, above_ref, *outs = outs
    above = table_for(info, tables, 1)
    grad_in, sums = input_grad(grad_resid, da_part, da_received, above_rows, above)
    above_ref[...] = table_of(sums)
    grad = grad_in.astype(bf16)
    grad_ref[...] = grad
    total = mlp_back_body(info, grad, pre, act, mlp_rows, weights, outs)
    outs[4][...] = table_of({UP_B: total})


def last_input_grad(ins, weights, outs):
    info, grad_resid, part, received, rows, out_one, *tables = ins
    grad_in, sums = input_grad(grad_resid, part, received, rows, table_for(info, tables[:2], 0))
    low_core = info[CORE] == 0
    top = out_one[...]
    outs[0][...] = jnp.where(low_core, grad_in, top)
    outs[1][...] = jnp.where(low_core, top, grad_in)
    outs[2][0] = table_of(sums) + tables[2][...] + tables[3][...]
    outs[2][1] = tables[4][...] + tables[5][...] + tables[6][...]


def attention_backward(layer, ins, weights, outs):
    info, grad_out, dc_part, dc_received, resid, proj, prob_in, context, attn_rows, *tables = ins
    if layer == 1:
        *outs, out_ref = outs
        top_part, top_received, *tables = tables
        top = table_for(info, tables, 1)
        out_ref[...] = (
            resid[...] + (top_part[...] + top_received[...].astype(f32)) + row(top, SHIFT_D)
        )
    grad_ref, resid_half_ref, proj_grad_ref, part_ref, sent_ref, cross_ref, sums_ref = outs
    table = table_for(info, tables, layer)
    grad_mlp = dc_part[...] + dc_received[...].astype(f32)
    normed, inv_std = norm_stats(resid[...])
    wide_out = grad_out[...].astype(f32)
    grad_resid = wide_out + norm_back(grad_mlp, normed, inv_std, row(table, GAIN_M))
    grad_ref[...] = grad_resid
    grad_ref.flush()
    resid_half = grad_resid.astype(bf16)
    resid_half_ref[...] = resid_half
    resid_half_ref.flush()
    grad_context = matmul_nt(resid_half, weights[0].ready()[...]).astype(bf16)
    first = head_lanes()
    query_sums = []
    value_sums = []
    for pair in range(HEADS_DEV // 2):
        lanes = slice(pair * PAIR, (pair + 1) * PAIR)
        query, key, value = (proj[c, :, lanes] for c in range(3))
        context_grad = grad_context[:, lanes]
        query_g, key_g, value_g = [], [], []
        for side in range(2):
            mask = first if side == 0 else ~first
            prob = prob_in[2 * pair + side]
            mine = jnp.where(mask, context_grad, jnp.zeros_like(context_grad))
            grad_prob = matmul_nt(mine, value)
            value_g.append(matmul_tn(prob.astype(bf16), context_grad))
            delta = jnp.sum(prob * grad_prob, axis=-1, keepdims=True)
            grad_scores = (prob * (grad_prob - delta) * 0.125).astype(bf16)
            query_g.append(matmul(grad_scores, key))
            key_g.append(matmul_tn(grad_scores, query))
        query_g, key_g, value_g = (
            jnp.where(first, low, high) for low, high in (query_g, key_g, value_g)
        )
        query_sums.append(column_sum(query_g))
        value_sums.append(column_sum(value_g))
        proj_grad_ref[0, :, lanes] = query_g.astype(bf16)
        proj_grad_ref[1, :, lanes] = key_g.astype(bf16)
        proj_grad_ref[2, :, lanes] = value_g.astype(bf16)
    proj_grad_ref.flush()
    qkv_w = weights[1].ready()
    part = matmul_nt(proj_grad_ref[0], qkv_w[0])
    part = part + matmul_nt(proj_grad_ref[1], qkv_w[1])
    part = part + matmul_nt(proj_grad_ref[2], qkv_w[2])
    part_ref[...] = part
    sent_ref[...] = part.astype(bf16)
    cross_ref[:, :512] = context[...]
    cross_ref[:, 512:1024] = halves(info, resid_half)[1]
    cross_ref[:, 1024:1536] = halves(info, attn_rows[...])[1]
    for c in range(3):
        cross_ref[:, 1536 + c * LOCAL : 1536 + (c + 1) * LOCAL] = proj_grad_ref[c]
    sums_ref[...] = table_of(
        {
            QV: jnp.concatenate(query_sums + value_sums, axis=1),
            GAIN_M: column_sum(grad_mlp * normed),
            SHIFT_O: column_sum(grad_resid),
            SHIFT_M: column_sum(grad_mlp),
            SHIFT_D: column_sum(wide_out),
        }
    )


def stacked(own, far):
    return jnp.concatenate([own, far], axis=0)


def bit_of(info, segment, level):
    return info[BITS + 5 * segment + level]


def split(info, segment, level, block, keep_ref, send_ref):
    half = block.shape[-2] // 2
    low, high = block[..., :half, :], block[..., half:, :]
    own_low = bit_of(info, segment, level) == 0
    keep_ref[...] = jnp.where(own_low, low, high)
    send_ref[...] = jnp.where(own_low, high, low).astype(bf16)


def mlp_weight_grads(ins, weights, outs):
    info, act, grad, mlp_rows, pre_half, crossed = ins
    left = stacked(halves(info, act[...])[0], crossed[:, :512])
    right = stacked(grad[...], crossed[:, 512:1536])
    split(info, 0, 0, matmul_tn(left, right), outs[0], outs[2])
    outs[0].flush()
    outs[2].flush()
    left = stacked(halves(info, mlp_rows[...])[0], crossed[:, 1536:2048])
    right = stacked(pre_half[...], crossed[:, 2048:])
    split(info, 1, 0, matmul_tn(left, right), outs[1], outs[3])


def attention_weight_grads(ins, weights, outs):
    info, context, resid_half, attn_rows, proj_grad, crossed = ins
    left = stacked(halves(info, attn_rows[...])[0], crossed[:, 1024:1536])
    blocks = []
    for c in range(3):
        far = crossed[:, 1536 + c * LOCAL : 1536 + (c + 1) * LOCAL]
        blocks.append(matmul_tn(left, stacked(proj_grad[c], far)))
    left = stacked(context[...], crossed[:, :512])
    right = stacked(halves(info, resid_half[...])[0], crossed[:, 512:1024])
    blocks.append(matmul_tn(left, right))
    split(info, 2, 0, jnp.concatenate(blocks[:2], axis=1), outs[0], outs[2])
    outs[0].flush()
    outs[2].flush()
    split(info, 3, 0, jnp.concatenate(blocks[2:], axis=1), outs[1], outs[3])


def two_parts(vector):
    high = vector.astype(bf16)
    low = (vector - high.astype(f32)).astype(bf16)
    return high, low, high.astype(f32) + low.astype(f32)


def join_layers(ins, weights, outs):
    info = ins[0]
    kept = (ins[1:5], ins[5:9])
    received = (ins[9:13], ins[13:17])
    vector, vector_in = ins[17:]
    for segment in range(4):
        for layer in range(2):
            total = kept[layer][segment][...] + received[layer][segment][...].astype(f32)
            sent = outs[5 + segment].at[layer, :128]
            split(info, segment, 1, total, outs[1 + segment].at[layer], sent)
        outs[1 + segment].flush()
        if segment:
            outs[5 + segment].flush()
    high, low, outs[0][...] = two_parts(vector[...] + vector_in[...])
    outs[5][:, 128:136] = high
    outs[5][:, 136:] = low


def reduce_level(level, ins, weights, outs):
    info, vector = ins[:2]
    rows = ins[2].shape[1]
    half = rows // 2
    total = vector[...] + (ins[6][:, rows : rows + 8].astype(f32) + ins[6][:, rows + 8 :].astype(f32))
    high, low, outs[0][...] = two_parts(total)
    for segment in range(4):
        total = ins[2 + segment][...] + ins[6 + segment][:, :rows].astype(f32)
        if level < 4:
            split(info, segment, level, total, outs[1 + segment], outs[5 + segment].at[:, :half])
            outs[1 + segment].flush()
            if segment:
                outs[5 + segment].flush()
        else:
            place = slice(2 * segment, 2 * segment + 2)
            split(info, segment, level, total, outs[1].at[place], outs[2].at[place])
    if level < 4:
        outs[5][:, half : half + 8] = high
        outs[5][:, half + 8 :] = low
    else:
        outs[2][8:, :8] = high
        outs[2][8:, 8:] = low


def reduce_last(ins, weights, outs):
    info, vector, kept, received = ins
    low_core = info[CORE] == 0
    for segment in range(4):
        place = slice(2 * segment, 2 * segment + 2)
        total = (kept[place] + received[place].astype(f32)).astype(bf16)
        outs[1][segment] = jnp.where(low_core, total[0], total[1])
        outs[2][segment] = jnp.where(low_core, total[1], total[0])
    total = vector[...] + (received[8:, :8].astype(f32) + received[8:, 8:].astype(f32))
    outs[0][...] = jnp.where(low_core, total[0], total[1])
    high, low, _ = two_parts(jnp.where(low_core, total[1], total[0]))
    outs[2][4, :8] = high
    outs[2][4, 8:] = low


def gather_start(ins, weights, outs):
    info, vector, own, far = ins
    low_core = info[CORE] == 0
    outs[0][...] = vector[...] + (far[4, :8].astype(f32) + far[4, 8:].astype(f32))
    for segment in range(4):
        outs[1][2 * segment] = jnp.where(low_core, own[segment], far[segment])
        outs[1][2 * segment + 1] = jnp.where(low_core, far[segment], own[segment])


def gather_first(ins, weights, outs):
    info, mine, theirs = ins
    for segment in range(4):
        place = slice(2 * segment, 2 * segment + 2)
        own, far = mine[place], theirs[place]
        own_low = bit_of(info, segment, 4) == 0
        outs[segment][:, :16] = jnp.where(own_low, own, far)
        outs[segment][:, 16:] = jnp.where(own_low, far, own)


def gather_level(level, ins, weights, outs):
    info = ins[0]
    for segment in range(4):
        own, far = ins[1 + segment][...], ins[5 + segment][...]
        half = own.shape[1]
        own_low = bit_of(info, segment, level) == 0
        outs[segment][:, :half] = jnp.where(own_low, own, far)
        outs[segment][:, half:] = jnp.where(own_low, far, own)
        outs[segment].flush()


class Loaded:
    def __init__(self, source, buffer, semaphore):
        self.copy = pltpu.make_async_copy(source, buffer, semaphore)
        self.copy.start()
        self.buffer = buffer
        self.waiting = True

    def ready(self):
        if self.waiting:
            self.waiting = False
            self.copy.wait()
        return self.buffer

    def __getitem__(self, place):
        return self.ready()[place]

    @property
    def shape(self):
        return self.buffer.shape


class Fetched(Loaded):
    def __init__(self, info, layer, own, far, buffer, semaphore):
        self.copy = pltpu.make_async_copy(own, buffer, semaphore)
        other = pltpu.make_async_copy(far, buffer, semaphore)
        pl.when(info[CORE] == layer)(self.copy.start)
        pl.when(info[CORE] != layer)(other.start)
        self.buffer = buffer
        self.waiting = True


class Stored:
    def __init__(self, target, buffer, semaphore):
        self.copy = pltpu.make_async_copy(buffer, target, semaphore)
        self.buffer = buffer
        self.sent = False

    def __setitem__(self, place, value):
        self.buffer[place] = value

    def __getitem__(self, place):
        return self.buffer[place]

    @property
    def at(self):
        return self.buffer.at

    def flush(self):
        if not self.sent:
            self.sent = True
            self.copy.start()


def device_kernel(body, name, scalars, shapes, layer=0):
    def call(*operands, weights=()):
        arrays = operands[scalars:]
        flat = [array for pair in weights for array in pair]
        count, total, results = len(arrays), len(weights), len(shapes)

        def kernel(*refs):
            numbers, refs = refs[:scalars], refs[scalars:]
            sources, refs = refs[:count], refs[count:]
            pairs, refs = refs[: 2 * total], refs[2 * total :]
            targets, refs = refs[:results], refs[results:]
            buffers, semaphores = refs[: count + total + results], refs[count + total + results :]
            slots = list(zip(buffers, semaphores))
            loaded = [Loaded(sources[i], *slots[i]) for i in range(count)]
            fetched = [
                Fetched(numbers[0], layer, pairs[2 * i], pairs[2 * i + 1], *slots[count + i])
                for i in range(total)
            ]
            stored = [Stored(targets[i], *slots[count + total + i]) for i in range(results)]
            body([*numbers, *loaded], fetched, stored)
            for operand in loaded + fetched:
                operand.ready()
            for result in stored:
                result.flush()
            for result in stored:
                result.copy.wait()

        smem = pl.BlockSpec(memory_space=pltpu.SMEM)
        hbm = pl.BlockSpec(memory_space=pl.ANY)
        held = [(array.shape, array.dtype) for array in arrays]
        held += [(own.shape, own.dtype) for own, _ in weights] + list(shapes)
        return pl.pallas_call(
            kernel,
            name=name,
            in_specs=[smem] * scalars + [hbm] * (count + len(flat)),
            out_specs=[hbm] * results,
            out_shape=[jax.ShapeDtypeStruct(shape, dtype) for shape, dtype in shapes],
            scratch_shapes=[pltpu.VMEM(shape, dtype) for shape, dtype in held]
            + [pltpu.SemaphoreType.DMA(())] * len(held),
            compiler_params=pltpu.CompilerParams(vmem_limit_bytes=63 * 1024 * 1024),
        )(*operands, *flat)

    return call


def assemble(info, blocks, far, results=()):
    def kernel(info, *refs):
        sources, refs = refs[:4], refs[4 + len(results) :]
        qkv_ref, out_ref, up_ref, down_ref = refs[:4]
        buffers, wide, semaphores = refs[4:8], refs[8], refs[9:]
        loaded = [Loaded(sources[i], buffers[i], semaphores[i]) for i in range(4)]
        copies = []

        def send(source, target):
            copies.append(pltpu.make_async_copy(source, target, semaphores[4 + len(copies)]))
            copies[-1].start()

        for segment in range(4):
            bit = bit_of(info, segment, 0) ^ far
            for half in range(2):
                wide[segment, half] = loaded[segment][half].astype(f32)
                block = wide.at[segment, half]
                rows = pl.ds(pl.multiple_of(half * 512 + bit * 256, 256), 256)
                left, right = block.at[:, :512], block.at[:, 512:]
                if segment == 0:
                    send(block, down_ref.at[rows, :])
                if segment == 1:
                    send(block, up_ref.at[rows, :])
                if segment == 2:
                    send(left, qkv_ref.at[0, rows, :])
                    send(right, qkv_ref.at[1, rows, :])
                if segment == 3:
                    send(left, qkv_ref.at[2, rows, :])
                    short = pl.ds(pl.multiple_of(bit * 256, 256), 256)
                    send(right, out_ref.at[short, half * 512 : (half + 1) * 512])
        for copy in copies:
            copy.wait()

    hbm = pl.BlockSpec(memory_space=pl.ANY)
    return pl.pallas_call(
        kernel,
        name="assemble",
        in_specs=[pl.BlockSpec(memory_space=pltpu.SMEM)] + [hbm] * (4 + len(results)),
        out_specs=[hbm] * 4,
        out_shape=[
            jax.ShapeDtypeStruct((3, 1024, 512), f32),
            jax.ShapeDtypeStruct((512, 1024), f32),
            jax.ShapeDtypeStruct((1024, 1024), f32),
            jax.ShapeDtypeStruct((1024, 1024), f32),
        ],
        scratch_shapes=[pltpu.VMEM((2, 256, WIDTH), bf16)] * 4
        + [pltpu.VMEM((4, 2, 256, WIDTH), f32)]
        + [pltpu.SemaphoreType.DMA(())] * 16,
        input_output_aliases={5 + i: i for i in range(len(results))},
        compiler_params=pltpu.CompilerParams(vmem_limit_bytes=63 * 1024 * 1024),
    )(info, *blocks, *results)


ROWS = (LEN, WIDTH)
TABLE = ((8, WIDTH), f32)
BOTH_TABLES = ((2, 8, WIDTH), f32)
ATTENTION_OUT = (
    (ROWS, bf16),
    (ROWS, bf16),
    ((3, LEN, LOCAL), bf16),
    ((HEADS_DEV, LEN, LEN), f32),
    ((LEN, LOCAL), bf16),
    (ROWS, f32),
    (ROWS, bf16),
)
MLP_OUT = ((ROWS, f32), (ROWS, bf16), (ROWS, f32), (ROWS, bf16), (ROWS, f32), (ROWS, bf16))
MLP_BACK_OUT = ((ROWS, bf16), (ROWS, f32), (ROWS, bf16), ((LEN, 3072), bf16), TABLE)
ATTENTION_BACK_OUT = (
    (ROWS, f32),
    (ROWS, bf16),
    ((3, LEN, LOCAL), bf16),
    (ROWS, f32),
    (ROWS, bf16),
    ((LEN, 3072), bf16),
    TABLE,
)
MAKE_TABLE = device_kernel(make_table, "make_table", 0, (TABLE,))
FIRST_ATTENTION = device_kernel(first_attention, "first_attention", 2, ATTENTION_OUT, 0)
NEXT_ATTENTION = device_kernel(next_attention, "next_attention", 2, ATTENTION_OUT, 1)
MLP_FORWARD = tuple(
    device_kernel(functools.partial(mlp_forward, layer), "mlp_forward", 1, MLP_OUT, layer)
    for layer in range(2)
)
MLP_BACKWARD = device_kernel(
    mlp_backward, "mlp_backward", 1, ((ROWS, bf16),) + MLP_BACK_OUT, 1
)
MLP_BACKWARD_BELOW = device_kernel(
    mlp_backward_below, "mlp_backward_below", 1, ((ROWS, bf16), TABLE) + MLP_BACK_OUT, 0
)
ATTENTION_BACKWARD = tuple(
    device_kernel(
        functools.partial(attention_backward, layer),
        "attention_backward",
        1,
        ATTENTION_BACK_OUT + ((ROWS, f32),) * layer,
        layer,
    )
    for layer in range(2)
)
LAST_INPUT_GRAD = device_kernel(last_input_grad, "last_input_grad", 1, ((ROWS, f32), (ROWS, f32), BOTH_TABLES))
FIRST_HALVES = (((256, WIDTH), f32),) * 2 + (((256, WIDTH), bf16),) * 2
MLP_WEIGHT_GRADS = device_kernel(mlp_weight_grads, "mlp_weight_grads", 1, FIRST_HALVES)
ATTENTION_WEIGHT_GRADS = device_kernel(
    attention_weight_grads, "attention_weight_grads", 1, FIRST_HALVES
)


def blocks(rows, dtype):
    return (((2, rows, WIDTH), dtype),) * 4


def sent_blocks(rows):
    return (((2, rows + 16, WIDTH), bf16),) + (((2, rows, WIDTH), bf16),) * 3


JOIN_LAYERS = device_kernel(
    join_layers, "join_layers", 1, (BOTH_TABLES,) + blocks(128, f32) + sent_blocks(128)
)
REDUCE_LEVEL = {
    level: device_kernel(
        functools.partial(reduce_level, level),
        "reduce_level",
        1,
        (BOTH_TABLES,) + blocks(256 >> level, f32) + sent_blocks(256 >> level)
        if level < 4
        else (BOTH_TABLES, ((8, 16, WIDTH), f32), ((10, 16, WIDTH), bf16)),
    )
    for level in (2, 3, 4)
}
REDUCE_LAST = device_kernel(
    reduce_last, "reduce_last", 1, (TABLE, ((4, 16, WIDTH), bf16), ((5, 16, WIDTH), bf16))
)
GATHER_START = device_kernel(gather_start, "gather_start", 1, (TABLE, ((8, 16, WIDTH), bf16)))
GATHER_FIRST = device_kernel(gather_first, "gather_first", 1, blocks(32, bf16))
GATHER_LEVEL = {
    level: device_kernel(
        functools.partial(gather_level, level), "gather_level", 1, blocks(512 >> level, bf16)
    )
    for level in (3, 2, 1)
}


def step_bit(axis, pairs):
    index = lax.axis_index(axis)
    if pairs is PAIR_E:
        return (index ^ (index >> 1)) & 1
    if pairs is PAIR_F:
        return (index >> 1) & 1
    return index


def local(
    section_in,
    lengths,
    qkv_weight,
    qv_bias,
    out_weight,
    up_weight,
    up_bias,
    down_weight,
    norm_gains,
    row_biases,
):
    core = lax.axis_index("pipe")
    tensor_index = lax.axis_index("tensor")
    place = core * 2 + tensor_index
    both = ("pipe", "tensor")

    own_rows = section_in[0, 0, 0]
    near = lax.ppermute(own_rows, both, ((0, 1), (1, 2)))
    far = lax.ppermute(own_rows, both, ((1, 3),))

    (table,) = MAKE_TABLE(qv_bias[0], up_bias, norm_gains[0], row_biases[0])
    first_far = [lax.ppermute(array, "pipe", SWAP) for array in (qkv_weight[0], out_weight[0], table)]
    up_own, down_own, near, far, *first_far = lax.optimization_barrier(
        (up_weight[0], down_weight[0], near, far, *first_far)
    )
    second_far = [lax.ppermute(array, "pipe", SWAP) for array in (up_own, down_own)]
    table_far = first_far[2]
    qkv_w = (qkv_weight[0], first_far[0])
    out_w = (out_weight[0], first_far[1])
    up_w = (up_weight[0], second_far[0])
    down_w = (down_weight[0], second_far[1])
    tables = (table, table_far)

    bits = [step_bit(axis, pairs) for route in ROUTES for axis, pairs in route]
    info = jnp.stack([core, tensor_index] + bits).astype(jnp.int32)

    def swapped(sent):
        return lax.ppermute(sent, "tensor", SWAP)

    def crossed(sent):
        return lax.ppermute(sent, "pipe", SWAP)

    rows_0, attn_0, proj_0, prob_0, context_0, part, sent = FIRST_ATTENTION(
        info, lengths, own_rows, near, far, *tables, weights=(qkv_w, out_w)
    )
    received, cot_own = lax.optimization_barrier((swapped(sent), own_rows))
    cot_near = lax.ppermute(cot_own, both, ((2, 0), (3, 2)))
    cot_far = lax.ppermute(cot_own, both, ((2, 1),))
    resid_0, mlp_0, pre_0, act_0, part, sent = MLP_FORWARD[0](
        info, rows_0, part, received, *tables, weights=(up_w, down_w)
    )
    rows_1, attn_1, proj_1, prob_1, context_1, part, sent = NEXT_ATTENTION(
        info, lengths, resid_0, part, swapped(sent), *tables, weights=(qkv_w, out_w)
    )
    resid_1, mlp_1, pre_1, act_1, top_part, top_sent = MLP_FORWARD[1](
        info, rows_1, part, swapped(sent), *tables, weights=(up_w, down_w)
    )

    cotangent, pre_half_1, part, sent, cross_mlp, sums_mlp_1 = MLP_BACKWARD(
        info, own_rows, cot_near, cot_far, pre_1, act_1, mlp_1, weights=(down_w, up_w)
    )
    early_1 = MLP_WEIGHT_GRADS(info, act_1, cotangent, mlp_1, pre_half_1, crossed(cross_mlp))
    received, *early_1 = lax.optimization_barrier((swapped(sent), *early_1))
    *back_1, out_one = ATTENTION_BACKWARD[1](
        info, cotangent, part, received, resid_1, proj_1, prob_1, context_1, attn_1,
        top_part, swapped(top_sent), *tables, weights=(out_w, qkv_w),
    )
    grad_1, resid_half_1, proj_grad_1, part, sent, cross_attn, sums_attn_1 = back_1
    late_1 = ATTENTION_WEIGHT_GRADS(
        info, context_1, resid_half_1, attn_1, proj_grad_1, crossed(cross_attn)
    )
    received, *late_1 = lax.optimization_barrier((swapped(sent), *late_1))
    grad_half, sums_in_1, pre_half_0, part, sent, cross_mlp, sums_mlp_0 = MLP_BACKWARD_BELOW(
        info, grad_1, part, received, rows_1, pre_0, act_0, mlp_0, *tables,
        weights=(down_w, up_w),
    )
    early_0 = MLP_WEIGHT_GRADS(info, act_0, grad_half, mlp_0, pre_half_0, crossed(cross_mlp))
    received, *early_0 = lax.optimization_barrier((swapped(sent), *early_0))
    grad_0, resid_half_0, proj_grad_0, part, sent, cross_attn, sums_attn_0 = ATTENTION_BACKWARD[0](
        info, grad_half, part, received, resid_0, proj_0, prob_0, context_0, attn_0, *tables,
        weights=(out_w, qkv_w),
    )
    late_0 = ATTENTION_WEIGHT_GRADS(
        info, context_0, resid_half_0, attn_0, proj_grad_0, crossed(cross_attn)
    )
    received, *late_0 = lax.optimization_barrier((swapped(sent), *late_0))

    def half_steps(arrays, level):
        arrays = lax.optimization_barrier(tuple(arrays))
        return [
            lax.ppermute(array, *route[level]) for array, route in zip(arrays, ROUTES)
        ]

    kept_1 = (*early_1[:2], *late_1[:2])
    kept_0 = (*early_0[:2], *late_0[:2])
    received_1 = half_steps((*early_1[2:], *late_1[2:]), 0)
    received_0 = half_steps((*early_0[2:], *late_0[2:]), 0)

    kept_rows, crossing, vectors = LAST_INPUT_GRAD(
        info, grad_0, part, received, rows_0, out_one, *tables,
        sums_mlp_0, sums_attn_0, sums_in_1, sums_mlp_1, sums_attn_1,
    )
    vectors_in = lax.ppermute(vectors, *ROUTES[0][0])
    vectors, *stepped = JOIN_LAYERS(
        info, *kept_0, *kept_1, *received_0, *received_1, vectors, vectors_in
    )
    for level in (1, 2, 3):
        kept, sent = stepped[:4], stepped[4:]
        arrived = lax.optimization_barrier(half_steps(sent, level))
        vectors, *stepped = REDUCE_LEVEL[level + 1](info, vectors, *kept, *arrived)
    kept, sent = stepped
    vectors, own, far = REDUCE_LAST(info, vectors, kept, lax.ppermute(sent, "xh", SWAP))
    vectors, held = GATHER_START(info, vectors, own, crossed(far))
    shared = vectors[GAIN_A:]
    shared = 0.5 * (shared + swapped(shared))
    held = GATHER_FIRST(info, held, lax.ppermute(held, "xh", SWAP))
    for level in (3, 2, 1):
        arrived = lax.optimization_barrier(half_steps(held, level))
        held = GATHER_LEVEL[level](info, *held, *arrived)
    arrived = lax.optimization_barrier(half_steps(held, 0))
    results = assemble(info, held, 0)
    qkv_g, out_g, up_g, down_g = assemble(info, arrived, 1, results)

    crossing = lax.ppermute(crossing, both, ((0, 2), (3, 1)))
    section_out = jnp.where(core == tensor_index, kept_rows, crossing)
    return (
        section_out[None, None, None],
        qkv_g[None],
        vectors[0].reshape(1, 2, 512),
        out_g[None],
        up_g[None],
        vectors[1][None],
        down_g[None],
        shared[:2][None],
        shared[2:][None],
    )


def solution(mesh):
    fine = Mesh(mesh.devices.reshape(2, 2, 4, 4, 2), ("pipe", "tensor", "y", "z", "xh"))
    dp = ("y", "z", "xh")
    in_specs = (
        P("pipe", dp, "tensor", None, None),
        P(dp, None),
        P("pipe", None, None, "tensor"),
        P("pipe", None, "tensor"),
        P("pipe", "tensor", None),
        P("pipe", None, "tensor"),
        P("pipe", "tensor"),
        P("pipe", "tensor", None),
        P("pipe", None, None),
        P("pipe", None, None),
    )
    out_specs = (
        P("pipe", dp, "tensor", None, None),
        P("pipe", None, None, "tensor"),
        P("pipe", None, "tensor"),
        P("pipe", "tensor", None),
        P("pipe", None, "tensor"),
        P("pipe", "tensor"),
        P("pipe", "tensor", None),
        P("pipe", None, None),
        P("pipe", None, None),
    )
    return jax.shard_map(local, mesh=fine, in_specs=in_specs, out_specs=out_specs, check_vma=False)
```

```python
import functools

import jax
import jax.numpy as jnp
from jax import lax
from jax.experimental import pallas as pl
from jax.experimental.pallas import tpu as pltpu
from jax.sharding import Mesh
from jax.sharding import PartitionSpec as P

HEADS = 16
HD = 64
LEN = 128
norm_eps = 1e-05

f32 = jnp.float32
bf16 = jnp.bfloat16

SWAP = ((0, 1), (1, 0))
PAIR_E = ((0, 1), (1, 0), (2, 3), (3, 2))
PAIR_F = ((0, 3), (3, 0), (1, 2), (2, 1))
DP = ("y", "z", "xh")
ROUTES = (
    (("y", PAIR_E), ("y", PAIR_F), ("z", PAIR_E), ("z", PAIR_F), ("xh", SWAP)),
    (("y", PAIR_F), ("y", PAIR_E), ("z", PAIR_F), ("z", PAIR_E), ("xh", SWAP)),
    (("z", PAIR_E), ("z", PAIR_F), ("y", PAIR_E), ("y", PAIR_F), ("xh", SWAP)),
    (("z", PAIR_F), ("z", PAIR_E), ("y", PAIR_F), ("y", PAIR_E), ("xh", SWAP)),
)
CORE, TENSOR, BITS = 0, 1, 2


GELU_A = 0.7978845608028654
GELU_B = 0.044715
WIDTH = 1024
HEADS_DEV = HEADS // 2
LOCAL = HEADS_DEV * HD
PAIR = 2 * HD


def matmul(left, right):
    return jnp.dot(left, right, preferred_element_type=f32)


def matmul_nt(left, right):
    return lax.dot_general(left, right, (((1,), (1,)), ((), ())), preferred_element_type=f32)


def matmul_tn(left, right):
    return lax.dot_general(left, right, (((0,), (0,)), ((), ())), preferred_element_type=f32)


def norm_stats(values):
    centred = values - jnp.mean(values, axis=-1, keepdims=True)
    inv_std = lax.rsqrt(jnp.mean(centred * centred, axis=-1, keepdims=True) + norm_eps)
    return centred * inv_std, inv_std


def norm_back(grad_norm, normed, inv_std, gain):
    scaled = grad_norm * gain
    return inv_std * (
        scaled
        - jnp.mean(scaled, axis=-1, keepdims=True)
        - normed * jnp.mean(scaled * normed, axis=-1, keepdims=True)
    )


QV, UP_B, GAIN_A, GAIN_M, SHIFT_A, SHIFT_O, SHIFT_M, SHIFT_D = range(8)


def row(table, index):
    return table[index : index + 1, :]


def table_of(rows):
    zero = jnp.zeros((1, WIDTH), f32)
    return jnp.concatenate([rows.get(index, zero) for index in range(8)], axis=0)


def column_sum(block):
    return jnp.sum(block, axis=0, keepdims=True)


def head_lanes():
    return lax.broadcasted_iota(jnp.int32, (LEN, PAIR), 1) < HD


def attention_rows(rows, table, info, lengths, weights, outs):
    attn_rows_ref, proj_ref, prob_ref, context_ref, part_ref, sent_ref = outs
    normed, _ = norm_stats(rows.astype(f32))
    attn_rows = (normed * row(table, GAIN_A) + row(table, SHIFT_A)).astype(bf16)
    attn_rows_ref[...] = attn_rows
    qkv_w = weights[0].ready()
    for c in range(3):
        block = matmul(attn_rows, qkv_w[c])
        if c == 0:
            block = block + table[QV : QV + 1, :LOCAL]
        if c == 2:
            block = block + table[QV : QV + 1, LOCAL:]
        proj_ref[c] = block.astype(bf16)
    spot_i = lax.broadcasted_iota(jnp.int32, (LEN, LEN), 0)
    spot_j = lax.broadcasted_iota(jnp.int32, (LEN, LEN), 1)
    allowed = (spot_j <= spot_i) & (spot_j < jnp.where(info[CORE] == 0, lengths[0, 0], lengths[0, 1]))
    offsets = (spot_i - spot_j).astype(f32)
    first = head_lanes()
    for pair in range(HEADS_DEV // 2):
        lanes = slice(pair * PAIR, (pair + 1) * PAIR)
        query, key, value = (proj_ref[c, :, lanes] for c in range(3))
        found = []
        for side in range(2):
            head = 2 * pair + side
            mine = jnp.where(first if side == 0 else ~first, query, jnp.zeros_like(query))
            slope = jnp.where(
                info[TENSOR] == 0,
                2.0 ** (-8.0 * (head + 1) / HEADS),
                2.0 ** (-8.0 * (head + HEADS_DEV + 1) / HEADS),
            )
            scores = matmul_nt(mine, key) * 0.125 - slope * offsets
            scores = jnp.where(allowed, scores, -jnp.inf)
            top_score = jnp.max(scores, axis=-1, keepdims=True)
            exp_scores = jnp.exp(scores - top_score)
            prob = exp_scores / jnp.sum(exp_scores, axis=-1, keepdims=True)
            prob_ref[head] = prob
            found.append(matmul(prob.astype(bf16), value))
        context_ref[:, lanes] = jnp.where(first, found[0], found[1]).astype(bf16)
    part = matmul(context_ref[...], weights[1].ready()[...])
    part_ref[...] = part
    sent_ref[...] = part.astype(bf16)


def make_table(ins, weights, outs):
    qv_b, up_b, gains, shifts = ins
    outs[0][QV : QV + 1, :LOCAL] = qv_b[0:1, :].astype(f32)
    outs[0][QV : QV + 1, LOCAL:] = qv_b[1:2, :].astype(f32)
    outs[0][UP_B : UP_B + 1, :] = up_b[...].astype(f32)
    outs[0][GAIN_A : SHIFT_A, :] = gains[...]
    outs[0][SHIFT_A:, :] = shifts[...]


def table_for(info, tables, layer):
    own, far = tables
    return jnp.where(info[CORE] == layer, own[...], far[...])


def first_attention(ins, weights, outs):
    info, lengths, own_rows, near, far, *tables = ins
    rows_ref, *outs = outs
    place = 2 * info[CORE] + info[TENSOR]
    rows = jnp.where(place == 0, own_rows[...], jnp.where(place == 3, far[...], near[...]))
    rows_ref[...] = rows
    attention_rows(rows, table_for(info, tables, 0), info, lengths, weights, outs)


def next_attention(ins, weights, outs):
    info, lengths, resid, part, received, *tables = ins
    rows_ref, *outs = outs
    below = table_for(info, tables, 0)
    layer_out = resid[...] + (part[...] + received[...].astype(f32)) + row(below, SHIFT_D)
    rows = layer_out.astype(bf16)
    rows_ref[...] = rows
    attention_rows(rows, table_for(info, tables, 1), info, lengths, weights, outs)


def mlp_forward(layer, ins, weights, outs):
    info, rows, part, received, *tables = ins
    resid_ref, mlp_ref, pre_ref, act_ref, out_ref, sent_ref = outs
    table = table_for(info, tables, layer)
    resid = (
        rows[...].astype(f32) + (part[...] + received[...].astype(f32)) + row(table, SHIFT_O)
    )
    resid_ref[...] = resid
    normed, _ = norm_stats(resid)
    mlp_rows = (normed * row(table, GAIN_M) + row(table, SHIFT_M)).astype(bf16)
    mlp_ref[...] = mlp_rows
    pre = matmul(mlp_rows, weights[0].ready()[...]) + row(table, UP_B)
    pre_ref[...] = pre
    act = (0.5 * pre * (1.0 + jnp.tanh(GELU_A * (pre + GELU_B * pre * pre * pre)))).astype(bf16)
    act_ref[...] = act
    out = matmul(act, weights[1].ready()[...])
    out_ref[...] = out
    sent_ref[...] = out.astype(bf16)


def halves(core, block):
    half = block.shape[1] // 2
    low, high = block[:, :half], block[:, half:]
    own = core[CORE] == 0
    return jnp.where(own, low, high), jnp.where(own, high, low)


def mlp_back_body(info, grad, pre_in, act, mlp_rows, weights, outs):
    pre_half_ref, part_ref, sent_ref, cross_ref, sums_ref = outs
    grad_act = matmul_nt(grad, weights[0].ready()[...])
    pre = pre_in[...]
    tanh = jnp.tanh(GELU_A * (pre + GELU_B * pre * pre * pre))
    slope = 0.5 * (1.0 + tanh) + 0.5 * pre * (1.0 - tanh * tanh) * (
        GELU_A * (1.0 + 3.0 * GELU_B * pre * pre)
    )
    grad_pre = grad_act * slope
    pre_half = grad_pre.astype(bf16)
    pre_half_ref[...] = pre_half
    part = matmul_nt(pre_half, weights[1].ready()[...])
    part_ref[...] = part
    sent_ref[...] = part.astype(bf16)
    cross_ref[:, :512] = halves(info, act[...])[1]
    cross_ref[:, 512:1536] = grad
    cross_ref[:, 1536:2048] = halves(info, mlp_rows[...])[1]
    cross_ref[:, 2048:] = pre_half
    return column_sum(grad_pre)


def mlp_backward(ins, weights, outs):
    info, cot_own, cot_near, cot_far, pre, act, mlp_rows = ins
    grad_ref, *outs = outs
    place = 2 * info[CORE] + info[TENSOR]
    grad = jnp.where(place == 3, cot_own[...], jnp.where(place == 1, cot_far[...], cot_near[...]))
    grad_ref[...] = grad
    total = mlp_back_body(info, grad, pre, act, mlp_rows, weights, outs)
    outs[4][...] = table_of({UP_B: total})


def input_grad(grad_resid, part, received, rows, table):
    grad_attn = part[...] + received[...].astype(f32)
    normed, inv_std = norm_stats(rows[...].astype(f32))
    grad_in = grad_resid[...] + norm_back(grad_attn, normed, inv_std, row(table, GAIN_A))
    sums = {GAIN_A: column_sum(grad_attn * normed), SHIFT_A: column_sum(grad_attn)}
    return grad_in, sums


def mlp_backward_below(ins, weights, outs):
    info, grad_resid, da_part, da_received, above_rows, pre, act, mlp_rows, *tables = ins
    grad_ref, above_ref, *outs = outs
    above = table_for(info, tables, 1)
    grad_in, sums = input_grad(grad_resid, da_part, da_received, above_rows, above)
    above_ref[...] = table_of(sums)
    grad = grad_in.astype(bf16)
    grad_ref[...] = grad
    total = mlp_back_body(info, grad, pre, act, mlp_rows, weights, outs)
    outs[4][...] = table_of({UP_B: total})


def last_input_grad(ins, weights, outs):
    info, grad_resid, part, received, rows, out_one, *tables = ins
    grad_in, sums = input_grad(grad_resid, part, received, rows, table_for(info, tables[:2], 0))
    low_core = info[CORE] == 0
    top = out_one[...]
    outs[0][...] = jnp.where(low_core, grad_in, top)
    outs[1][...] = jnp.where(low_core, top, grad_in)
    outs[2][0] = table_of(sums) + tables[2][...] + tables[3][...]
    outs[2][1] = tables[4][...] + tables[5][...] + tables[6][...]


def attention_backward(layer, ins, weights, outs):
    info, grad_out, dc_part, dc_received, resid, proj, prob_in, context, attn_rows, *tables = ins
    if layer == 1:
        *outs, out_ref = outs
        top_part, top_received, *tables = tables
        top = table_for(info, tables, 1)
        out_ref[...] = (
            resid[...] + (top_part[...] + top_received[...].astype(f32)) + row(top, SHIFT_D)
        )
    grad_ref, resid_half_ref, proj_grad_ref, part_ref, sent_ref, cross_ref, sums_ref = outs
    table = table_for(info, tables, layer)
    grad_mlp = dc_part[...] + dc_received[...].astype(f32)
    normed, inv_std = norm_stats(resid[...])
    wide_out = grad_out[...].astype(f32)
    grad_resid = wide_out + norm_back(grad_mlp, normed, inv_std, row(table, GAIN_M))
    grad_ref[...] = grad_resid
    resid_half = grad_resid.astype(bf16)
    resid_half_ref[...] = resid_half
    grad_context = matmul_nt(resid_half, weights[0].ready()[...]).astype(bf16)
    first = head_lanes()
    query_sums = []
    value_sums = []
    for pair in range(HEADS_DEV // 2):
        lanes = slice(pair * PAIR, (pair + 1) * PAIR)
        query, key, value = (proj[c, :, lanes] for c in range(3))
        context_grad = grad_context[:, lanes]
        query_g, key_g, value_g = [], [], []
        for side in range(2):
            mask = first if side == 0 else ~first
            prob = prob_in[2 * pair + side]
            mine = jnp.where(mask, context_grad, jnp.zeros_like(context_grad))
            grad_prob = matmul_nt(mine, value)
            value_g.append(matmul_tn(prob.astype(bf16), context_grad))
            delta = jnp.sum(prob * grad_prob, axis=-1, keepdims=True)
            grad_scores = (prob * (grad_prob - delta) * 0.125).astype(bf16)
            query_g.append(matmul(grad_scores, key))
            key_g.append(matmul_tn(grad_scores, query))
        query_g, key_g, value_g = (
            jnp.where(first, low, high) for low, high in (query_g, key_g, value_g)
        )
        query_sums.append(column_sum(query_g))
        value_sums.append(column_sum(value_g))
        proj_grad_ref[0, :, lanes] = query_g.astype(bf16)
        proj_grad_ref[1, :, lanes] = key_g.astype(bf16)
        proj_grad_ref[2, :, lanes] = value_g.astype(bf16)
    qkv_w = weights[1].ready()
    part = matmul_nt(proj_grad_ref[0], qkv_w[0])
    part = part + matmul_nt(proj_grad_ref[1], qkv_w[1])
    part = part + matmul_nt(proj_grad_ref[2], qkv_w[2])
    part_ref[...] = part
    sent_ref[...] = part.astype(bf16)
    cross_ref[:, :512] = context[...]
    cross_ref[:, 512:1024] = halves(info, resid_half)[1]
    cross_ref[:, 1024:1536] = halves(info, attn_rows[...])[1]
    for c in range(3):
        cross_ref[:, 1536 + c * LOCAL : 1536 + (c + 1) * LOCAL] = proj_grad_ref[c]
    sums_ref[...] = table_of(
        {
            QV: jnp.concatenate(query_sums + value_sums, axis=1),
            GAIN_M: column_sum(grad_mlp * normed),
            SHIFT_O: column_sum(grad_resid),
            SHIFT_M: column_sum(grad_mlp),
            SHIFT_D: column_sum(wide_out),
        }
    )


def stacked(own, far):
    return jnp.concatenate([own, far], axis=0)


def bit_of(info, segment, level):
    return info[BITS + 5 * segment + level]


def split(info, segment, level, block, keep_ref, send_ref):
    half = block.shape[-2] // 2
    low, high = block[..., :half, :], block[..., half:, :]
    own_low = bit_of(info, segment, level) == 0
    keep_ref[...] = jnp.where(own_low, low, high)
    send_ref[...] = jnp.where(own_low, high, low).astype(bf16)


def mlp_weight_grads(ins, weights, outs):
    info, act, grad, mlp_rows, pre_half, crossed = ins
    left = stacked(halves(info, act[...])[0], crossed[:, :512])
    right = stacked(grad[...], crossed[:, 512:1536])
    split(info, 0, 0, matmul_tn(left, right), outs[0], outs[2])
    left = stacked(halves(info, mlp_rows[...])[0], crossed[:, 1536:2048])
    right = stacked(pre_half[...], crossed[:, 2048:])
    split(info, 1, 0, matmul_tn(left, right), outs[1], outs[3])


def attention_weight_grads(ins, weights, outs):
    info, context, resid_half, attn_rows, proj_grad, crossed = ins
    left = stacked(halves(info, attn_rows[...])[0], crossed[:, 1024:1536])
    blocks = []
    for c in range(3):
        far = crossed[:, 1536 + c * LOCAL : 1536 + (c + 1) * LOCAL]
        blocks.append(matmul_tn(left, stacked(proj_grad[c], far)))
    left = stacked(context[...], crossed[:, :512])
    right = stacked(halves(info, resid_half[...])[0], crossed[:, 512:1024])
    blocks.append(matmul_tn(left, right))
    split(info, 2, 0, jnp.concatenate(blocks[:2], axis=1), outs[0], outs[2])
    split(info, 3, 0, jnp.concatenate(blocks[2:], axis=1), outs[1], outs[3])


def two_parts(vector):
    high = vector.astype(bf16)
    low = (vector - high.astype(f32)).astype(bf16)
    return high, low, high.astype(f32) + low.astype(f32)


def join_layers(ins, weights, outs):
    info = ins[0]
    kept = (ins[1:5], ins[5:9])
    received = (ins[9:13], ins[13:17])
    vector, vector_in = ins[17:]
    for segment in range(4):
        for layer in range(2):
            total = kept[layer][segment][...] + received[layer][segment][...].astype(f32)
            sent = outs[5 + segment].at[layer, :128]
            split(info, segment, 1, total, outs[1 + segment].at[layer], sent)
    high, low, outs[0][...] = two_parts(vector[...] + vector_in[...])
    outs[5][:, 128:136] = high
    outs[5][:, 136:] = low


def reduce_level(level, ins, weights, outs):
    info, vector = ins[:2]
    rows = ins[2].shape[1]
    half = rows // 2
    total = vector[...] + (ins[6][:, rows : rows + 8].astype(f32) + ins[6][:, rows + 8 :].astype(f32))
    high, low, outs[0][...] = two_parts(total)
    for segment in range(4):
        total = ins[2 + segment][...] + ins[6 + segment][:, :rows].astype(f32)
        if level < 4:
            split(info, segment, level, total, outs[1 + segment], outs[5 + segment].at[:, :half])
        else:
            place = slice(2 * segment, 2 * segment + 2)
            split(info, segment, level, total, outs[1].at[place], outs[2].at[place])
    if level < 4:
        outs[5][:, half : half + 8] = high
        outs[5][:, half + 8 :] = low
    else:
        outs[2][8:, :8] = high
        outs[2][8:, 8:] = low


def reduce_last(ins, weights, outs):
    info, vector, kept, received = ins
    low_core = info[CORE] == 0
    for segment in range(4):
        place = slice(2 * segment, 2 * segment + 2)
        total = (kept[place] + received[place].astype(f32)).astype(bf16)
        outs[1][segment] = jnp.where(low_core, total[0], total[1])
        outs[2][segment] = jnp.where(low_core, total[1], total[0])
    total = vector[...] + (received[8:, :8].astype(f32) + received[8:, 8:].astype(f32))
    outs[0][...] = jnp.where(low_core, total[0], total[1])
    high, low, _ = two_parts(jnp.where(low_core, total[1], total[0]))
    outs[2][4, :8] = high
    outs[2][4, 8:] = low


def gather_start(ins, weights, outs):
    info, vector, own, far = ins
    low_core = info[CORE] == 0
    outs[0][...] = vector[...] + (far[4, :8].astype(f32) + far[4, 8:].astype(f32))
    for segment in range(4):
        outs[1][2 * segment] = jnp.where(low_core, own[segment], far[segment])
        outs[1][2 * segment + 1] = jnp.where(low_core, far[segment], own[segment])


def gather_first(ins, weights, outs):
    info, mine, theirs = ins
    for segment in range(4):
        place = slice(2 * segment, 2 * segment + 2)
        own, far = mine[place], theirs[place]
        own_low = bit_of(info, segment, 4) == 0
        outs[segment][:, :16] = jnp.where(own_low, own, far)
        outs[segment][:, 16:] = jnp.where(own_low, far, own)


def gather_level(level, ins, weights, outs):
    info = ins[0]
    for segment in range(4):
        own, far = ins[1 + segment][...], ins[5 + segment][...]
        half = own.shape[1]
        own_low = bit_of(info, segment, level) == 0
        outs[segment][:, :half] = jnp.where(own_low, own, far)
        outs[segment][:, half:] = jnp.where(own_low, far, own)


STAGED = False
LIMIT_STAGED = 63
LIMIT_HELD = 24


class Loaded:
    def __init__(self, source, buffer, semaphore):
        self.copy = pltpu.make_async_copy(source, buffer, semaphore)
        self.copy.start()
        self.buffer = buffer
        self.waiting = True

    def ready(self):
        if self.waiting:
            self.waiting = False
            self.copy.wait()
        return self.buffer

    def __getitem__(self, place):
        return self.ready()[place]

    @property
    def shape(self):
        return self.buffer.shape


class Fetched(Loaded):
    def __init__(self, info, layer, own, far, buffer, semaphore):
        self.copy = pltpu.make_async_copy(own, buffer, semaphore)
        other = pltpu.make_async_copy(far, buffer, semaphore)
        pl.when(info[CORE] == layer)(self.copy.start)
        pl.when(info[CORE] != layer)(other.start)
        self.buffer = buffer
        self.waiting = True


def device_kernel(body, name, scalars, shapes, layer=0, staged=STAGED):
    def call(*operands, weights=()):
        arrays = operands[scalars:]
        flat = [array for pair in weights for array in pair]
        count, total, results = len(arrays), len(weights), len(shapes)

        def kernel(*refs):
            ins, refs = refs[: scalars + count], refs[scalars + count :]
            pairs, refs = refs[: 2 * total], refs[2 * total :]
            outs, rest = refs[:results], refs[results:]
            fetched = [
                Fetched(ins[0], layer, pairs[2 * i], pairs[2 * i + 1], rest[i], rest[total + i])
                for i in range(total)
            ]
            body(ins, fetched, outs)

        def whole(shape):
            zeros = (0,) * len(shape)
            if staged:
                return pl.BlockSpec(shape, lambda i: zeros)
            return pl.BlockSpec(memory_space=pltpu.VMEM)

        smem = pl.BlockSpec(memory_space=pltpu.SMEM)
        hbm = pl.BlockSpec(memory_space=pl.ANY)
        return pl.pallas_call(
            kernel,
            name=name,
            grid=(1,) if staged else (),
            in_specs=[smem] * scalars + [whole(array.shape) for array in arrays] + [hbm] * len(flat),
            out_specs=[whole(shape) for shape, _ in shapes],
            out_shape=[jax.ShapeDtypeStruct(shape, dtype) for shape, dtype in shapes],
            scratch_shapes=[pltpu.VMEM(own.shape, own.dtype) for own, _ in weights]
            + [pltpu.SemaphoreType.DMA(())] * total,
            compiler_params=pltpu.CompilerParams(
                vmem_limit_bytes=(LIMIT_STAGED if staged else LIMIT_HELD) * 1024 * 1024
            ),
        )(*operands, *flat)

    return call


def assemble(info, blocks, far, results=()):
    def kernel(info, *refs):
        sources, refs = refs[:4], refs[4 + len(results) :]
        qkv_ref, out_ref, up_ref, down_ref = refs[:4]
        buffers, wide, semaphores = refs[4:8], refs[8], refs[9:]
        loaded = [Loaded(sources[i], buffers[i], semaphores[i]) for i in range(4)]
        copies = []

        def send(source, target):
            copies.append(pltpu.make_async_copy(source, target, semaphores[4 + len(copies)]))
            copies[-1].start()

        for segment in range(4):
            bit = bit_of(info, segment, 0) ^ far
            for half in range(2):
                wide[segment, half] = loaded[segment][half].astype(f32)
                block = wide.at[segment, half]
                rows = pl.ds(pl.multiple_of(half * 512 + bit * 256, 256), 256)
                left, right = block.at[:, :512], block.at[:, 512:]
                if segment == 0:
                    send(block, down_ref.at[rows, :])
                if segment == 1:
                    send(block, up_ref.at[rows, :])
                if segment == 2:
                    send(left, qkv_ref.at[0, rows, :])
                    send(right, qkv_ref.at[1, rows, :])
                if segment == 3:
                    send(left, qkv_ref.at[2, rows, :])
                    short = pl.ds(pl.multiple_of(bit * 256, 256), 256)
                    send(right, out_ref.at[short, half * 512 : (half + 1) * 512])
        for copy in copies:
            copy.wait()

    hbm = pl.BlockSpec(memory_space=pl.ANY)
    return pl.pallas_call(
        kernel,
        name="assemble",
        in_specs=[pl.BlockSpec(memory_space=pltpu.SMEM)] + [hbm] * (4 + len(results)),
        out_specs=[hbm] * 4,
        out_shape=[
            jax.ShapeDtypeStruct((3, 1024, 512), f32),
            jax.ShapeDtypeStruct((512, 1024), f32),
            jax.ShapeDtypeStruct((1024, 1024), f32),
            jax.ShapeDtypeStruct((1024, 1024), f32),
        ],
        scratch_shapes=[pltpu.VMEM((2, 256, WIDTH), bf16)] * 4
        + [pltpu.VMEM((4, 2, 256, WIDTH), f32)]
        + [pltpu.SemaphoreType.DMA(())] * 16,
        input_output_aliases={5 + i: i for i in range(len(results))},
        compiler_params=pltpu.CompilerParams(vmem_limit_bytes=32 * 1024 * 1024),
    )(info, *blocks, *results)


ROWS = (LEN, WIDTH)
TABLE = ((8, WIDTH), f32)
BOTH_TABLES = ((2, 8, WIDTH), f32)
ATTENTION_OUT = (
    (ROWS, bf16),
    (ROWS, bf16),
    ((3, LEN, LOCAL), bf16),
    ((HEADS_DEV, LEN, LEN), f32),
    ((LEN, LOCAL), bf16),
    (ROWS, f32),
    (ROWS, bf16),
)
MLP_OUT = ((ROWS, f32), (ROWS, bf16), (ROWS, f32), (ROWS, bf16), (ROWS, f32), (ROWS, bf16))
MLP_BACK_OUT = ((ROWS, bf16), (ROWS, f32), (ROWS, bf16), ((LEN, 3072), bf16), TABLE)
ATTENTION_BACK_OUT = (
    (ROWS, f32),
    (ROWS, bf16),
    ((3, LEN, LOCAL), bf16),
    (ROWS, f32),
    (ROWS, bf16),
    ((LEN, 3072), bf16),
    TABLE,
)
MAKE_TABLE = device_kernel(make_table, "make_table", 0, (TABLE,))
FIRST_ATTENTION = device_kernel(first_attention, "first_attention", 2, ATTENTION_OUT, 0)
NEXT_ATTENTION = device_kernel(next_attention, "next_attention", 2, ATTENTION_OUT, 1)
MLP_FORWARD = tuple(
    device_kernel(functools.partial(mlp_forward, layer), "mlp_forward", 1, MLP_OUT, layer)
    for layer in range(2)
)
MLP_BACKWARD = device_kernel(
    mlp_backward, "mlp_backward", 1, ((ROWS, bf16),) + MLP_BACK_OUT, 1
)
MLP_BACKWARD_BELOW = device_kernel(
    mlp_backward_below, "mlp_backward_below", 1, ((ROWS, bf16), TABLE) + MLP_BACK_OUT, 0
)
ATTENTION_BACKWARD = tuple(
    device_kernel(
        functools.partial(attention_backward, layer),
        "attention_backward",
        1,
        ATTENTION_BACK_OUT + ((ROWS, f32),) * layer,
        layer,
    )
    for layer in range(2)
)
LAST_INPUT_GRAD = device_kernel(last_input_grad, "last_input_grad", 1, ((ROWS, f32), (ROWS, f32), BOTH_TABLES))
FIRST_HALVES = (((256, WIDTH), f32),) * 2 + (((256, WIDTH), bf16),) * 2
MLP_WEIGHT_GRADS = device_kernel(mlp_weight_grads, "mlp_weight_grads", 1, FIRST_HALVES)
ATTENTION_WEIGHT_GRADS = device_kernel(
    attention_weight_grads, "attention_weight_grads", 1, FIRST_HALVES
)


def blocks(rows, dtype):
    return (((2, rows, WIDTH), dtype),) * 4


def sent_blocks(rows):
    return (((2, rows + 16, WIDTH), bf16),) + (((2, rows, WIDTH), bf16),) * 3


JOIN_LAYERS = device_kernel(
    join_layers, "join_layers", 1, (BOTH_TABLES,) + blocks(128, f32) + sent_blocks(128)
)
REDUCE_LEVEL = {
    level: device_kernel(
        functools.partial(reduce_level, level),
        "reduce_level",
        1,
        (BOTH_TABLES,) + blocks(256 >> level, f32) + sent_blocks(256 >> level)
        if level < 4
        else (BOTH_TABLES, ((8, 16, WIDTH), f32), ((10, 16, WIDTH), bf16)),
    )
    for level in (2, 3, 4)
}
REDUCE_LAST = device_kernel(
    reduce_last, "reduce_last", 1, (TABLE, ((4, 16, WIDTH), bf16), ((5, 16, WIDTH), bf16))
)
GATHER_START = device_kernel(gather_start, "gather_start", 1, (TABLE, ((8, 16, WIDTH), bf16)))
GATHER_FIRST = device_kernel(gather_first, "gather_first", 1, blocks(32, bf16))
GATHER_LEVEL = {
    level: device_kernel(
        functools.partial(gather_level, level), "gather_level", 1, blocks(512 >> level, bf16)
    )
    for level in (3, 2, 1)
}


def step_bit(axis, pairs):
    index = lax.axis_index(axis)
    if pairs is PAIR_E:
        return (index ^ (index >> 1)) & 1
    if pairs is PAIR_F:
        return (index >> 1) & 1
    return index


def local(
    section_in,
    lengths,
    qkv_weight,
    qv_bias,
    out_weight,
    up_weight,
    up_bias,
    down_weight,
    norm_gains,
    row_biases,
):
    core = lax.axis_index("pipe")
    tensor_index = lax.axis_index("tensor")
    place = core * 2 + tensor_index
    both = ("pipe", "tensor")

    own_rows = section_in[0, 0, 0]
    near = lax.ppermute(own_rows, both, ((0, 1), (1, 2)))
    far = lax.ppermute(own_rows, both, ((1, 3),))

    (table,) = MAKE_TABLE(qv_bias[0], up_bias, norm_gains[0], row_biases[0])
    first_far = [lax.ppermute(array, "pipe", SWAP) for array in (qkv_weight[0], out_weight[0], table)]
    up_own, down_own, near, far, *first_far = lax.optimization_barrier(
        (up_weight[0], down_weight[0], near, far, *first_far)
    )
    second_far = [lax.ppermute(array, "pipe", SWAP) for array in (up_own, down_own)]
    table_far = first_far[2]
    qkv_w = (qkv_weight[0], first_far[0])
    out_w = (out_weight[0], first_far[1])
    up_w = (up_weight[0], second_far[0])
    down_w = (down_weight[0], second_far[1])
    tables = (table, table_far)

    bits = [step_bit(axis, pairs) for route in ROUTES for axis, pairs in route]
    info = jnp.stack([core, tensor_index] + bits).astype(jnp.int32)

    def swapped(sent):
        return lax.ppermute(sent, "tensor", SWAP)

    def crossed(sent):
        return lax.ppermute(sent, "pipe", SWAP)

    rows_0, attn_0, proj_0, prob_0, context_0, part, sent = FIRST_ATTENTION(
        info, lengths, own_rows, near, far, *tables, weights=(qkv_w, out_w)
    )
    received, cot_own = lax.optimization_barrier((swapped(sent), own_rows))
    cot_near = lax.ppermute(cot_own, both, ((2, 0), (3, 2)))
    cot_far = lax.ppermute(cot_own, both, ((2, 1),))
    resid_0, mlp_0, pre_0, act_0, part, sent = MLP_FORWARD[0](
        info, rows_0, part, received, *tables, weights=(up_w, down_w)
    )
    rows_1, attn_1, proj_1, prob_1, context_1, part, sent = NEXT_ATTENTION(
        info, lengths, resid_0, part, swapped(sent), *tables, weights=(qkv_w, out_w)
    )
    resid_1, mlp_1, pre_1, act_1, top_part, top_sent = MLP_FORWARD[1](
        info, rows_1, part, swapped(sent), *tables, weights=(up_w, down_w)
    )

    cotangent, pre_half_1, part, sent, cross_mlp, sums_mlp_1 = MLP_BACKWARD(
        info, own_rows, cot_near, cot_far, pre_1, act_1, mlp_1, weights=(down_w, up_w)
    )
    early_1 = MLP_WEIGHT_GRADS(info, act_1, cotangent, mlp_1, pre_half_1, crossed(cross_mlp))
    received, *early_1 = lax.optimization_barrier((swapped(sent), *early_1))
    *back_1, out_one = ATTENTION_BACKWARD[1](
        info, cotangent, part, received, resid_1, proj_1, prob_1, context_1, attn_1,
        top_part, swapped(top_sent), *tables, weights=(out_w, qkv_w),
    )
    grad_1, resid_half_1, proj_grad_1, part, sent, cross_attn, sums_attn_1 = back_1
    late_1 = ATTENTION_WEIGHT_GRADS(
        info, context_1, resid_half_1, attn_1, proj_grad_1, crossed(cross_attn)
    )
    received, *late_1 = lax.optimization_barrier((swapped(sent), *late_1))
    grad_half, sums_in_1, pre_half_0, part, sent, cross_mlp, sums_mlp_0 = MLP_BACKWARD_BELOW(
        info, grad_1, part, received, rows_1, pre_0, act_0, mlp_0, *tables,
        weights=(down_w, up_w),
    )
    early_0 = MLP_WEIGHT_GRADS(info, act_0, grad_half, mlp_0, pre_half_0, crossed(cross_mlp))
    received, *early_0 = lax.optimization_barrier((swapped(sent), *early_0))
    grad_0, resid_half_0, proj_grad_0, part, sent, cross_attn, sums_attn_0 = ATTENTION_BACKWARD[0](
        info, grad_half, part, received, resid_0, proj_0, prob_0, context_0, attn_0, *tables,
        weights=(out_w, qkv_w),
    )
    late_0 = ATTENTION_WEIGHT_GRADS(
        info, context_0, resid_half_0, attn_0, proj_grad_0, crossed(cross_attn)
    )
    received, *late_0 = lax.optimization_barrier((swapped(sent), *late_0))

    def half_steps(arrays, level):
        arrays = lax.optimization_barrier(tuple(arrays))
        return [
            lax.ppermute(array, *route[level]) for array, route in zip(arrays, ROUTES)
        ]

    kept_1 = (*early_1[:2], *late_1[:2])
    kept_0 = (*early_0[:2], *late_0[:2])
    received_1 = half_steps((*early_1[2:], *late_1[2:]), 0)
    received_0 = half_steps((*early_0[2:], *late_0[2:]), 0)

    kept_rows, crossing, vectors = LAST_INPUT_GRAD(
        info, grad_0, part, received, rows_0, out_one, *tables,
        sums_mlp_0, sums_attn_0, sums_in_1, sums_mlp_1, sums_attn_1,
    )
    vectors_in = lax.ppermute(vectors, *ROUTES[0][0])
    vectors, *stepped = JOIN_LAYERS(
        info, *kept_0, *kept_1, *received_0, *received_1, vectors, vectors_in
    )
    for level in (1, 2, 3):
        kept, sent = stepped[:4], stepped[4:]
        arrived = lax.optimization_barrier(half_steps(sent, level))
        vectors, *stepped = REDUCE_LEVEL[level + 1](info, vectors, *kept, *arrived)
    kept, sent = stepped
    vectors, own, far = REDUCE_LAST(info, vectors, kept, lax.ppermute(sent, "xh", SWAP))
    vectors, held = GATHER_START(info, vectors, own, crossed(far))
    shared = vectors[GAIN_A:]
    shared = 0.5 * (shared + swapped(shared))
    held = GATHER_FIRST(info, held, lax.ppermute(held, "xh", SWAP))
    for level in (3, 2, 1):
        arrived = lax.optimization_barrier(half_steps(held, level))
        held = GATHER_LEVEL[level](info, *held, *arrived)
    arrived = lax.optimization_barrier(half_steps(held, 0))
    results = assemble(info, held, 0)
    qkv_g, out_g, up_g, down_g = assemble(info, arrived, 1, results)

    crossing = lax.ppermute(crossing, both, ((0, 2), (3, 1)))
    section_out = jnp.where(core == tensor_index, kept_rows, crossing)
    return (
        section_out[None, None, None],
        qkv_g[None],
        vectors[0].reshape(1, 2, 512),
        out_g[None],
        up_g[None],
        vectors[1][None],
        down_g[None],
        shared[:2][None],
        shared[2:][None],
    )


def solution(mesh):
    fine = Mesh(mesh.devices.reshape(2, 2, 4, 4, 2), ("pipe", "tensor", "y", "z", "xh"))
    dp = ("y", "z", "xh")
    in_specs = (
        P("pipe", dp, "tensor", None, None),
        P(dp, None),
        P("pipe", None, None, "tensor"),
        P("pipe", None, "tensor"),
        P("pipe", "tensor", None),
        P("pipe", None, "tensor"),
        P("pipe", "tensor"),
        P("pipe", "tensor", None),
        P("pipe", None, None),
        P("pipe", None, None),
    )
    out_specs = (
        P("pipe", dp, "tensor", None, None),
        P("pipe", None, None, "tensor"),
        P("pipe", None, "tensor"),
        P("pipe", "tensor", None),
        P("pipe", None, "tensor"),
        P("pipe", "tensor"),
        P("pipe", "tensor", None),
        P("pipe", None, None),
        P("pipe", None, None),
    )
    return jax.shard_map(local, mesh=fine, in_specs=in_specs, out_specs=out_specs, check_vma=False)
```

```python
import functools

import jax
import jax.numpy as jnp
from jax import lax
from jax.experimental import pallas as pl
from jax.experimental.pallas import tpu as pltpu
from jax.sharding import Mesh
from jax.sharding import PartitionSpec as P

HEADS = 16
HD = 64
LEN = 128
norm_eps = 1e-05

f32 = jnp.float32
bf16 = jnp.bfloat16

SWAP = ((0, 1), (1, 0))
PAIR_E = ((0, 1), (1, 0), (2, 3), (3, 2))
PAIR_F = ((0, 3), (3, 0), (1, 2), (2, 1))
DP = ("y", "z", "xh")
ROUTES = (
    (("y", PAIR_E), ("y", PAIR_F), ("z", PAIR_E), ("z", PAIR_F), ("xh", SWAP)),
    (("y", PAIR_F), ("y", PAIR_E), ("z", PAIR_F), ("z", PAIR_E), ("xh", SWAP)),
    (("z", PAIR_E), ("z", PAIR_F), ("y", PAIR_E), ("y", PAIR_F), ("xh", SWAP)),
    (("z", PAIR_F), ("z", PAIR_E), ("y", PAIR_F), ("y", PAIR_E), ("xh", SWAP)),
)
CORE, TENSOR, BITS = 0, 1, 2


GELU_A = 0.7978845608028654
GELU_B = 0.044715
WIDTH = 1024
HEADS_DEV = HEADS // 2
LOCAL = HEADS_DEV * HD
PAIR = 2 * HD


def matmul(left, right):
    return jnp.dot(left, right, preferred_element_type=f32)


def matmul_nt(left, right):
    return lax.dot_general(left, right, (((1,), (1,)), ((), ())), preferred_element_type=f32)


def matmul_tn(left, right):
    return lax.dot_general(left, right, (((0,), (0,)), ((), ())), preferred_element_type=f32)


def norm_stats(values):
    centred = values - jnp.mean(values, axis=-1, keepdims=True)
    inv_std = lax.rsqrt(jnp.mean(centred * centred, axis=-1, keepdims=True) + norm_eps)
    return centred * inv_std, inv_std


def norm_back(grad_norm, normed, inv_std, gain):
    scaled = grad_norm * gain
    return inv_std * (
        scaled
        - jnp.mean(scaled, axis=-1, keepdims=True)
        - normed * jnp.mean(scaled * normed, axis=-1, keepdims=True)
    )


QV, UP_B, GAIN_A, GAIN_M, SHIFT_A, SHIFT_O, SHIFT_M, SHIFT_D = range(8)


def row(table, index):
    return table[index : index + 1, :]


def table_of(rows):
    zero = jnp.zeros((1, WIDTH), f32)
    return jnp.concatenate([rows.get(index, zero) for index in range(8)], axis=0)


def column_sum(block):
    return jnp.sum(block, axis=0, keepdims=True)


def head_lanes():
    return lax.broadcasted_iota(jnp.int32, (LEN, PAIR), 1) < HD


def attention_rows(rows, table, info, lengths, weights, outs):
    attn_rows_ref, proj_ref, prob_ref, context_ref, part_ref, sent_ref = outs
    normed, _ = norm_stats(rows.astype(f32))
    attn_rows = (normed * row(table, GAIN_A) + row(table, SHIFT_A)).astype(bf16)
    attn_rows_ref[...] = attn_rows
    qkv_w = weights[0].ready()
    for c in range(3):
        block = matmul(attn_rows, qkv_w[c])
        if c == 0:
            block = block + table[QV : QV + 1, :LOCAL]
        if c == 2:
            block = block + table[QV : QV + 1, LOCAL:]
        proj_ref[c] = block.astype(bf16)
    spot_i = lax.broadcasted_iota(jnp.int32, (LEN, LEN), 0)
    spot_j = lax.broadcasted_iota(jnp.int32, (LEN, LEN), 1)
    allowed = (spot_j <= spot_i) & (spot_j < jnp.where(info[CORE] == 0, lengths[0, 0], lengths[0, 1]))
    offsets = (spot_i - spot_j).astype(f32)
    first = head_lanes()
    for pair in range(HEADS_DEV // 2):
        lanes = slice(pair * PAIR, (pair + 1) * PAIR)
        query, key, value = (proj_ref[c, :, lanes] for c in range(3))
        found = []
        for side in range(2):
            head = 2 * pair + side
            mine = jnp.where(first if side == 0 else ~first, query, jnp.zeros_like(query))
            slope = jnp.where(
                info[TENSOR] == 0,
                2.0 ** (-8.0 * (head + 1) / HEADS),
                2.0 ** (-8.0 * (head + HEADS_DEV + 1) / HEADS),
            )
            scores = matmul_nt(mine, key) * 0.125 - slope * offsets
            scores = jnp.where(allowed, scores, -jnp.inf)
            top_score = jnp.max(scores, axis=-1, keepdims=True)
            exp_scores = jnp.exp(scores - top_score)
            prob = exp_scores / jnp.sum(exp_scores, axis=-1, keepdims=True)
            prob_ref[head] = prob
            found.append(matmul(prob.astype(bf16), value))
        context_ref[:, lanes] = jnp.where(first, found[0], found[1]).astype(bf16)
    part = matmul(context_ref[...], weights[1].ready()[...])
    part_ref[...] = part
    sent_ref[...] = part.astype(bf16)


def make_table(ins, weights, outs):
    qv_b, up_b, gains, shifts = ins
    outs[0][QV : QV + 1, :LOCAL] = qv_b[0:1, :].astype(f32)
    outs[0][QV : QV + 1, LOCAL:] = qv_b[1:2, :].astype(f32)
    outs[0][UP_B : UP_B + 1, :] = up_b[...].astype(f32)
    outs[0][GAIN_A : SHIFT_A, :] = gains[...]
    outs[0][SHIFT_A:, :] = shifts[...]


def table_for(info, tables, layer):
    own, far = tables
    return jnp.where(info[CORE] == layer, own[...], far[...])


def first_attention(ins, weights, outs):
    info, lengths, own_rows, near, far, *tables = ins
    rows_ref, *outs = outs
    place = 2 * info[CORE] + info[TENSOR]
    rows = jnp.where(place == 0, own_rows[...], jnp.where(place == 3, far[...], near[...]))
    rows_ref[...] = rows
    attention_rows(rows, table_for(info, tables, 0), info, lengths, weights, outs)


def next_attention(ins, weights, outs):
    info, lengths, resid, part, received, *tables = ins
    rows_ref, *outs = outs
    below = table_for(info, tables, 0)
    layer_out = resid[...] + (part[...] + received[...].astype(f32)) + row(below, SHIFT_D)
    rows = layer_out.astype(bf16)
    rows_ref[...] = rows
    attention_rows(rows, table_for(info, tables, 1), info, lengths, weights, outs)


def mlp_forward(layer, ins, weights, outs):
    info, rows, part, received, *tables = ins
    resid_ref, mlp_ref, pre_ref, act_ref, out_ref, sent_ref = outs
    table = table_for(info, tables, layer)
    resid = (
        rows[...].astype(f32) + (part[...] + received[...].astype(f32)) + row(table, SHIFT_O)
    )
    resid_ref[...] = resid
    normed, _ = norm_stats(resid)
    mlp_rows = (normed * row(table, GAIN_M) + row(table, SHIFT_M)).astype(bf16)
    mlp_ref[...] = mlp_rows
    pre = matmul(mlp_rows, weights[0].ready()[...]) + row(table, UP_B)
    pre_ref[...] = pre
    act = (0.5 * pre * (1.0 + jnp.tanh(GELU_A * (pre + GELU_B * pre * pre * pre)))).astype(bf16)
    act_ref[...] = act
    out = matmul(act, weights[1].ready()[...])
    out_ref[...] = out
    sent_ref[...] = out.astype(bf16)


def halves(core, block):
    half = block.shape[1] // 2
    low, high = block[:, :half], block[:, half:]
    own = core[CORE] == 0
    return jnp.where(own, low, high), jnp.where(own, high, low)


def mlp_back_body(info, grad, pre_in, act, mlp_rows, weights, outs):
    pre_half_ref, part_ref, sent_ref, cross_ref, sums_ref = outs
    grad_act = matmul_nt(grad, weights[0].ready()[...])
    pre = pre_in[...]
    tanh = jnp.tanh(GELU_A * (pre + GELU_B * pre * pre * pre))
    slope = 0.5 * (1.0 + tanh) + 0.5 * pre * (1.0 - tanh * tanh) * (
        GELU_A * (1.0 + 3.0 * GELU_B * pre * pre)
    )
    grad_pre = grad_act * slope
    pre_half = grad_pre.astype(bf16)
    pre_half_ref[...] = pre_half
    part = matmul_nt(pre_half, weights[1].ready()[...])
    part_ref[...] = part
    sent_ref[...] = part.astype(bf16)
    cross_ref[:, :512] = halves(info, act[...])[1]
    cross_ref[:, 512:1536] = grad
    cross_ref[:, 1536:2048] = halves(info, mlp_rows[...])[1]
    cross_ref[:, 2048:] = pre_half
    return column_sum(grad_pre)


def mlp_backward(ins, weights, outs):
    info, cot_own, cot_near, cot_far, pre, act, mlp_rows = ins
    grad_ref, *outs = outs
    place = 2 * info[CORE] + info[TENSOR]
    grad = jnp.where(place == 3, cot_own[...], jnp.where(place == 1, cot_far[...], cot_near[...]))
    grad_ref[...] = grad
    total = mlp_back_body(info, grad, pre, act, mlp_rows, weights, outs)
    outs[4][...] = table_of({UP_B: total})


def input_grad(grad_resid, part, received, rows, table):
    grad_attn = part[...] + received[...].astype(f32)
    normed, inv_std = norm_stats(rows[...].astype(f32))
    grad_in = grad_resid[...] + norm_back(grad_attn, normed, inv_std, row(table, GAIN_A))
    sums = {GAIN_A: column_sum(grad_attn * normed), SHIFT_A: column_sum(grad_attn)}
    return grad_in, sums


def mlp_backward_below(ins, weights, outs):
    info, grad_resid, da_part, da_received, above_rows, pre, act, mlp_rows, *tables = ins
    grad_ref, above_ref, *outs = outs
    above = table_for(info, tables, 1)
    grad_in, sums = input_grad(grad_resid, da_part, da_received, above_rows, above)
    above_ref[...] = table_of(sums)
    grad = grad_in.astype(bf16)
    grad_ref[...] = grad
    total = mlp_back_body(info, grad, pre, act, mlp_rows, weights, outs)
    outs[4][...] = table_of({UP_B: total})


def last_input_grad(ins, weights, outs):
    info, grad_resid, part, received, rows, *tables = ins
    grad_in, sums = input_grad(grad_resid, part, received, rows, table_for(info, tables[:2], 0))
    outs[0][...] = grad_in
    outs[1][0] = table_of(sums) + tables[2][...] + tables[3][...]
    outs[1][1] = tables[4][...] + tables[5][...] + tables[6][...]


def finish_rows(ins, weights, outs):
    info, grad_zero, resid, part, received, *tables = ins
    top = resid[...] + (part[...] + received[...].astype(f32))
    top = top + row(table_for(info, tables, 1), SHIFT_D)
    low_core = info[CORE] == 0
    outs[0][...] = jnp.where(low_core, grad_zero[...], top)
    outs[1][...] = jnp.where(low_core, top, grad_zero[...])


def attention_backward(layer, ins, weights, outs):
    info, grad_out, dc_part, dc_received, resid, proj, prob_in, context, attn_rows, *tables = ins
    grad_ref, resid_half_ref, proj_grad_ref, part_ref, sent_ref, cross_ref, sums_ref = outs
    table = table_for(info, tables, layer)
    grad_mlp = dc_part[...] + dc_received[...].astype(f32)
    normed, inv_std = norm_stats(resid[...])
    wide_out = grad_out[...].astype(f32)
    grad_resid = wide_out + norm_back(grad_mlp, normed, inv_std, row(table, GAIN_M))
    grad_ref[...] = grad_resid
    resid_half = grad_resid.astype(bf16)
    resid_half_ref[...] = resid_half
    grad_context = matmul_nt(resid_half, weights[0].ready()[...]).astype(bf16)
    first = head_lanes()
    query_sums = []
    value_sums = []
    for pair in range(HEADS_DEV // 2):
        lanes = slice(pair * PAIR, (pair + 1) * PAIR)
        query, key, value = (proj[c, :, lanes] for c in range(3))
        context_grad = grad_context[:, lanes]
        query_g, key_g, value_g = [], [], []
        for side in range(2):
            mask = first if side == 0 else ~first
            prob = prob_in[2 * pair + side]
            mine = jnp.where(mask, context_grad, jnp.zeros_like(context_grad))
            grad_prob = matmul_nt(mine, value)
            value_g.append(matmul_tn(prob.astype(bf16), context_grad))
            delta = jnp.sum(prob * grad_prob, axis=-1, keepdims=True)
            grad_scores = (prob * (grad_prob - delta) * 0.125).astype(bf16)
            query_g.append(matmul(grad_scores, key))
            key_g.append(matmul_tn(grad_scores, query))
        query_g, key_g, value_g = (
            jnp.where(first, low, high) for low, high in (query_g, key_g, value_g)
        )
        query_sums.append(column_sum(query_g))
        value_sums.append(column_sum(value_g))
        proj_grad_ref[0, :, lanes] = query_g.astype(bf16)
        proj_grad_ref[1, :, lanes] = key_g.astype(bf16)
        proj_grad_ref[2, :, lanes] = value_g.astype(bf16)
    qkv_w = weights[1].ready()
    part = matmul_nt(proj_grad_ref[0], qkv_w[0])
    part = part + matmul_nt(proj_grad_ref[1], qkv_w[1])
    part = part + matmul_nt(proj_grad_ref[2], qkv_w[2])
    part_ref[...] = part
    sent_ref[...] = part.astype(bf16)
    cross_ref[:, :512] = context[...]
    cross_ref[:, 512:1024] = halves(info, resid_half)[1]
    cross_ref[:, 1024:1536] = halves(info, attn_rows[...])[1]
    for c in range(3):
        cross_ref[:, 1536 + c * LOCAL : 1536 + (c + 1) * LOCAL] = proj_grad_ref[c]
    sums_ref[...] = table_of(
        {
            QV: jnp.concatenate(query_sums + value_sums, axis=1),
            GAIN_M: column_sum(grad_mlp * normed),
            SHIFT_O: column_sum(grad_resid),
            SHIFT_M: column_sum(grad_mlp),
            SHIFT_D: column_sum(wide_out),
        }
    )


def stacked(own, far):
    return jnp.concatenate([own, far], axis=0)


def bit_of(info, segment, level):
    return info[BITS + 5 * segment + level]


def split(info, segment, level, block, keep_ref, send_ref):
    half = block.shape[-2] // 2
    low, high = block[..., :half, :], block[..., half:, :]
    own_low = bit_of(info, segment, level) == 0
    keep_ref[...] = jnp.where(own_low, low, high)
    send_ref[...] = jnp.where(own_low, high, low).astype(bf16)


def mlp_weight_grads(ins, weights, outs):
    info, act, grad, mlp_rows, pre_half, crossed = ins
    left = stacked(halves(info, act[...])[0], crossed[:, :512])
    right = stacked(grad[...], crossed[:, 512:1536])
    split(info, 0, 0, matmul_tn(left, right), outs[0], outs[2])
    left = stacked(halves(info, mlp_rows[...])[0], crossed[:, 1536:2048])
    right = stacked(pre_half[...], crossed[:, 2048:])
    split(info, 1, 0, matmul_tn(left, right), outs[1], outs[3])


def attention_weight_grads(ins, weights, outs):
    info, context, resid_half, attn_rows, proj_grad, crossed = ins
    left = stacked(halves(info, attn_rows[...])[0], crossed[:, 1024:1536])
    blocks = []
    for c in range(3):
        far = crossed[:, 1536 + c * LOCAL : 1536 + (c + 1) * LOCAL]
        blocks.append(matmul_tn(left, stacked(proj_grad[c], far)))
    left = stacked(context[...], crossed[:, :512])
    right = stacked(halves(info, resid_half[...])[0], crossed[:, 512:1024])
    blocks.append(matmul_tn(left, right))
    split(info, 2, 0, jnp.concatenate(blocks[:2], axis=1), outs[0], outs[2])
    split(info, 3, 0, jnp.concatenate(blocks[2:], axis=1), outs[1], outs[3])


def two_parts(vector):
    high = vector.astype(bf16)
    low = (vector - high.astype(f32)).astype(bf16)
    return high, low, high.astype(f32) + low.astype(f32)


def join_layers(ins, weights, outs):
    info = ins[0]
    kept = (ins[1:5], ins[5:9])
    received = (ins[9:13], ins[13:17])
    vector, vector_in = ins[17:]
    for segment in range(4):
        for layer in range(2):
            total = kept[layer][segment][...] + received[layer][segment][...].astype(f32)
            sent = outs[5 + segment].at[layer, :128]
            split(info, segment, 1, total, outs[1 + segment].at[layer], sent)
    high, low, outs[0][...] = two_parts(vector[...] + vector_in[...])
    outs[5][:, 128:136] = high
    outs[5][:, 136:] = low


def reduce_level(level, ins, weights, outs):
    info, vector = ins[:2]
    rows = ins[2].shape[1]
    half = rows // 2
    total = vector[...] + (ins[6][:, rows : rows + 8].astype(f32) + ins[6][:, rows + 8 :].astype(f32))
    high, low, outs[0][...] = two_parts(total)
    for segment in range(4):
        total = ins[2 + segment][...] + ins[6 + segment][:, :rows].astype(f32)
        if level < 4:
            split(info, segment, level, total, outs[1 + segment], outs[5 + segment].at[:, :half])
        else:
            place = slice(2 * segment, 2 * segment + 2)
            split(info, segment, level, total, outs[1].at[place], outs[2].at[place])
    if level < 4:
        outs[5][:, half : half + 8] = high
        outs[5][:, half + 8 :] = low
    else:
        outs[2][8:, :8] = high
        outs[2][8:, 8:] = low


def reduce_last(ins, weights, outs):
    info, vector, kept, received = ins
    low_core = info[CORE] == 0
    for segment in range(4):
        place = slice(2 * segment, 2 * segment + 2)
        total = (kept[place] + received[place].astype(f32)).astype(bf16)
        outs[1][segment] = jnp.where(low_core, total[0], total[1])
        outs[2][segment] = jnp.where(low_core, total[1], total[0])
    total = vector[...] + (received[8:, :8].astype(f32) + received[8:, 8:].astype(f32))
    outs[0][...] = jnp.where(low_core, total[0], total[1])
    high, low, _ = two_parts(jnp.where(low_core, total[1], total[0]))
    outs[2][4, :8] = high
    outs[2][4, 8:] = low


def gather_start(ins, weights, outs):
    info, vector, own, far = ins
    low_core = info[CORE] == 0
    outs[0][...] = vector[...] + (far[4, :8].astype(f32) + far[4, 8:].astype(f32))
    for segment in range(4):
        outs[1][2 * segment] = jnp.where(low_core, own[segment], far[segment])
        outs[1][2 * segment + 1] = jnp.where(low_core, far[segment], own[segment])


def gather_first(ins, weights, outs):
    info, mine, theirs = ins
    for segment in range(4):
        place = slice(2 * segment, 2 * segment + 2)
        own, far = mine[place], theirs[place]
        own_low = bit_of(info, segment, 4) == 0
        outs[segment][:, :16] = jnp.where(own_low, own, far)
        outs[segment][:, 16:] = jnp.where(own_low, far, own)


def gather_level(level, ins, weights, outs):
    info = ins[0]
    for segment in range(4):
        own, far = ins[1 + segment][...], ins[5 + segment][...]
        half = own.shape[1]
        own_low = bit_of(info, segment, level) == 0
        outs[segment][:, :half] = jnp.where(own_low, own, far)
        outs[segment][:, half:] = jnp.where(own_low, far, own)


class Loaded:
    def __init__(self, source, buffer, semaphore):
        self.copy = pltpu.make_async_copy(source, buffer, semaphore)
        self.copy.start()
        self.buffer = buffer
        self.waiting = True

    def ready(self):
        if self.waiting:
            self.waiting = False
            self.copy.wait()
        return self.buffer

    def __getitem__(self, place):
        return self.ready()[place]

    @property
    def shape(self):
        return self.buffer.shape


class Fetched(Loaded):
    def __init__(self, info, layer, own, far, buffer, semaphore):
        self.copy = pltpu.make_async_copy(own, buffer, semaphore)
        other = pltpu.make_async_copy(far, buffer, semaphore)
        pl.when(info[CORE] == layer)(self.copy.start)
        pl.when(info[CORE] != layer)(other.start)
        self.buffer = buffer
        self.waiting = True


def device_kernel(body, name, scalars, shapes, layer=0, staged=False, limit=24):
    def call(*operands, weights=()):
        arrays = operands[scalars:]
        flat = [array for pair in weights for array in pair]
        count, total, results = len(arrays), len(weights), len(shapes)

        def kernel(*refs):
            ins, refs = refs[: scalars + count], refs[scalars + count :]
            pairs, refs = refs[: 2 * total], refs[2 * total :]
            outs, rest = refs[:results], refs[results:]
            fetched = [
                Fetched(ins[0], layer, pairs[2 * i], pairs[2 * i + 1], rest[i], rest[total + i])
                for i in range(total)
            ]
            body(ins, fetched, outs)

        def whole(shape):
            zeros = (0,) * len(shape)
            if staged:
                return pl.BlockSpec(shape, lambda i: zeros)
            return pl.BlockSpec(memory_space=pltpu.VMEM)

        smem = pl.BlockSpec(memory_space=pltpu.SMEM)
        hbm = pl.BlockSpec(memory_space=pl.ANY)
        return pl.pallas_call(
            kernel,
            name=name,
            grid=(1,) if staged else (),
            in_specs=[smem] * scalars + [whole(array.shape) for array in arrays] + [hbm] * len(flat),
            out_specs=[whole(shape) for shape, _ in shapes],
            out_shape=[jax.ShapeDtypeStruct(shape, dtype) for shape, dtype in shapes],
            scratch_shapes=[pltpu.VMEM(own.shape, own.dtype) for own, _ in weights]
            + [pltpu.SemaphoreType.DMA(())] * total,
            compiler_params=pltpu.CompilerParams(
                vmem_limit_bytes=limit * 1024 * 1024
            ),
        )(*operands, *flat)

    return call


def assemble(info, blocks, far, results=()):
    def kernel(info, *refs):
        sources, refs = refs[:4], refs[4 + len(results) :]
        qkv_ref, out_ref, up_ref, down_ref = refs[:4]
        buffers, wide, semaphores = refs[4:8], refs[8], refs[9:]
        loaded = [Loaded(sources[i], buffers[i], semaphores[i]) for i in range(4)]
        copies = []

        def send(source, target):
            copies.append(pltpu.make_async_copy(source, target, semaphores[4 + len(copies)]))
            copies[-1].start()

        for segment in range(4):
            bit = bit_of(info, segment, 0) ^ far
            for half in range(2):
                wide[segment, half] = loaded[segment][half].astype(f32)
                block = wide.at[segment, half]
                rows = pl.ds(pl.multiple_of(half * 512 + bit * 256, 256), 256)
                left, right = block.at[:, :512], block.at[:, 512:]
                if segment == 0:
                    send(block, down_ref.at[rows, :])
                if segment == 1:
                    send(block, up_ref.at[rows, :])
                if segment == 2:
                    send(left, qkv_ref.at[0, rows, :])
                    send(right, qkv_ref.at[1, rows, :])
                if segment == 3:
                    send(left, qkv_ref.at[2, rows, :])
                    short = pl.ds(pl.multiple_of(bit * 256, 256), 256)
                    send(right, out_ref.at[short, half * 512 : (half + 1) * 512])
        for copy in copies:
            copy.wait()

    hbm = pl.BlockSpec(memory_space=pl.ANY)
    return pl.pallas_call(
        kernel,
        name="assemble",
        in_specs=[pl.BlockSpec(memory_space=pltpu.SMEM)] + [hbm] * (4 + len(results)),
        out_specs=[hbm] * 4,
        out_shape=[
            jax.ShapeDtypeStruct((3, 1024, 512), f32),
            jax.ShapeDtypeStruct((512, 1024), f32),
            jax.ShapeDtypeStruct((1024, 1024), f32),
            jax.ShapeDtypeStruct((1024, 1024), f32),
        ],
        scratch_shapes=[pltpu.VMEM((2, 256, WIDTH), bf16)] * 4
        + [pltpu.VMEM((4, 2, 256, WIDTH), f32)]
        + [pltpu.SemaphoreType.DMA(())] * 16,
        input_output_aliases={5 + i: i for i in range(len(results))},
        compiler_params=pltpu.CompilerParams(vmem_limit_bytes=32 * 1024 * 1024),
    )(info, *blocks, *results)


ROWS = (LEN, WIDTH)
TABLE = ((8, WIDTH), f32)
BOTH_TABLES = ((2, 8, WIDTH), f32)
ATTENTION_OUT = (
    (ROWS, bf16),
    (ROWS, bf16),
    ((3, LEN, LOCAL), bf16),
    ((HEADS_DEV, LEN, LEN), f32),
    ((LEN, LOCAL), bf16),
    (ROWS, f32),
    (ROWS, bf16),
)
MLP_OUT = ((ROWS, f32), (ROWS, bf16), (ROWS, f32), (ROWS, bf16), (ROWS, f32), (ROWS, bf16))
MLP_BACK_OUT = ((ROWS, bf16), (ROWS, f32), (ROWS, bf16), ((LEN, 3072), bf16), TABLE)
ATTENTION_BACK_OUT = (
    (ROWS, f32),
    (ROWS, bf16),
    ((3, LEN, LOCAL), bf16),
    (ROWS, f32),
    (ROWS, bf16),
    ((LEN, 3072), bf16),
    TABLE,
)
MAKE_TABLE = device_kernel(make_table, "make_table", 0, (TABLE,), staged=True)
FIRST_ATTENTION = device_kernel(first_attention, "first_attention", 2, ATTENTION_OUT, 0)
NEXT_ATTENTION = device_kernel(next_attention, "next_attention", 2, ATTENTION_OUT, 1)
MLP_FORWARD = tuple(
    device_kernel(functools.partial(mlp_forward, layer), "mlp_forward", 1, MLP_OUT, layer)
    for layer in range(2)
)
MLP_BACKWARD = device_kernel(
    mlp_backward, "mlp_backward", 1, ((ROWS, bf16),) + MLP_BACK_OUT, 1
)
MLP_BACKWARD_BELOW = device_kernel(
    mlp_backward_below, "mlp_backward_below", 1, ((ROWS, bf16), TABLE) + MLP_BACK_OUT, 0
)
ATTENTION_BACKWARD = tuple(
    device_kernel(
        functools.partial(attention_backward, layer),
        "attention_backward",
        1,
        ATTENTION_BACK_OUT,
        layer,
    )
    for layer in range(2)
)
LAST_INPUT_GRAD = device_kernel(last_input_grad, "last_input_grad", 1, ((ROWS, f32), BOTH_TABLES))
FINISH_ROWS = device_kernel(finish_rows, "finish_rows", 1, ((ROWS, f32), (ROWS, f32)))
FIRST_HALVES = (((256, WIDTH), f32),) * 2 + (((256, WIDTH), bf16),) * 2
MLP_WEIGHT_GRADS = device_kernel(mlp_weight_grads, "mlp_weight_grads", 1, FIRST_HALVES)
ATTENTION_WEIGHT_GRADS = device_kernel(
    attention_weight_grads, "attention_weight_grads", 1, FIRST_HALVES
)


def blocks(rows, dtype):
    return (((2, rows, WIDTH), dtype),) * 4


def sent_blocks(rows):
    return (((2, rows + 16, WIDTH), bf16),) + (((2, rows, WIDTH), bf16),) * 3


JOIN_LAYERS = device_kernel(
    join_layers, "join_layers", 1, (BOTH_TABLES,) + blocks(128, f32) + sent_blocks(128)
)
REDUCE_LEVEL = {
    level: device_kernel(
        functools.partial(reduce_level, level),
        "reduce_level",
        1,
        (BOTH_TABLES,) + blocks(256 >> level, f32) + sent_blocks(256 >> level)
        if level < 4
        else (BOTH_TABLES, ((8, 16, WIDTH), f32), ((10, 16, WIDTH), bf16)),
    )
    for level in (2, 3, 4)
}
REDUCE_LAST = device_kernel(
    reduce_last, "reduce_last", 1, (TABLE, ((4, 16, WIDTH), bf16), ((5, 16, WIDTH), bf16))
)
GATHER_START = device_kernel(gather_start, "gather_start", 1, (TABLE, ((8, 16, WIDTH), bf16)))
GATHER_FIRST = device_kernel(gather_first, "gather_first", 1, blocks(32, bf16))
GATHER_LEVEL = {
    level: device_kernel(
        functools.partial(gather_level, level), "gather_level", 1, blocks(512 >> level, bf16)
    )
    for level in (3, 2, 1)
}


def step_bit(axis, pairs):
    index = lax.axis_index(axis)
    if pairs is PAIR_E:
        return (index ^ (index >> 1)) & 1
    if pairs is PAIR_F:
        return (index >> 1) & 1
    return index


def local(
    section_in,
    lengths,
    qkv_weight,
    qv_bias,
    out_weight,
    up_weight,
    up_bias,
    down_weight,
    norm_gains,
    row_biases,
):
    core = lax.axis_index("pipe")
    tensor_index = lax.axis_index("tensor")
    place = core * 2 + tensor_index
    both = ("pipe", "tensor")

    own_rows = section_in[0, 0, 0]
    near = lax.ppermute(own_rows, both, ((0, 1), (1, 2)))
    far = lax.ppermute(own_rows, both, ((1, 3),))

    (table,) = MAKE_TABLE(qv_bias[0], up_bias, norm_gains[0], row_biases[0])
    first_far = [lax.ppermute(array, "pipe", SWAP) for array in (qkv_weight[0], out_weight[0], table)]
    up_own, down_own, near, far, *first_far = lax.optimization_barrier(
        (up_weight[0], down_weight[0], near, far, *first_far)
    )
    second_far = [lax.ppermute(array, "pipe", SWAP) for array in (up_own, down_own)]
    table_far = first_far[2]
    qkv_w = (qkv_weight[0], first_far[0])
    out_w = (out_weight[0], first_far[1])
    up_w = (up_weight[0], second_far[0])
    down_w = (down_weight[0], second_far[1])
    tables = (table, table_far)

    bits = [step_bit(axis, pairs) for route in ROUTES for axis, pairs in route]
    info = jnp.stack([core, tensor_index] + bits).astype(jnp.int32)

    def swapped(sent):
        return lax.ppermute(sent, "tensor", SWAP)

    def crossed(sent):
        return lax.ppermute(sent, "pipe", SWAP)

    rows_0, attn_0, proj_0, prob_0, context_0, part, sent = FIRST_ATTENTION(
        info, lengths, own_rows, near, far, *tables, weights=(qkv_w, out_w)
    )
    received, cot_own = lax.optimization_barrier((swapped(sent), own_rows))
    cot_near = lax.ppermute(cot_own, both, ((2, 0), (3, 2)))
    cot_far = lax.ppermute(cot_own, both, ((2, 1),))
    resid_0, mlp_0, pre_0, act_0, part, sent = MLP_FORWARD[0](
        info, rows_0, part, received, *tables, weights=(up_w, down_w)
    )
    rows_1, attn_1, proj_1, prob_1, context_1, part, sent = NEXT_ATTENTION(
        info, lengths, resid_0, part, swapped(sent), *tables, weights=(qkv_w, out_w)
    )
    resid_1, mlp_1, pre_1, act_1, top_part, top_sent = MLP_FORWARD[1](
        info, rows_1, part, swapped(sent), *tables, weights=(up_w, down_w)
    )

    cotangent, pre_half_1, part, sent, cross_mlp, sums_mlp_1 = MLP_BACKWARD(
        info, own_rows, cot_near, cot_far, pre_1, act_1, mlp_1, weights=(down_w, up_w)
    )
    early_1 = MLP_WEIGHT_GRADS(info, act_1, cotangent, mlp_1, pre_half_1, crossed(cross_mlp))
    received, *early_1 = lax.optimization_barrier((swapped(sent), *early_1))
    grad_1, resid_half_1, proj_grad_1, part, sent, cross_attn, sums_attn_1 = ATTENTION_BACKWARD[1](
        info, cotangent, part, received, resid_1, proj_1, prob_1, context_1, attn_1, *tables,
        weights=(out_w, qkv_w),
    )
    late_1 = ATTENTION_WEIGHT_GRADS(
        info, context_1, resid_half_1, attn_1, proj_grad_1, crossed(cross_attn)
    )
    received, *late_1 = lax.optimization_barrier((swapped(sent), *late_1))
    grad_half, sums_in_1, pre_half_0, part, sent, cross_mlp, sums_mlp_0 = MLP_BACKWARD_BELOW(
        info, grad_1, part, received, rows_1, pre_0, act_0, mlp_0, *tables,
        weights=(down_w, up_w),
    )
    early_0 = MLP_WEIGHT_GRADS(info, act_0, grad_half, mlp_0, pre_half_0, crossed(cross_mlp))
    received, *early_0 = lax.optimization_barrier((swapped(sent), *early_0))
    grad_0, resid_half_0, proj_grad_0, part, sent, cross_attn, sums_attn_0 = ATTENTION_BACKWARD[0](
        info, grad_half, part, received, resid_0, proj_0, prob_0, context_0, attn_0, *tables,
        weights=(out_w, qkv_w),
    )
    late_0 = ATTENTION_WEIGHT_GRADS(
        info, context_0, resid_half_0, attn_0, proj_grad_0, crossed(cross_attn)
    )
    received, top_sent, *late_0 = lax.optimization_barrier((swapped(sent), top_sent, *late_0))

    def half_steps(arrays, level):
        arrays = lax.optimization_barrier(tuple(arrays))
        return [
            lax.ppermute(array, *route[level]) for array, route in zip(arrays, ROUTES)
        ]

    kept_1 = (*early_1[:2], *late_1[:2])
    kept_0 = (*early_0[:2], *late_0[:2])
    received_1 = half_steps((*early_1[2:], *late_1[2:]), 0)
    received_0 = half_steps((*early_0[2:], *late_0[2:]), 0)

    grad_zero, vectors = LAST_INPUT_GRAD(
        info, grad_0, part, received, rows_0, *tables,
        sums_mlp_0, sums_attn_0, sums_in_1, sums_mlp_1, sums_attn_1,
    )
    vectors_in = lax.ppermute(vectors, *ROUTES[0][0])
    vectors, *stepped = JOIN_LAYERS(
        info, *kept_0, *kept_1, *received_0, *received_1, vectors, vectors_in
    )
    for level in (1, 2, 3):
        kept, sent = stepped[:4], stepped[4:]
        arrived = lax.optimization_barrier(half_steps(sent, level))
        vectors, *stepped = REDUCE_LEVEL[level + 1](info, vectors, *kept, *arrived)
    kept_rows, crossing = FINISH_ROWS(
        info, grad_zero, resid_1, top_part, swapped(top_sent), *tables
    )
    kept, sent = stepped
    vectors, own, far = REDUCE_LAST(info, vectors, kept, lax.ppermute(sent, "xh", SWAP))
    vectors, held = GATHER_START(info, vectors, own, crossed(far))
    shared = vectors[GAIN_A:]
    shared = 0.5 * (shared + swapped(shared))
    held = GATHER_FIRST(info, held, lax.ppermute(held, "xh", SWAP))
    for level in (3, 2, 1):
        arrived = lax.optimization_barrier(half_steps(held, level))
        held = GATHER_LEVEL[level](info, *held, *arrived)
    arrived = lax.optimization_barrier(half_steps(held, 0))
    results = assemble(info, held, 0)
    qkv_g, out_g, up_g, down_g = assemble(info, arrived, 1, results)

    crossing = lax.ppermute(crossing, both, ((0, 2), (3, 1)))
    section_out = jnp.where(core == tensor_index, kept_rows, crossing)
    return (
        section_out[None, None, None],
        qkv_g[None],
        vectors[0].reshape(1, 2, 512),
        out_g[None],
        up_g[None],
        vectors[1][None],
        down_g[None],
        shared[:2][None],
        shared[2:][None],
    )


def solution(mesh):
    fine = Mesh(mesh.devices.reshape(2, 2, 4, 4, 2), ("pipe", "tensor", "y", "z", "xh"))
    dp = ("y", "z", "xh")
    in_specs = (
        P("pipe", dp, "tensor", None, None),
        P(dp, None),
        P("pipe", None, None, "tensor"),
        P("pipe", None, "tensor"),
        P("pipe", "tensor", None),
        P("pipe", None, "tensor"),
        P("pipe", "tensor"),
        P("pipe", "tensor", None),
        P("pipe", None, None),
        P("pipe", None, None),
    )
    out_specs = (
        P("pipe", dp, "tensor", None, None),
        P("pipe", None, None, "tensor"),
        P("pipe", None, "tensor"),
        P("pipe", "tensor", None),
        P("pipe", None, "tensor"),
        P("pipe", "tensor"),
        P("pipe", "tensor", None),
        P("pipe", None, None),
        P("pipe", None, None),
    )
    return jax.shard_map(local, mesh=fine, in_specs=in_specs, out_specs=out_specs, check_vma=False)
```

```python
import functools

import jax
import jax.numpy as jnp
from jax import lax
from jax.experimental import pallas as pl
from jax.experimental.pallas import tpu as pltpu
from jax.sharding import Mesh
from jax.sharding import PartitionSpec as P

HEADS = 16
HD = 64
LEN = 128
norm_eps = 1e-05

f32 = jnp.float32
bf16 = jnp.bfloat16

SWAP = ((0, 1), (1, 0))
PAIR_E = ((0, 1), (1, 0), (2, 3), (3, 2))
PAIR_F = ((0, 3), (3, 0), (1, 2), (2, 1))
DP = ("y", "z", "xh")
ROUTES = (
    (("y", PAIR_E), ("y", PAIR_F), ("z", PAIR_E), ("z", PAIR_F), ("xh", SWAP)),
    (("y", PAIR_F), ("y", PAIR_E), ("z", PAIR_F), ("z", PAIR_E), ("xh", SWAP)),
    (("z", PAIR_E), ("z", PAIR_F), ("y", PAIR_E), ("y", PAIR_F), ("xh", SWAP)),
    (("z", PAIR_F), ("z", PAIR_E), ("y", PAIR_F), ("y", PAIR_E), ("xh", SWAP)),
)
CORE, TENSOR, BITS = 0, 1, 2


GELU_A = 0.7978845608028654
GELU_B = 0.044715
WIDTH = 1024
HEADS_DEV = HEADS // 2
LOCAL = HEADS_DEV * HD
PAIR = 2 * HD


def matmul(left, right):
    return jnp.dot(left, right, preferred_element_type=f32)


def matmul_nt(left, right):
    return lax.dot_general(left, right, (((1,), (1,)), ((), ())), preferred_element_type=f32)


def matmul_tn(left, right):
    return lax.dot_general(left, right, (((0,), (0,)), ((), ())), preferred_element_type=f32)


def norm_stats(values):
    centred = values - jnp.mean(values, axis=-1, keepdims=True)
    inv_std = lax.rsqrt(jnp.mean(centred * centred, axis=-1, keepdims=True) + norm_eps)
    return centred * inv_std, inv_std


def norm_back(grad_norm, normed, inv_std, gain):
    scaled = grad_norm * gain
    return inv_std * (
        scaled
        - jnp.mean(scaled, axis=-1, keepdims=True)
        - normed * jnp.mean(scaled * normed, axis=-1, keepdims=True)
    )


QV, UP_B, GAIN_A, GAIN_M, SHIFT_A, SHIFT_O, SHIFT_M, SHIFT_D = range(8)


def row(table, index):
    return table[index : index + 1, :]


def table_of(rows):
    zero = jnp.zeros((1, WIDTH), f32)
    return jnp.concatenate([rows.get(index, zero) for index in range(8)], axis=0)


def column_sum(block):
    return jnp.sum(block, axis=0, keepdims=True)


def head_lanes():
    return lax.broadcasted_iota(jnp.int32, (LEN, PAIR), 1) < HD


def attention_rows(rows, table, info, lengths, weights, outs):
    attn_rows_ref, proj_ref, prob_ref, context_ref, part_ref, sent_ref = outs
    normed, _ = norm_stats(rows.astype(f32))
    attn_rows = (normed * row(table, GAIN_A) + row(table, SHIFT_A)).astype(bf16)
    attn_rows_ref[...] = attn_rows
    qkv_w = weights[0].ready()
    for c in range(3):
        block = matmul(attn_rows, qkv_w[c])
        if c == 0:
            block = block + table[QV : QV + 1, :LOCAL]
        if c == 2:
            block = block + table[QV : QV + 1, LOCAL:]
        proj_ref[c] = block.astype(bf16)
    spot_i = lax.broadcasted_iota(jnp.int32, (LEN, LEN), 0)
    spot_j = lax.broadcasted_iota(jnp.int32, (LEN, LEN), 1)
    allowed = (spot_j <= spot_i) & (spot_j < jnp.where(info[CORE] == 0, lengths[0, 0], lengths[0, 1]))
    offsets = (spot_i - spot_j).astype(f32)
    first = head_lanes()
    for pair in range(HEADS_DEV // 2):
        lanes = slice(pair * PAIR, (pair + 1) * PAIR)
        query, key, value = (proj_ref[c, :, lanes] for c in range(3))
        found = []
        for side in range(2):
            head = 2 * pair + side
            mine = jnp.where(first if side == 0 else ~first, query, jnp.zeros_like(query))
            slope = jnp.where(
                info[TENSOR] == 0,
                2.0 ** (-8.0 * (head + 1) / HEADS),
                2.0 ** (-8.0 * (head + HEADS_DEV + 1) / HEADS),
            )
            scores = matmul_nt(mine, key) * 0.125 - slope * offsets
            scores = jnp.where(allowed, scores, -jnp.inf)
            top_score = jnp.max(scores, axis=-1, keepdims=True)
            exp_scores = jnp.exp(scores - top_score)
            prob = exp_scores / jnp.sum(exp_scores, axis=-1, keepdims=True)
            prob_ref[head] = prob
            found.append(matmul(prob.astype(bf16), value))
        context_ref[:, lanes] = jnp.where(first, found[0], found[1]).astype(bf16)
    part = matmul(context_ref[...], weights[1].ready()[...])
    part_ref[...] = part
    sent_ref[...] = part.astype(bf16)


def make_table(ins, weights, outs):
    qv_b, up_b, gains, shifts = ins
    outs[0][QV : QV + 1, :LOCAL] = qv_b[0:1, :].astype(f32)
    outs[0][QV : QV + 1, LOCAL:] = qv_b[1:2, :].astype(f32)
    outs[0][UP_B : UP_B + 1, :] = up_b[...].astype(f32)
    outs[0][GAIN_A : SHIFT_A, :] = gains[...]
    outs[0][SHIFT_A:, :] = shifts[...]


def table_for(info, tables, layer):
    own, far = tables
    return jnp.where(info[CORE] == layer, own[...], far[...])


def first_attention(ins, weights, outs):
    info, lengths, own_rows, near, far, *tables = ins
    rows_ref, *outs = outs
    place = 2 * info[CORE] + info[TENSOR]
    rows = jnp.where(place == 0, own_rows[...], jnp.where(place == 3, far[...], near[...]))
    rows_ref[...] = rows
    attention_rows(rows, table_for(info, tables, 0), info, lengths, weights, outs)


def next_attention(ins, weights, outs):
    info, lengths, resid, part, received, *tables = ins
    rows_ref, *outs = outs
    below = table_for(info, tables, 0)
    layer_out = resid[...] + (part[...] + received[...].astype(f32)) + row(below, SHIFT_D)
    rows = layer_out.astype(bf16)
    rows_ref[...] = rows
    attention_rows(rows, table_for(info, tables, 1), info, lengths, weights, outs)


def mlp_forward(layer, ins, weights, outs):
    info, rows, part, received, *tables = ins
    resid_ref, mlp_ref, pre_ref, act_ref, out_ref, sent_ref = outs
    table = table_for(info, tables, layer)
    resid = (
        rows[...].astype(f32) + (part[...] + received[...].astype(f32)) + row(table, SHIFT_O)
    )
    resid_ref[...] = resid
    normed, _ = norm_stats(resid)
    mlp_rows = (normed * row(table, GAIN_M) + row(table, SHIFT_M)).astype(bf16)
    mlp_ref[...] = mlp_rows
    pre = matmul(mlp_rows, weights[0].ready()[...]) + row(table, UP_B)
    pre_ref[...] = pre
    act = (0.5 * pre * (1.0 + jnp.tanh(GELU_A * (pre + GELU_B * pre * pre * pre)))).astype(bf16)
    act_ref[...] = act
    out = matmul(act, weights[1].ready()[...])
    out_ref[...] = out
    sent_ref[...] = out.astype(bf16)


def halves(core, block):
    half = block.shape[1] // 2
    low, high = block[:, :half], block[:, half:]
    own = core[CORE] == 0
    return jnp.where(own, low, high), jnp.where(own, high, low)


def mlp_back_body(info, grad, pre_in, act, mlp_rows, weights, outs):
    pre_half_ref, part_ref, sent_ref, cross_ref, sums_ref = outs
    grad_act = matmul_nt(grad, weights[0].ready()[...])
    pre = pre_in[...]
    tanh = jnp.tanh(GELU_A * (pre + GELU_B * pre * pre * pre))
    slope = 0.5 * (1.0 + tanh) + 0.5 * pre * (1.0 - tanh * tanh) * (
        GELU_A * (1.0 + 3.0 * GELU_B * pre * pre)
    )
    grad_pre = grad_act * slope
    pre_half = grad_pre.astype(bf16)
    pre_half_ref[...] = pre_half
    part = matmul_nt(pre_half, weights[1].ready()[...])
    part_ref[...] = part
    sent_ref[...] = part.astype(bf16)
    cross_ref[:, :512] = halves(info, act[...])[1]
    cross_ref[:, 512:1536] = grad
    cross_ref[:, 1536:2048] = halves(info, mlp_rows[...])[1]
    cross_ref[:, 2048:] = pre_half
    return column_sum(grad_pre)


def mlp_backward(ins, weights, outs):
    info, cot_own, cot_near, cot_far, pre, act, mlp_rows = ins
    grad_ref, *outs = outs
    place = 2 * info[CORE] + info[TENSOR]
    grad = jnp.where(place == 3, cot_own[...], jnp.where(place == 1, cot_far[...], cot_near[...]))
    grad_ref[...] = grad
    total = mlp_back_body(info, grad, pre, act, mlp_rows, weights, outs)
    outs[4][...] = table_of({UP_B: total})


def input_grad(grad_resid, part, received, rows, table):
    grad_attn = part[...] + received[...].astype(f32)
    normed, inv_std = norm_stats(rows[...].astype(f32))
    grad_in = grad_resid[...] + norm_back(grad_attn, normed, inv_std, row(table, GAIN_A))
    sums = {GAIN_A: column_sum(grad_attn * normed), SHIFT_A: column_sum(grad_attn)}
    return grad_in, sums


def mlp_backward_below(ins, weights, outs):
    info, grad_resid, da_part, da_received, above_rows, pre, act, mlp_rows, *tables = ins
    grad_ref, above_ref, *outs = outs
    above = table_for(info, tables, 1)
    grad_in, sums = input_grad(grad_resid, da_part, da_received, above_rows, above)
    above_ref[...] = table_of(sums)
    grad = grad_in.astype(bf16)
    grad_ref[...] = grad
    total = mlp_back_body(info, grad, pre, act, mlp_rows, weights, outs)
    outs[4][...] = table_of({UP_B: total})


def last_input_grad(ins, weights, outs):
    info, grad_resid, part, received, rows, *tables = ins
    grad_in, sums = input_grad(grad_resid, part, received, rows, table_for(info, tables[:2], 0))
    outs[0][...] = grad_in
    outs[1][0] = table_of(sums) + tables[2][...] + tables[3][...]
    outs[1][1] = tables[4][...] + tables[5][...] + tables[6][...]


def finish_rows(ins, weights, outs):
    info, grad_zero, resid, part, received, *tables = ins
    top = resid[...] + (part[...] + received[...].astype(f32))
    top = top + row(table_for(info, tables, 1), SHIFT_D)
    low_core = info[CORE] == 0
    outs[0][...] = jnp.where(low_core, grad_zero[...], top)
    outs[1][...] = jnp.where(low_core, top, grad_zero[...])


def attention_backward(layer, ins, weights, outs):
    info, grad_out, dc_part, dc_received, resid, proj, prob_in, context, attn_rows, *tables = ins
    grad_ref, resid_half_ref, proj_grad_ref, part_ref, sent_ref, cross_ref, sums_ref = outs
    table = table_for(info, tables, layer)
    grad_mlp = dc_part[...] + dc_received[...].astype(f32)
    normed, inv_std = norm_stats(resid[...])
    wide_out = grad_out[...].astype(f32)
    grad_resid = wide_out + norm_back(grad_mlp, normed, inv_std, row(table, GAIN_M))
    grad_ref[...] = grad_resid
    resid_half = grad_resid.astype(bf16)
    resid_half_ref[...] = resid_half
    grad_context = matmul_nt(resid_half, weights[0].ready()[...]).astype(bf16)
    first = head_lanes()
    query_sums = []
    value_sums = []
    for pair in range(HEADS_DEV // 2):
        lanes = slice(pair * PAIR, (pair + 1) * PAIR)
        query, key, value = (proj[c, :, lanes] for c in range(3))
        context_grad = grad_context[:, lanes]
        query_g, key_g, value_g = [], [], []
        for side in range(2):
            mask = first if side == 0 else ~first
            prob = prob_in[2 * pair + side]
            mine = jnp.where(mask, context_grad, jnp.zeros_like(context_grad))
            grad_prob = matmul_nt(mine, value)
            value_g.append(matmul_tn(prob.astype(bf16), context_grad))
            delta = jnp.sum(prob * grad_prob, axis=-1, keepdims=True)
            grad_scores = (prob * (grad_prob - delta) * 0.125).astype(bf16)
            query_g.append(matmul(grad_scores, key))
            key_g.append(matmul_tn(grad_scores, query))
        query_g, key_g, value_g = (
            jnp.where(first, low, high) for low, high in (query_g, key_g, value_g)
        )
        query_sums.append(column_sum(query_g))
        value_sums.append(column_sum(value_g))
        proj_grad_ref[0, :, lanes] = query_g.astype(bf16)
        proj_grad_ref[1, :, lanes] = key_g.astype(bf16)
        proj_grad_ref[2, :, lanes] = value_g.astype(bf16)
    qkv_w = weights[1].ready()
    part = matmul_nt(proj_grad_ref[0], qkv_w[0])
    part = part + matmul_nt(proj_grad_ref[1], qkv_w[1])
    part = part + matmul_nt(proj_grad_ref[2], qkv_w[2])
    part_ref[...] = part
    sent_ref[...] = part.astype(bf16)
    cross_ref[:, :512] = context[...]
    cross_ref[:, 512:1024] = halves(info, resid_half)[1]
    cross_ref[:, 1024:1536] = halves(info, attn_rows[...])[1]
    for c in range(3):
        cross_ref[:, 1536 + c * LOCAL : 1536 + (c + 1) * LOCAL] = proj_grad_ref[c]
    sums_ref[...] = table_of(
        {
            QV: jnp.concatenate(query_sums + value_sums, axis=1),
            GAIN_M: column_sum(grad_mlp * normed),
            SHIFT_O: column_sum(grad_resid),
            SHIFT_M: column_sum(grad_mlp),
            SHIFT_D: column_sum(wide_out),
        }
    )


def stacked(own, far):
    return jnp.concatenate([own, far], axis=0)


def bit_of(info, segment, level):
    return info[BITS + 5 * segment + level]


def split(info, segment, level, block, keep_ref, send_ref):
    half = block.shape[-2] // 2
    low, high = block[..., :half, :], block[..., half:, :]
    own_low = bit_of(info, segment, level) == 0
    keep_ref[...] = jnp.where(own_low, low, high)
    send_ref[...] = jnp.where(own_low, high, low).astype(bf16)


def mlp_weight_grads(ins, weights, outs):
    info, act, grad, mlp_rows, pre_half, crossed = ins
    left = stacked(halves(info, act[...])[0], crossed[:, :512])
    right = stacked(grad[...], crossed[:, 512:1536])
    split(info, 0, 0, matmul_tn(left, right), outs[0], outs[2])
    left = stacked(halves(info, mlp_rows[...])[0], crossed[:, 1536:2048])
    right = stacked(pre_half[...], crossed[:, 2048:])
    split(info, 1, 0, matmul_tn(left, right), outs[1], outs[3])


def attention_weight_grads(ins, weights, outs):
    info, context, resid_half, attn_rows, proj_grad, crossed = ins
    left = stacked(halves(info, attn_rows[...])[0], crossed[:, 1024:1536])
    blocks = []
    for c in range(3):
        far = crossed[:, 1536 + c * LOCAL : 1536 + (c + 1) * LOCAL]
        blocks.append(matmul_tn(left, stacked(proj_grad[c], far)))
    left = stacked(context[...], crossed[:, :512])
    right = stacked(halves(info, resid_half[...])[0], crossed[:, 512:1024])
    blocks.append(matmul_tn(left, right))
    split(info, 2, 0, jnp.concatenate(blocks[:2], axis=1), outs[0], outs[2])
    split(info, 3, 0, jnp.concatenate(blocks[2:], axis=1), outs[1], outs[3])


def two_parts(vector):
    high = vector.astype(bf16)
    low = (vector - high.astype(f32)).astype(bf16)
    return high, low, high.astype(f32) + low.astype(f32)


def join_layers(ins, weights, outs):
    info = ins[0]
    kept = (ins[1:5], ins[5:9])
    received = (ins[9:13], ins[13:17])
    vector, vector_in = ins[17:]
    for segment in range(4):
        for layer in range(2):
            total = kept[layer][segment][...] + received[layer][segment][...].astype(f32)
            sent = outs[5 + segment].at[layer, :128]
            split(info, segment, 1, total, outs[1 + segment].at[layer], sent)
    high, low, outs[0][...] = two_parts(vector[...] + vector_in[...])
    outs[5][:, 128:136] = high
    outs[5][:, 136:] = low


def reduce_level(level, ins, weights, outs):
    info, vector = ins[:2]
    rows = ins[2].shape[1]
    half = rows // 2
    total = vector[...] + (ins[6][:, rows : rows + 8].astype(f32) + ins[6][:, rows + 8 :].astype(f32))
    high, low, outs[0][...] = two_parts(total)
    for segment in range(4):
        total = ins[2 + segment][...] + ins[6 + segment][:, :rows].astype(f32)
        if level < 4:
            split(info, segment, level, total, outs[1 + segment], outs[5 + segment].at[:, :half])
        else:
            place = slice(2 * segment, 2 * segment + 2)
            split(info, segment, level, total, outs[1].at[place], outs[2].at[place])
    if level < 4:
        outs[5][:, half : half + 8] = high
        outs[5][:, half + 8 :] = low
    else:
        outs[2][8:, :8] = high
        outs[2][8:, 8:] = low


def reduce_last(ins, weights, outs):
    info, vector, kept, received = ins
    low_core = info[CORE] == 0
    for segment in range(4):
        place = slice(2 * segment, 2 * segment + 2)
        total = (kept[place] + received[place].astype(f32)).astype(bf16)
        outs[1][segment] = jnp.where(low_core, total[0], total[1])
        outs[2][segment] = jnp.where(low_core, total[1], total[0])
    total = vector[...] + (received[8:, :8].astype(f32) + received[8:, 8:].astype(f32))
    outs[0][...] = jnp.where(low_core, total[0], total[1])
    high, low, _ = two_parts(jnp.where(low_core, total[1], total[0]))
    outs[2][4, :8] = high
    outs[2][4, 8:] = low


def gather_start(ins, weights, outs):
    info, vector, own, far = ins
    low_core = info[CORE] == 0
    outs[0][...] = vector[...] + (far[4, :8].astype(f32) + far[4, 8:].astype(f32))
    for segment in range(4):
        outs[1][2 * segment] = jnp.where(low_core, own[segment], far[segment])
        outs[1][2 * segment + 1] = jnp.where(low_core, far[segment], own[segment])


def gather_first(ins, weights, outs):
    info, mine, theirs = ins
    for segment in range(4):
        place = slice(2 * segment, 2 * segment + 2)
        own, far = mine[place], theirs[place]
        own_low = bit_of(info, segment, 4) == 0
        outs[segment][:, :16] = jnp.where(own_low, own, far)
        outs[segment][:, 16:] = jnp.where(own_low, far, own)


def gather_level(level, ins, weights, outs):
    info = ins[0]
    for segment in range(4):
        own, far = ins[1 + segment][...], ins[5 + segment][...]
        half = own.shape[1]
        own_low = bit_of(info, segment, level) == 0
        outs[segment][:, :half] = jnp.where(own_low, own, far)
        outs[segment][:, half:] = jnp.where(own_low, far, own)


class Loaded:
    def __init__(self, source, buffer, semaphore):
        self.copy = pltpu.make_async_copy(source, buffer, semaphore)
        self.copy.start()
        self.buffer = buffer
        self.waiting = True

    def ready(self):
        if self.waiting:
            self.waiting = False
            self.copy.wait()
        return self.buffer

    def __getitem__(self, place):
        return self.ready()[place]

    @property
    def shape(self):
        return self.buffer.shape


class Fetched(Loaded):
    def __init__(self, info, layer, own, far, buffer, semaphore):
        self.copy = pltpu.make_async_copy(own, buffer, semaphore)
        other = pltpu.make_async_copy(far, buffer, semaphore)
        pl.when(info[CORE] == layer)(self.copy.start)
        pl.when(info[CORE] != layer)(other.start)
        self.buffer = buffer
        self.waiting = True


def device_kernel(body, name, scalars, shapes, layer=0, staged=False, limit=24):
    def call(*operands, weights=()):
        arrays = operands[scalars:]
        flat = [array for pair in weights for array in pair]
        count, total, results = len(arrays), len(weights), len(shapes)

        def kernel(*refs):
            ins, refs = refs[: scalars + count], refs[scalars + count :]
            pairs, refs = refs[: 2 * total], refs[2 * total :]
            outs, rest = refs[:results], refs[results:]
            fetched = [
                Fetched(ins[0], layer, pairs[2 * i], pairs[2 * i + 1], rest[i], rest[total + i])
                for i in range(total)
            ]
            body(ins, fetched, outs)

        def whole(shape):
            zeros = (0,) * len(shape)
            if staged:
                return pl.BlockSpec(shape, lambda i: zeros)
            return pl.BlockSpec(memory_space=pltpu.VMEM)

        smem = pl.BlockSpec(memory_space=pltpu.SMEM)
        hbm = pl.BlockSpec(memory_space=pl.ANY)
        return pl.pallas_call(
            kernel,
            name=name,
            grid=(1,) if staged else (),
            in_specs=[smem] * scalars + [whole(array.shape) for array in arrays] + [hbm] * len(flat),
            out_specs=[whole(shape) for shape, _ in shapes],
            out_shape=[jax.ShapeDtypeStruct(shape, dtype) for shape, dtype in shapes],
            scratch_shapes=[pltpu.VMEM(own.shape, own.dtype) for own, _ in weights]
            + [pltpu.SemaphoreType.DMA(())] * total,
            compiler_params=pltpu.CompilerParams(
                vmem_limit_bytes=limit * 1024 * 1024
            ),
        )(*operands, *flat)

    return call


def assemble(info, blocks, far, results=()):
    def kernel(info, *refs):
        sources, refs = refs[:4], refs[4 + len(results) :]
        qkv_ref, out_ref, up_ref, down_ref = refs[:4]
        wide, semaphores = refs[4], refs[5:]
        copies = []

        def send(source, target):
            copies.append(pltpu.make_async_copy(source, target, semaphores[len(copies)]))
            copies[-1].start()

        for segment in range(4):
            bit = bit_of(info, segment, 0) ^ far
            for half in range(2):
                wide[segment, half] = sources[segment][half].astype(f32)
                block = wide.at[segment, half]
                rows = pl.ds(pl.multiple_of(half * 512 + bit * 256, 256), 256)
                left, right = block.at[:, :512], block.at[:, 512:]
                if segment == 0:
                    send(block, down_ref.at[rows, :])
                if segment == 1:
                    send(block, up_ref.at[rows, :])
                if segment == 2:
                    send(left, qkv_ref.at[0, rows, :])
                    send(right, qkv_ref.at[1, rows, :])
                if segment == 3:
                    send(left, qkv_ref.at[2, rows, :])
                    short = pl.ds(pl.multiple_of(bit * 256, 256), 256)
                    send(right, out_ref.at[short, half * 512 : (half + 1) * 512])
        for copy in copies:
            copy.wait()

    hbm = pl.BlockSpec(memory_space=pl.ANY)
    return pl.pallas_call(
        kernel,
        name="assemble",
        in_specs=[pl.BlockSpec(memory_space=pltpu.SMEM)]
        + [pl.BlockSpec(memory_space=pltpu.VMEM)] * 4
        + [hbm] * len(results),
        out_specs=[hbm] * 4,
        out_shape=[
            jax.ShapeDtypeStruct((3, 1024, 512), f32),
            jax.ShapeDtypeStruct((512, 1024), f32),
            jax.ShapeDtypeStruct((1024, 1024), f32),
            jax.ShapeDtypeStruct((1024, 1024), f32),
        ],
        scratch_shapes=[pltpu.VMEM((4, 2, 256, WIDTH), f32)] + [pltpu.SemaphoreType.DMA(())] * 12,
        input_output_aliases={5 + i: i for i in range(len(results))},
        compiler_params=pltpu.CompilerParams(vmem_limit_bytes=24 * 1024 * 1024),
    )(info, *blocks, *results)


ROWS = (LEN, WIDTH)
TABLE = ((8, WIDTH), f32)
BOTH_TABLES = ((2, 8, WIDTH), f32)
ATTENTION_OUT = (
    (ROWS, bf16),
    (ROWS, bf16),
    ((3, LEN, LOCAL), bf16),
    ((HEADS_DEV, LEN, LEN), f32),
    ((LEN, LOCAL), bf16),
    (ROWS, f32),
    (ROWS, bf16),
)
MLP_OUT = ((ROWS, f32), (ROWS, bf16), (ROWS, f32), (ROWS, bf16), (ROWS, f32), (ROWS, bf16))
MLP_BACK_OUT = ((ROWS, bf16), (ROWS, f32), (ROWS, bf16), ((LEN, 3072), bf16), TABLE)
ATTENTION_BACK_OUT = (
    (ROWS, f32),
    (ROWS, bf16),
    ((3, LEN, LOCAL), bf16),
    (ROWS, f32),
    (ROWS, bf16),
    ((LEN, 3072), bf16),
    TABLE,
)
MAKE_TABLE = device_kernel(make_table, "make_table", 0, (TABLE,), staged=True)
FIRST_ATTENTION = device_kernel(first_attention, "first_attention", 2, ATTENTION_OUT, 0)
NEXT_ATTENTION = device_kernel(next_attention, "next_attention", 2, ATTENTION_OUT, 1)
MLP_FORWARD = tuple(
    device_kernel(functools.partial(mlp_forward, layer), "mlp_forward", 1, MLP_OUT, layer)
    for layer in range(2)
)
MLP_BACKWARD = device_kernel(
    mlp_backward, "mlp_backward", 1, ((ROWS, bf16),) + MLP_BACK_OUT, 1
)
MLP_BACKWARD_BELOW = device_kernel(
    mlp_backward_below, "mlp_backward_below", 1, ((ROWS, bf16), TABLE) + MLP_BACK_OUT, 0
)
ATTENTION_BACKWARD = tuple(
    device_kernel(
        functools.partial(attention_backward, layer),
        "attention_backward",
        1,
        ATTENTION_BACK_OUT,
        layer,
    )
    for layer in range(2)
)
LAST_INPUT_GRAD = device_kernel(last_input_grad, "last_input_grad", 1, ((ROWS, f32), BOTH_TABLES))
FINISH_ROWS = device_kernel(finish_rows, "finish_rows", 1, ((ROWS, f32), (ROWS, f32)))
FIRST_HALVES = (((256, WIDTH), f32),) * 2 + (((256, WIDTH), bf16),) * 2
MLP_WEIGHT_GRADS = device_kernel(mlp_weight_grads, "mlp_weight_grads", 1, FIRST_HALVES)
ATTENTION_WEIGHT_GRADS = device_kernel(
    attention_weight_grads, "attention_weight_grads", 1, FIRST_HALVES
)


def blocks(rows, dtype):
    return (((2, rows, WIDTH), dtype),) * 4


def sent_blocks(rows):
    return (((2, rows + 16, WIDTH), bf16),) + (((2, rows, WIDTH), bf16),) * 3


JOIN_LAYERS = device_kernel(
    join_layers, "join_layers", 1, (BOTH_TABLES,) + blocks(128, f32) + sent_blocks(128)
)
REDUCE_LEVEL = {
    level: device_kernel(
        functools.partial(reduce_level, level),
        "reduce_level",
        1,
        (BOTH_TABLES,) + blocks(256 >> level, f32) + sent_blocks(256 >> level)
        if level < 4
        else (BOTH_TABLES, ((8, 16, WIDTH), f32), ((10, 16, WIDTH), bf16)),
    )
    for level in (2, 3, 4)
}
REDUCE_LAST = device_kernel(
    reduce_last, "reduce_last", 1, (TABLE, ((4, 16, WIDTH), bf16), ((5, 16, WIDTH), bf16))
)
GATHER_START = device_kernel(gather_start, "gather_start", 1, (TABLE, ((8, 16, WIDTH), bf16)))
GATHER_FIRST = device_kernel(gather_first, "gather_first", 1, blocks(32, bf16))
GATHER_LEVEL = {
    level: device_kernel(
        functools.partial(gather_level, level), "gather_level", 1, blocks(512 >> level, bf16)
    )
    for level in (3, 2, 1)
}


def step_bit(axis, pairs):
    index = lax.axis_index(axis)
    if pairs is PAIR_E:
        return (index ^ (index >> 1)) & 1
    if pairs is PAIR_F:
        return (index >> 1) & 1
    return index


def local(
    section_in,
    lengths,
    qkv_weight,
    qv_bias,
    out_weight,
    up_weight,
    up_bias,
    down_weight,
    norm_gains,
    row_biases,
):
    core = lax.axis_index("pipe")
    tensor_index = lax.axis_index("tensor")
    place = core * 2 + tensor_index
    both = ("pipe", "tensor")

    own_rows = section_in[0, 0, 0]
    near = lax.ppermute(own_rows, both, ((0, 1), (1, 2)))
    far = lax.ppermute(own_rows, both, ((1, 3),))

    (table,) = MAKE_TABLE(qv_bias[0], up_bias, norm_gains[0], row_biases[0])
    first_far = [lax.ppermute(array, "pipe", SWAP) for array in (qkv_weight[0], out_weight[0], table)]
    up_own, down_own, near, far, *first_far = lax.optimization_barrier(
        (up_weight[0], down_weight[0], near, far, *first_far)
    )
    second_far = [lax.ppermute(array, "pipe", SWAP) for array in (up_own, down_own)]
    table_far = first_far[2]
    qkv_w = (qkv_weight[0], first_far[0])
    out_w = (out_weight[0], first_far[1])
    up_w = (up_weight[0], second_far[0])
    down_w = (down_weight[0], second_far[1])
    tables = (table, table_far)

    bits = [step_bit(axis, pairs) for route in ROUTES for axis, pairs in route]
    info = jnp.stack([core, tensor_index] + bits).astype(jnp.int32)

    def swapped(sent):
        return lax.ppermute(sent, "tensor", SWAP)

    def crossed(sent):
        return lax.ppermute(sent, "pipe", SWAP)

    rows_0, attn_0, proj_0, prob_0, context_0, part, sent = FIRST_ATTENTION(
        info, lengths, own_rows, near, far, *tables, weights=(qkv_w, out_w)
    )
    received, cot_own = lax.optimization_barrier((swapped(sent), own_rows))
    cot_near = lax.ppermute(cot_own, both, ((2, 0), (3, 2)))
    cot_far = lax.ppermute(cot_own, both, ((2, 1),))
    resid_0, mlp_0, pre_0, act_0, part, sent = MLP_FORWARD[0](
        info, rows_0, part, received, *tables, weights=(up_w, down_w)
    )
    rows_1, attn_1, proj_1, prob_1, context_1, part, sent = NEXT_ATTENTION(
        info, lengths, resid_0, part, swapped(sent), *tables, weights=(qkv_w, out_w)
    )
    resid_1, mlp_1, pre_1, act_1, top_part, top_sent = MLP_FORWARD[1](
        info, rows_1, part, swapped(sent), *tables, weights=(up_w, down_w)
    )

    cotangent, pre_half_1, part, sent, cross_mlp, sums_mlp_1 = MLP_BACKWARD(
        info, own_rows, cot_near, cot_far, pre_1, act_1, mlp_1, weights=(down_w, up_w)
    )
    early_1 = MLP_WEIGHT_GRADS(info, act_1, cotangent, mlp_1, pre_half_1, crossed(cross_mlp))
    received, *early_1 = lax.optimization_barrier((swapped(sent), *early_1))
    grad_1, resid_half_1, proj_grad_1, part, sent, cross_attn, sums_attn_1 = ATTENTION_BACKWARD[1](
        info, cotangent, part, received, resid_1, proj_1, prob_1, context_1, attn_1, *tables,
        weights=(out_w, qkv_w),
    )
    late_1 = ATTENTION_WEIGHT_GRADS(
        info, context_1, resid_half_1, attn_1, proj_grad_1, crossed(cross_attn)
    )
    received, *late_1 = lax.optimization_barrier((swapped(sent), *late_1))
    grad_half, sums_in_1, pre_half_0, part, sent, cross_mlp, sums_mlp_0 = MLP_BACKWARD_BELOW(
        info, grad_1, part, received, rows_1, pre_0, act_0, mlp_0, *tables,
        weights=(down_w, up_w),
    )
    early_0 = MLP_WEIGHT_GRADS(info, act_0, grad_half, mlp_0, pre_half_0, crossed(cross_mlp))
    received, *early_0 = lax.optimization_barrier((swapped(sent), *early_0))
    grad_0, resid_half_0, proj_grad_0, part, sent, cross_attn, sums_attn_0 = ATTENTION_BACKWARD[0](
        info, grad_half, part, received, resid_0, proj_0, prob_0, context_0, attn_0, *tables,
        weights=(out_w, qkv_w),
    )
    late_0 = ATTENTION_WEIGHT_GRADS(
        info, context_0, resid_half_0, attn_0, proj_grad_0, crossed(cross_attn)
    )
    received, top_sent, *late_0 = lax.optimization_barrier((swapped(sent), top_sent, *late_0))

    def half_steps(arrays, level):
        arrays = lax.optimization_barrier(tuple(arrays))
        return [
            lax.ppermute(array, *route[level]) for array, route in zip(arrays, ROUTES)
        ]

    kept_1 = (*early_1[:2], *late_1[:2])
    kept_0 = (*early_0[:2], *late_0[:2])
    received_1 = half_steps((*early_1[2:], *late_1[2:]), 0)
    received_0 = half_steps((*early_0[2:], *late_0[2:]), 0)

    grad_zero, vectors = LAST_INPUT_GRAD(
        info, grad_0, part, received, rows_0, *tables,
        sums_mlp_0, sums_attn_0, sums_in_1, sums_mlp_1, sums_attn_1,
    )
    vectors_in = lax.ppermute(vectors, *ROUTES[0][0])
    vectors, *stepped = JOIN_LAYERS(
        info, *kept_0, *kept_1, *received_0, *received_1, vectors, vectors_in
    )
    for level in (1, 2, 3):
        kept, sent = stepped[:4], stepped[4:]
        arrived = lax.optimization_barrier(half_steps(sent, level))
        vectors, *stepped = REDUCE_LEVEL[level + 1](info, vectors, *kept, *arrived)
    kept_rows, crossing = FINISH_ROWS(
        info, grad_zero, resid_1, top_part, swapped(top_sent), *tables
    )
    kept, sent = stepped
    vectors, own, far = REDUCE_LAST(info, vectors, kept, lax.ppermute(sent, "xh", SWAP))
    vectors, held = GATHER_START(info, vectors, own, crossed(far))
    shared = vectors[GAIN_A:]
    shared = 0.5 * (shared + swapped(shared))
    held = GATHER_FIRST(info, held, lax.ppermute(held, "xh", SWAP))
    for level in (3, 2, 1):
        arrived = lax.optimization_barrier(half_steps(held, level))
        held = GATHER_LEVEL[level](info, *held, *arrived)
    arrived = lax.optimization_barrier(half_steps(held, 0))
    results = assemble(info, held, 0)
    qkv_g, out_g, up_g, down_g = assemble(info, arrived, 1, results)

    crossing = lax.ppermute(crossing, both, ((0, 2), (3, 1)))
    section_out = jnp.where(core == tensor_index, kept_rows, crossing)
    return (
        section_out[None, None, None],
        qkv_g[None],
        vectors[0].reshape(1, 2, 512),
        out_g[None],
        up_g[None],
        vectors[1][None],
        down_g[None],
        shared[:2][None],
        shared[2:][None],
    )


def solution(mesh):
    fine = Mesh(mesh.devices.reshape(2, 2, 4, 4, 2), ("pipe", "tensor", "y", "z", "xh"))
    dp = ("y", "z", "xh")
    in_specs = (
        P("pipe", dp, "tensor", None, None),
        P(dp, None),
        P("pipe", None, None, "tensor"),
        P("pipe", None, "tensor"),
        P("pipe", "tensor", None),
        P("pipe", None, "tensor"),
        P("pipe", "tensor"),
        P("pipe", "tensor", None),
        P("pipe", None, None),
        P("pipe", None, None),
    )
    out_specs = (
        P("pipe", dp, "tensor", None, None),
        P("pipe", None, None, "tensor"),
        P("pipe", None, "tensor"),
        P("pipe", "tensor", None),
        P("pipe", None, "tensor"),
        P("pipe", "tensor"),
        P("pipe", "tensor", None),
        P("pipe", None, None),
        P("pipe", None, None),
    )
    return jax.shard_map(local, mesh=fine, in_specs=in_specs, out_specs=out_specs, check_vma=False)
```
